256 devices in a mesh: mp: 2 (over core), dev: 128 (over y, x, z).
Axes of the slice: x: 4, y: 4, z: 8, core: 2. Of those that a mesh axis runs over, the one named last changes fastest.
Arguments:
- spectrum: float32 [1024, 65536], P(None, ('mp', 'dev')), may hold values from 0.05 to 1
- water_mask: int32 [65536], P(('mp', 'dev')), may hold values 0 or 1
- courant: float32 [2, 1024], replicated, may hold values from 0.05 to 0.3
- stencil_sign: int32 [2, 1024], replicated, may hold values from 0 to 1
- quad_index: int32 [4, 1024, 2], replicated, may hold values from 0 to 1023
- quad_weight: float32 [4, 1024, 2], replicated, may hold values from 0.2 to 1
- nonlinear: float32 [1024], replicated, may hold values from 0.01 to 0.1
- stokes_table: bfloat16 [128, 1024], replicated, may hold values from -0.1875 to 0.1875
- point_index: int32 [4, 65536], P(None, ('mp', 'dev')), may hold values from 0 to 32767, as said below
- point_weight: float32 [4, 65536], P(None, ('mp', 'dev')), may hold values from 0.1 to 0.4
- ocean_index: int32 [4, 32768], P(None, ('mp', 'dev')), may hold values from 0 to 65535, as said below
- ocean_weight: float32 [4, 32768], P(None, ('mp', 'dev')), may hold values from 0.1 to 0.4
- currents: float32 [2, 64, 32768], P(None, None, ('mp', 'dev')), may hold values from -3 to 3
- coriolis: float32 [32768], P(('mp', 'dev')), may hold values from 0.2 to 0.6
- mixing: float32 [64], replicated, may hold values from 0.05 to 0.2
- surface_weights: float32 [64], replicated, may hold values from 0.005 to 0.05
Outputs:
- spectrum_out: float32 [1024, 65536], P(None, ('mp', 'dev'))
- currents_out: float32 [2, 64, 32768], P(None, None, ('mp', 'dev'))
The draws below stay inside these ranges and needn't reach their ends.
Inputs may be any that keep to these rules, and one draw needn't show every extreme that they name: `point_index`: entry j of point p names an ocean cell in row p // 256 plus -1, 0 or 1 and column (p % 256) // 2 plus -1, 0 or 1, both wrapping. `ocean_index`: entry j of cell c names a wave point in row c // 128 plus -1, 0 or 1 and column 2 (c % 128) plus -2 to 3, both wrapping.
All inputs are finite; a program needn't handle non-finite values. No bound on the sum of `water_mask` on one device may be relied on, other than what follows from the above.
Results may differ from the reference program's by a relative error of at most 0.0003.
The reference program's roundings to bfloat16 on the way count: a program that leaves them out, or rounds other values in their place, can miss the bound.
Values sent between devices are 32-bit elements; how exact they have to be, the bound alone decides.
No kernel may reach another device: no remote copies, remote signals or barrier semaphores. Data moves between devices by JAX's collectives and lax.ppermute only.
A program may use at most 64 MiB of HBM per device.

```python
import math
import jax
import jax.numpy as jnp
from jax import lax

K = 1024
L = 64
MX = 256
STEPS = 2
OX = 128
MY = 256
P_SIZE = 65536
NOC = 32768


def draw_point_index(key, part):
    point_total = MX * MY
    position = jnp.arange(point_total, dtype=jnp.int32)
    row_key, column_key = jax.random.split(jax.random.fold_in(key, 11))
    row_pick = (position // MX)[None, :] + jax.random.randint(row_key, (4, point_total), -1, 2)
    column_pick = (position % MX // 2)[None, :] + jax.random.randint(column_key, (4, point_total), -1, 2)
    return (jnp.mod(row_pick, MY) * OX + jnp.mod(column_pick, OX)).astype(jnp.int32)


def draw_ocean_index(key, part):
    cell_total = OX * MY
    position = jnp.arange(cell_total, dtype=jnp.int32)
    row_key, column_key = jax.random.split(jax.random.fold_in(key, 23))
    row_pick = (position // OX)[None, :] + jax.random.randint(row_key, (4, cell_total), -1, 2)
    column_pick = (2 * (position % OX))[None, :] + jax.random.randint(column_key, (4, cell_total), -2, 4)
    return (jnp.mod(row_pick, MY) * MX + jnp.mod(column_pick, MX)).astype(jnp.int32)


def place_ends(drawn, stream_key, low, high):
    place = [jax.random.randint(jax.random.fold_in(stream_key, axis), (), 0, length) for axis, length in enumerate(drawn.shape)]
    longest = drawn.shape.index(max(drawn.shape))
    beside = place[:longest] + [(place[longest] + 1) % drawn.shape[longest]] + place[longest + 1:]
    return drawn.at[tuple(place)].set(low).at[tuple(beside)].set(high)


def block_levels(rng, extent, cuts, smallest, top_value):
    def one(dim, parts):
        steps = jax.random.uniform(jax.random.fold_in(jax.random.fold_in(rng, 6), dim), (parts,), jnp.float32, smallest / len(cuts), top_value / len(cuts))
        return jnp.repeat(jnp.exp(steps), extent[dim] // parts).reshape((-1,) + (1,) * (len(extent) - dim - 1))

    level = one(*cuts[0])
    for cut in cuts[1:]:
        level = level * one(*cut)
    return level


def noise(own_key, extent, deviation, bound, cuts=(), held_as=jnp.bfloat16):
    factor_of = block_levels(own_key, extent, cuts, -0.22, 0.18) if cuts else 1.0
    values = jax.random.normal(own_key, extent, jnp.float32) * deviation * factor_of
    return jnp.minimum(jnp.maximum(values, -bound), bound).astype(held_as)


def setup_inputs(seed: int = 0) -> dict:
    key_of = jax.random.split(jax.random.key(seed), 17)
    spectrum = jnp.clip(jnp.exp(math.log(1.0) - 2.9957323 * jax.random.uniform(key_of[0], (K, P_SIZE), jnp.float32) ** block_levels(key_of[0], (K, P_SIZE), ((1, 256),), -0.2, 0.2)), 0.05, 1.0)
    water_mask = place_ends((jax.random.randint(key_of[1], (P_SIZE,), 0, 8) < 7).astype(jnp.int32), jax.random.fold_in(key_of[1], 1), 0, 1)
    courant = jnp.clip(jnp.exp(jax.random.uniform(key_of[2], (2, K), jnp.float32, math.log(0.05), math.log(0.3))), 0.05, 0.3)
    stencil_sign = place_ends(jax.random.randint(key_of[3], (2, K), 0, 2), jax.random.fold_in(key_of[3], 1), 0, 1).astype(jnp.int32)
    quad_index = place_ends(jax.random.randint(key_of[4], (4, K, 2), 0, K), jax.random.fold_in(key_of[4], 1), 0, K - 1).astype(jnp.int32)
    quad_weight = jnp.clip(jax.random.uniform(key_of[5], (4, K, 2), jnp.float32, 0.2, 1.0), 0.2, 1.0)
    nonlinear = jnp.clip(jnp.exp(jax.random.uniform(key_of[6], (K,), jnp.float32, math.log(0.01), math.log(0.1))), 0.01, 0.1)
    stokes_table = noise(key_of[7], (2 * L, K), K ** -0.5, 0.1875)
    point_index = draw_point_index(jax.random.fold_in(key_of[16], 71), 0)
    point_weight = jnp.clip(0.1 + 0.3 * jax.random.uniform(key_of[9], (4, P_SIZE), jnp.float32) ** block_levels(key_of[9], (4, P_SIZE), ((1, 256),), -0.2, 0.2), 0.1, 0.4)
    ocean_index = draw_ocean_index(jax.random.fold_in(key_of[16], 71), 0)
    ocean_weight = jnp.clip(0.1 + 0.3 * jax.random.uniform(key_of[11], (4, NOC), jnp.float32) ** block_levels(key_of[11], (4, NOC), ((1, 256),), -0.2, 0.2), 0.1, 0.4)
    currents = noise(key_of[12], (2, L, NOC), 0.5, 3.0, ((2, 256),), jnp.float32)
    coriolis = jnp.clip(0.2 + 0.400000021 * jax.random.uniform(key_of[13], (NOC,), jnp.float32) ** block_levels(key_of[13], (NOC,), ((0, 256),), -0.2, 0.2), 0.2, 0.6)
    mixing = jnp.clip(jax.random.uniform(key_of[14], (L,), jnp.float32, 0.05, 0.2), 0.05, 0.2)
    surface_weights = jnp.clip(jnp.exp(jax.random.uniform(key_of[15], (L,), jnp.float32, math.log(0.005), math.log(0.05))), 0.005, 0.05)
    return dict(spectrum=spectrum, water_mask=water_mask, courant=courant, stencil_sign=stencil_sign, quad_index=quad_index, quad_weight=quad_weight, nonlinear=nonlinear, stokes_table=stokes_table, point_index=point_index, point_weight=point_weight, ocean_index=ocean_index, ocean_weight=ocean_weight, currents=currents, coriolis=coriolis, mixing=mixing, surface_weights=surface_weights)


ocean_step_size = 0.5


def advect(spectra, padded, point_flow, courant, stencil_sign):
    eastward = stencil_sign[0][:, None, None] == 1
    northward = stencil_sign[1][:, None, None] == 1
    sense_x = (2 * stencil_sign[0] - 1).astype(jnp.float32)[:, None, None]
    sense_y = (2 * stencil_sign[1] - 1).astype(jnp.float32)[:, None, None]
    behind_x = jnp.where(eastward, jnp.roll(spectra, 1, axis=2), jnp.roll(spectra, -1, axis=2))
    behind_y = jnp.where(northward, padded[:, :-2], padded[:, 2:])
    speed_x = courant[0][:, None, None] * (1.0 + 0.5 * jnp.tanh(sense_x * point_flow[0][None]))
    speed_y = courant[1][:, None, None] * (1.0 + 0.5 * jnp.tanh(sense_y * point_flow[1][None]))
    return spectra - speed_x * (spectra - behind_x) - speed_y * (spectra - behind_y)


def nonlinear_update(advected, interps, gain_rows, wet_row):
    total_sum = interps[0] + interps[1] + interps[2] + interps[3]
    pair_sum = interps[0] * interps[1] + interps[2] * interps[3]
    source = advected * advected * total_sum - advected * pair_sum
    return wet_row[None, :] * (advected + gain_rows[:, None] * source)


def vertical_mix(profile, mixing):
    above_level = jnp.concatenate([profile[:1], profile[:-1]], axis=0)
    below_level = jnp.concatenate([profile[1:], profile[-1:]], axis=0)
    return mixing[:, None, None] * (above_level - 2.0 * profile + below_level)


def ocean_tendency(zonal_flow, meridional, padded_zonal, mixing):
    vorticity = 0.5 * (jnp.roll(meridional, -1, axis=2) - jnp.roll(meridional, 1, axis=2)) - 0.5 * (padded_zonal[:, 2:] - padded_zonal[:, :-2])
    return vorticity, vertical_mix(zonal_flow, mixing), vertical_mix(meridional, mixing)


def ocean_advance(zonal_flow, meridional, tendency, stokes_drift, rotation):
    vorticity, mix_zonal, mix_meridional = tendency
    drift_x = stokes_drift[0]
    drift_y = stokes_drift[1]
    new_zonal = zonal_flow + ocean_step_size * (rotation[None] * (meridional + drift_y) + vorticity * drift_y + mix_zonal)
    new_meridional = meridional + ocean_step_size * (-rotation[None] * (zonal_flow + drift_x) - vorticity * drift_x + mix_meridional)
    return jnp.stack([new_zonal, new_meridional])


def reference(spectrum, water_mask, courant, stencil_sign, quad_index, quad_weight, nonlinear, stokes_table, point_index, point_weight, ocean_index, ocean_weight, currents, coriolis, mixing, surface_weights):
    repeated = quad_index[:, :, 0] == quad_index[:, :, 1]
    first_weight = jnp.where(repeated, quad_weight[:, :, 0] + quad_weight[:, :, 1], quad_weight[:, :, 0]).astype(jnp.bfloat16).astype(jnp.float32)
    second_weight = jnp.where(repeated, jnp.zeros_like(quad_weight[:, :, 1]), quad_weight[:, :, 1]).astype(jnp.bfloat16).astype(jnp.float32)
    first_index = quad_index[:, :, 0]
    second_index = quad_index[:, :, 1]
    wet_points = water_mask.astype(jnp.float32)
    stokes_rows = stokes_table.astype(jnp.float32)
    rotation = coriolis.reshape(MY, OX)
    ocean_state = currents
    spectra = spectrum
    for step_index in range(STEPS):
        surface = jnp.sum(surface_weights[None, :, None] * ocean_state, axis=1)
        point_flow = sum(point_weight[config][None, :] * surface[:, point_index[config]] for config in range(4))
        map_grid = spectra.reshape(K, MY, MX)
        padded = jnp.concatenate([map_grid[:, -1:], map_grid, map_grid[:, :1]], axis=1)
        advected = advect(map_grid, padded, point_flow.reshape(2, MY, MX), courant, stencil_sign)
        rounded = lax.optimization_barrier(advected.astype(jnp.bfloat16)).astype(jnp.float32)

        def one_block(pieces):
            block_rows, block_rounded, block_wet = pieces
            interps = first_weight[:, :, None] * block_rounded[first_index] + second_weight[:, :, None] * block_rounded[second_index]
            return nonlinear_update(block_rows, interps, nonlinear, block_wet)

        updated = lax.map(one_block, (advected.transpose(1, 0, 2), rounded.transpose(1, 0, 2), wet_points.reshape(MY, MX)))
        spectra = updated.transpose(1, 0, 2).reshape(K, MY * MX)
        spectra_rounded = lax.optimization_barrier(spectra.astype(jnp.bfloat16)).astype(jnp.float32)
        stokes = jnp.dot(stokes_rows, spectra_rounded, precision=lax.Precision.HIGHEST)
        stokes_drift = sum(ocean_weight[config][None, :] * stokes[:, ocean_index[config]] for config in range(4))
        stokes_drift = stokes_drift.reshape(2, L, MY, OX)
        zonal_flow = ocean_state[0].reshape(L, MY, OX)
        meridional = ocean_state[1].reshape(L, MY, OX)
        padded_zonal = jnp.concatenate([zonal_flow[:, -1:], zonal_flow, zonal_flow[:, :1]], axis=1)
        tendency = ocean_tendency(zonal_flow, meridional, padded_zonal, mixing)
        ocean_state = ocean_advance(zonal_flow, meridional, tendency, stokes_drift, rotation).reshape(2, L, MY * OX)
    return spectra, ocean_state
```

```python
import functools

import jax
import jax.numpy as jnp
from jax import lax
from jax.experimental import pallas as pl
from jax.experimental.pallas import tpu as pltpu
from jax.sharding import PartitionSpec as P

K = 1024
L = 64
MX = 256
OX = 128
AXES = ("mp", "dev")
EXTRA = 40
FAST = 576
F32 = jnp.float32
BF16 = jnp.bfloat16
VMEM = pl.BlockSpec(memory_space=pltpu.VMEM)
SMEM = pl.BlockSpec(memory_space=pltpu.SMEM)
HIGHEST = lax.Precision.HIGHEST


def dot_nt(a, b):
    return lax.dot_general(a, b, (((1,), (1,)), ((), ())), preferred_element_type=F32)


def dot_nn(a, b):
    return jnp.dot(a, b, preferred_element_type=F32)


def dot_exact(a, b):
    return jnp.dot(a, b, precision=HIGHEST, preferred_element_type=F32)


def split3(x):
    high = x.astype(BF16)
    rest = x - high.astype(F32)
    middle = rest.astype(BF16)
    low = (rest - middle.astype(F32)).astype(BF16)
    return high, middle, low


def one_hot_rows(select_ref, pos_ref):
    place = lax.broadcasted_iota(jnp.int32, (K, 128), 0).astype(F32)
    for block in range(8):
        hit = place == pos_ref[block : block + 1, :]
        select_ref[:, block * 128 : (block + 1) * 128] = jnp.where(hit, 1.0, 0.0).astype(BF16)


def pack_kernel(
    count, sign, spectrum, currents, level, ocean_index, ocean_weight,
    up, down, pos, surface, select, parts,
):
    for block in range(8):
        pos[block : block + 1, :] = sign[1:2, block * 128 : (block + 1) * 128].astype(F32)
    ones = pos[...]
    upper = lax.broadcasted_iota(jnp.int32, (128, 128), 0) <= lax.broadcasted_iota(
        jnp.int32, (128, 128), 1
    )
    before = dot_nn(ones.astype(BF16), jnp.where(upper, 1.0, 0.0).astype(BF16))
    running = jnp.zeros((1, 1), F32)
    counts = []
    for block in range(8):
        counts.append(before[block : block + 1, :] + running)
        running = running + before[block : block + 1, 127:128]
    lane = lax.broadcasted_iota(jnp.int32, (1, 128), 1).astype(F32)
    for block in range(8):
        index = lane + float(block * 128)
        first = counts[block] - 1.0
        second = running + index - counts[block]
        pos[block : block + 1, :] = jnp.where(ones[block : block + 1, :] > 0.5, first, second)
    one_hot_rows(select, pos)
    high, middle, low = split3(spectrum[...])
    parts[:, 0:MX] = high
    parts[:, MX : 2 * MX] = middle
    parts[:, 2 * MX : 3 * MX] = low
    for block in range(4):
        rows = slice(block * 256, (block + 1) * 256)
        got = dot_nn(select[rows, :], parts[...])
        value = got[:, 0:MX] + (got[:, MX : 2 * MX] + got[:, 2 * MX :])
        top = min((block + 1) * 256, count)
        if top > block * 256:
            up[block * 256 : top, :] = value[: top - block * 256]
        skip = K - count
        start = max(block * 256, skip)
        if start < (block + 1) * 256:
            down[start - skip : (block + 1) * 256 - skip, :] = value[start - block * 256 :]
    weights = jnp.broadcast_to(level[...], (8, L))
    flat_u = dot_exact(weights, currents[0])
    flat_v = dot_exact(weights, currents[1])
    surface[...] = flat_u
    surface[1:2, :] = flat_v[0:1, :]
    for message in (up, down):
        message[count : count + 1, 0:OX] = flat_u[0:1, :]
        message[count : count + 1, OX : 2 * OX] = flat_v[0:1, :]
        message[count + 1 : count + 5, 0:OX] = ocean_index[...].astype(F32)
        message[count + 1 : count + 5, OX : 2 * OX] = ocean_weight[...]
        message[count + 5 : count + 8, :] = jnp.zeros((3, MX), F32)
        message[count + 8 : count + 40, 0:OX] = currents[0, 0 : L // 2, :]
        message[count + 8 : count + 40, OX : 2 * OX] = currents[0, L // 2 :, :]


def table_kernel(
    row, pos, sign, courant, nonlinear, quad_index, quad_weight, stokes_table, point_index,
    point_weight, quad, back, stokes_sorted, wide, spread, select, rows, parts,
):
    one_hot_rows(select, pos)
    sense = (2 * sign[...] - 1).astype(F32)
    speed = courant[...]
    rows[...] = jnp.zeros((32, K), F32)
    rows[0:2, :] = speed
    rows[2:4, :] = 0.5 * speed * sense
    rows[4:6, :] = sense
    rows[6:7, :] = nonlinear[...]
    for config in range(4):
        index = quad_index[config]
        weight = quad_weight[config]
        same = index[0:1] == index[1:2]
        first = jnp.where(same, weight[0:1] + weight[1:2], weight[0:1])
        second = jnp.where(same, 0.0, weight[1:2])
        rows[8 + 2 * config : 9 + 2 * config, :] = first.astype(BF16).astype(F32)
        rows[9 + 2 * config : 10 + 2 * config, :] = second.astype(BF16).astype(F32)
        rows[16 + 2 * config : 18 + 2 * config, :] = index.astype(F32)
    high, middle, low = split3(rows[...])
    parts[0:32, :] = high
    parts[32:64, :] = middle
    parts[64:96, :] = low
    component = lax.broadcasted_iota(jnp.int32, (16, K), 1)
    line = lax.broadcasted_iota(jnp.int32, (16, K), 0)
    digits = jnp.where(line == 0, component // 32, component % 32).astype(F32).astype(BF16)
    found = dot_nt(digits, select[...])
    order = found[0:1] * 32.0 + found[1:2]
    stokes_sorted[...] = dot_nt(stokes_table[...], select[...]).astype(BF16)

    def block_rows(block, carry):
        at = pl.ds(pl.multiple_of(block * 64, 64), 64)
        got = dot_nt(select[at, :], parts[...])
        column = got[:, 0:32] + (got[:, 32:64] + got[:, 64:96])
        for item in range(7):
            wide[item, at, :] = jnp.broadcast_to(column[:, item : item + 1], (64, 128))
        original = (lax.broadcasted_iota(jnp.int32, (64, K), 0) + block * 64).astype(F32)
        back[at, :] = jnp.where(order == original, 1.0, 0.0).astype(BF16)
        for config in range(4):
            a = 8 + 2 * config
            b = 16 + 2 * config
            value = jnp.where(
                order == column[:, b : b + 1],
                column[:, a : a + 1],
                jnp.where(order == column[:, b + 1 : b + 2], column[:, a + 1 : a + 2], 0.0),
            )
            quad[config, at, :] = value.astype(BF16)
        return carry

    lax.fori_loop(0, K // 64, block_rows, 0)
    here = row[0]
    for shift in range(3):
        base = ((here + (shift + 255)) % 256) * OX
        slot = lax.broadcasted_iota(jnp.int32, (OX, MX), 0) + base
        total = jnp.zeros((OX, MX), F32)
        for config in range(4):
            total = total + jnp.where(
                point_index[config : config + 1, :] == slot, point_weight[config : config + 1, :], 0.0
            )
        spread[shift * OX : (shift + 1) * OX, :] = total


def cell_table(base, index, weight):
    point = (lax.broadcasted_iota(jnp.int32, (MX, OX), 0) + base).astype(F32)
    total = jnp.zeros((MX, OX), F32)
    for config in range(4):
        total = total + jnp.where(
            index[config : config + 1, :] == point, weight[config : config + 1, :], 0.0
        )
    return total


def update(count, own_up, own_down, from_below, from_above, flow, quad, wide, stokes_sorted, wet,
           write, advected, rounded, finished):
    bend = jnp.tanh(flow)
    bend_x = bend[0:1, :]
    bend_y = bend[1:2, :]
    skip = K - count
    size = 32

    def advect(start, own, shift, behind):
        def body(block, carry):
            at = pl.multiple_of(block * size + start, size)
            here = own[pl.ds(at - shift, size), :]
            west = pltpu.roll(here, 1, 1)
            east = pltpu.roll(here, MX - 1, 1)

            def both(item):
                half = wide[item, pl.ds(at, size), :]
                return jnp.concatenate([half, half], axis=1)

            behind_x = jnp.where(both(4) > 0.0, west, east)
            speed_x = both(0) + both(2) * bend_x
            speed_y = both(1) + both(3) * bend_y
            value = here - speed_x * (here - behind_x) - speed_y * (here - behind(at, both))
            advected[pl.ds(at, size), :] = value
            rounded[pl.ds(at, size), :] = value.astype(BF16)
            return carry

        return body

    def below(at, both):
        return from_below[pl.ds(at, size), :]

    def above(at, both):
        return from_above[pl.ds(at - skip, size), :]

    def either(at, both):
        return jnp.where(both(5) > 0.0, below(at, both), above(at, both))

    if skip:
        lax.fori_loop(0, skip // size, advect(0, own_up, 0, below), 0)
    lax.fori_loop(0, (count - skip) // size, advect(skip, own_up, 0, either), 0)
    if skip:
        lax.fori_loop(0, skip // size, advect(count, own_down, skip, above), 0)

    def source(block, carry):
        at = pl.ds(pl.multiple_of(block * 64, 64), 64)
        interp = [dot_nn(quad[config, at, :], rounded[...]) for config in range(4)]
        value = advected[at, :]
        pairs = interp[0] * interp[1] + interp[2] * interp[3]
        total = (interp[0] + interp[1]) + (interp[2] + interp[3])
        gain = wide[6, at, :]
        gain = jnp.concatenate([gain, gain], axis=1)
        result = wet * (value + gain * (value * (value * total - pairs)))
        advected[at, :] = result
        finished[at, :] = result.astype(BF16)
        return carry

    lax.fori_loop(0, K // 64, source, 0)
    write(advected)
    return dot_nn(stokes_sorted[...], finished[...])


def flow_of(below_surface, own_surface, above_surface, spread):
    wide_u = jnp.concatenate([below_surface[0], own_surface[0], above_surface[0]], axis=1)
    wide_v = jnp.concatenate([below_surface[1], own_surface[1], above_surface[1]], axis=1)
    line = lax.broadcasted_iota(jnp.int32, (8, 3 * OX), 0)
    both = jnp.where(line == 0, wide_u, wide_v)
    return dot_exact(both, spread[...])


def first_kernel(
    count, row, own_up, own_down, from_below, from_above, surface, quad, wide, stokes_sorted, spread,
    wet, ocean_index, ocean_weight, up, down, to_below, own_part, to_above, cells,
    advected, rounded, finished,
):
    base = row[0] * MX
    cells[:, 0:OX] = cell_table(
        base, from_below[count + 1 : count + 5, 0:OX], from_below[count + 1 : count + 5, OX:]
    )
    cells[:, OX : 2 * OX] = cell_table(base, ocean_index[...].astype(F32), ocean_weight[...])
    cells[:, 2 * OX :] = cell_table(
        base, from_above[count + 1 : count + 5, 0:OX], from_above[count + 1 : count + 5, OX:]
    )
    sides = [
        (message[count : count + 1, 0:OX], message[count : count + 1, OX:])
        for message in (from_below, from_above)
    ]
    flow = flow_of(sides[0], (surface[0:1, :], surface[1:2, :]), sides[1], spread)

    def write(result):
        up[...] = result[0:count, :]
        down[...] = result[K - count :, :]

    stokes = update(count, own_up, own_down, from_below, from_above, flow, quad, wide, stokes_sorted,
                    wet[...], write, advected, rounded, finished)
    part = dot_exact(stokes, cells[...])
    to_below[...] = part[:, 0:OX]
    own_part[...] = part[:, OX : 2 * OX]
    to_above[...] = part[:, 2 * OX :]


def second_kernel(
    count, own_up, own_down, from_below, from_above, ocean_below, ocean_own, ocean_above, quad, wide,
    stokes_sorted, spread, wet, cells, spectra, to_below, own_part, to_above,
    advected, rounded, finished,
):
    sides = [
        (message[L : L + 1, :], message[L + 1 : L + 2, :])
        for message in (ocean_below, ocean_own, ocean_above)
    ]
    flow = flow_of(sides[0], sides[1], sides[2], spread)

    def write(result):
        spectra[...] = result[...]

    stokes = update(count, own_up, own_down, from_below, from_above, flow, quad, wide, stokes_sorted,
                    wet[...], write, advected, rounded, finished)
    part = dot_exact(stokes, cells[...])
    to_below[...] = part[:, 0:OX]
    own_part[...] = part[:, OX : 2 * OX]
    to_above[...] = part[:, 2 * OX :]


def restore_kernel(spectra, back, out):
    high, middle, low = split3(spectra[...])
    out[...] = dot_nn(back[...], high) + (dot_nn(back[...], middle) + dot_nn(back[...], low))


def mix(profile, mixing):
    line = lax.broadcasted_iota(jnp.int32, (L, OX), 0)
    before = jnp.where(line == 0, profile, pltpu.roll(profile, 1, 0))
    after = jnp.where(line == L - 1, profile, pltpu.roll(profile, L - 1, 0))
    return mixing * (before - 2.0 * profile + after)


def ocean_step(u, v, u_below, u_above, drift, rotation, mixing):
    vorticity = 0.5 * (pltpu.roll(v, OX - 1, 1) - pltpu.roll(v, 1, 1)) - 0.5 * (u_above - u_below)
    drift_x = drift[0:L, :]
    drift_y = drift[L:, :]
    new_u = u + 0.5 * (rotation * (v + drift_y) + vorticity * drift_y + mix(u, mixing))
    new_v = v + 0.5 * (-rotation * (u + drift_x) - vorticity * drift_x + mix(v, mixing))
    return new_u, new_v


def first_ocean(
    count, currents, from_below, from_above, part_below, own_part, part_above, coriolis, mixing, level,
    state, message,
):
    half = L // 2

    def zonal(block):
        rows = block[count + 8 : count + 40, :]
        return jnp.concatenate([rows[0:half, 0:OX], rows[0:half, OX:]], axis=0)

    drift = own_part[...] + part_below[...] + part_above[...]
    new_u, new_v = ocean_step(
        currents[0], currents[1], zonal(from_below), zonal(from_above), drift, coriolis[...], mixing[...]
    )
    state[0] = new_u
    state[1] = new_v
    weights = jnp.broadcast_to(level[...], (8, L))
    message[0:L, :] = new_u
    message[L:, :] = dot_exact(weights, new_u)
    message[L + 1 : L + 2, :] = dot_exact(weights, new_v)[0:1, :]


def second_ocean(
    state, ocean_below, ocean_above, part_below, own_part, part_above, coriolis, mixing, out
):
    drift = own_part[...] + part_below[...] + part_above[...]
    new_u, new_v = ocean_step(
        state[0], state[1], ocean_below[0:L, :], ocean_above[0:L, :], drift, coriolis[...], mixing[...]
    )
    out[0] = new_u
    out[1] = new_v


def shape(*dims, dtype=F32):
    return jax.ShapeDtypeStruct(dims, dtype)


def call(body, outs, scratch=(), scalars=0, inputs=0, flops=0, data=0, name=None):
    return pl.pallas_call(
        body,
        out_shape=outs,
        in_specs=[SMEM] * scalars + [VMEM] * (inputs - scalars),
        out_specs=jax.tree.map(lambda _: VMEM, outs),
        scratch_shapes=scratch,
        cost_estimate=pl.CostEstimate(flops=flops, bytes_accessed=data, transcendentals=0),
        compiler_params=pltpu.CompilerParams(vmem_limit_bytes=40 << 20),
        name=name,
    )


def exchange(to_above, to_below):
    total = lax.axis_size("mp") * lax.axis_size("dev")
    up = [(i, (i + 1) % total) for i in range(total)]
    return (
        lax.ppermute(to_above, AXES, up),
        lax.ppermute(to_below, AXES, [(b, a) for a, b in up]),
    )


def program(
    count, row, spectrum, wet, courant, stencil_sign, quad_index, quad_weight, nonlinear, stokes_table,
    point_index, point_weight, ocean_index, ocean_weight, currents, coriolis, mixing, level,
):
    part = shape(128, OX)
    work = (pltpu.VMEM((K, MX), F32), pltpu.VMEM((K, MX), BF16), pltpu.VMEM((K, MX), BF16))
    up, down, pos, surface = call(
        functools.partial(pack_kernel, count),
        (shape(count + EXTRA, MX), shape(count + EXTRA, MX), shape(8, 128), shape(8, 128)),
        (pltpu.VMEM((K, K), BF16), pltpu.VMEM((K, 3 * MX), BF16)),
        inputs=6, flops=2 * K * K * 3 * MX, data=1 << 20, name="pack",
    )(stencil_sign, spectrum, currents, level, ocean_index, ocean_weight)
    below, above = exchange(up, down)
    quad, back, stokes_sorted, wide, spread = call(
        table_kernel,
        (
            shape(4, K, K, dtype=BF16), shape(K, K, dtype=BF16), shape(128, K, dtype=BF16),
            shape(7, K, 128), shape(3 * OX, MX),
        ),
        (pltpu.VMEM((K, K), BF16), pltpu.VMEM((32, K), F32), pltpu.VMEM((96, K), BF16)),
        scalars=1, inputs=10, flops=8 << 30, data=12 << 20, name="tables",
    )(row, pos, stencil_sign, courant, nonlinear, quad_index, quad_weight, stokes_table, point_index,
      point_weight)
    up, down, to_below, own_part, to_above, cells = call(
        functools.partial(first_kernel, count),
        (shape(count, MX), shape(count, MX), part, part, part, shape(MX, 3 * OX)),
        work, scalars=1, inputs=13, flops=3 << 30, data=12 << 20, name="first",
    )(row, up, down, below, above, surface, quad, wide, stokes_sorted, spread, wet, ocean_index,
      ocean_weight)
    part_below, part_above = exchange(to_above, to_below)
    next_below, next_above = exchange(up, down)
    state, message = call(
        functools.partial(first_ocean, count),
        (shape(2, L, OX), shape(L + 8, OX)),
        inputs=9, flops=1 << 20, data=1 << 18, name="ocean",
    )(currents, below, above, part_below, own_part, part_above, coriolis, mixing, level)
    ocean_below, ocean_above = exchange(message, message)
    spectra, to_below, own_part, to_above = call(
        functools.partial(second_kernel, count),
        (shape(K, MX), part, part, part),
        work, inputs=13, flops=3 << 30, data=12 << 20, name="second",
    )(up, down, next_below, next_above, ocean_below, message, ocean_above, quad, wide, stokes_sorted,
      spread, wet, cells)
    part_below, part_above = exchange(to_above, to_below)
    out = call(
        restore_kernel, shape(K, MX), inputs=2, flops=2 * K * K * 3 * MX, data=4 << 20, name="restore",
    )(spectra, back)
    final = call(
        second_ocean, shape(2, L, OX), inputs=8, flops=1 << 20, data=1 << 18, name="ocean_end",
    )(state, ocean_below, ocean_above, part_below, own_part, part_above, coriolis, mixing)
    return out, final


def local(
    spectrum, water_mask, courant, stencil_sign, quad_index, quad_weight, nonlinear, stokes_table,
    point_index, point_weight, ocean_index, ocean_weight, currents, coriolis, mixing, surface_weights,
):
    row = (lax.axis_index("mp") * lax.axis_size("dev") + lax.axis_index("dev")).reshape(1)
    arguments = (
        row.astype(jnp.int32),
        spectrum,
        water_mask.astype(F32).reshape(1, MX),
        courant,
        stencil_sign,
        quad_index.transpose(0, 2, 1),
        quad_weight.transpose(0, 2, 1),
        nonlinear.reshape(1, K),
        stokes_table,
        point_index,
        point_weight,
        ocean_index,
        ocean_weight,
        currents,
        coriolis.reshape(1, OX),
        jnp.broadcast_to(mixing[:, None], (L, OX)),
        surface_weights.reshape(1, L),
    )
    northward = jnp.sum(stencil_sign[1])
    balanced = jnp.logical_and(northward <= FAST, K - northward <= FAST)
    return lax.cond(
        balanced, functools.partial(program, FAST), functools.partial(program, K), *arguments
    )


def solution(mesh):
    whole = P(AXES)
    last = P(None, AXES)
    return jax.shard_map(
        local,
        mesh=mesh,
        in_specs=(
            last, whole, P(), P(), P(), P(), P(), P(), last, last, last, last,
            P(None, None, AXES), whole, P(), P(),
        ),
        out_specs=(last, P(None, None, AXES)),
        check_vma=False,
    )
```

```python
import functools

import jax
import jax.numpy as jnp
from jax import lax
from jax.experimental import pallas as pl
from jax.experimental.pallas import tpu as pltpu
from jax.sharding import PartitionSpec as P

K = 1024
L = 64
MX = 256
OX = 128
AXES = ("mp", "dev")
EXTRA = 72
LIMIT = 24 << 20
FAST = 576
F32 = jnp.float32
BF16 = jnp.bfloat16
VMEM = pl.BlockSpec(memory_space=pltpu.VMEM)
SMEM = pl.BlockSpec(memory_space=pltpu.SMEM)
HIGHEST = lax.Precision.HIGHEST


def dot_nt(a, b):
    return lax.dot_general(a, b, (((1,), (1,)), ((), ())), preferred_element_type=F32)


def dot_nn(a, b):
    return jnp.dot(a, b, preferred_element_type=F32)


def dot_exact(a, b):
    return jnp.dot(a, b, precision=HIGHEST, preferred_element_type=F32)


def split3(x):
    high = x.astype(BF16)
    rest = x - high.astype(F32)
    middle = rest.astype(BF16)
    low = (rest - middle.astype(F32)).astype(BF16)
    return high, middle, low


def one_hot_rows(select_ref, pos_ref):
    place = lax.broadcasted_iota(jnp.int32, (K, 128), 0).astype(F32)
    for block in range(8):
        hit = place == pos_ref[block : block + 1, :]
        select_ref[:, block * 128 : (block + 1) * 128] = jnp.where(hit, 1.0, 0.0).astype(BF16)


def pack_kernel(
    count, sign, spectrum, currents, level, coriolis, ocean_index, ocean_weight,
    up, down, pos, surface, zonal, fits, select, parts,
):
    for block in range(8):
        pos[block : block + 1, :] = sign[1:2, block * 128 : (block + 1) * 128].astype(F32)
    ones = pos[...]
    upper = lax.broadcasted_iota(jnp.int32, (128, 128), 0) <= lax.broadcasted_iota(
        jnp.int32, (128, 128), 1
    )
    before = dot_nn(ones.astype(BF16), jnp.where(upper, 1.0, 0.0).astype(BF16))
    running = jnp.zeros((1, 1), F32)
    counts = []
    for block in range(8):
        counts.append(before[block : block + 1, :] + running)
        running = running + before[block : block + 1, 127:128]
    northward = jnp.sum(running)
    fits[0] = jnp.logical_and(northward <= count, K - northward <= count).astype(jnp.int32)
    lane = lax.broadcasted_iota(jnp.int32, (1, 128), 1).astype(F32)
    for block in range(8):
        index = lane + float(block * 128)
        first = counts[block] - 1.0
        second = running + index - counts[block]
        pos[block : block + 1, :] = jnp.where(ones[block : block + 1, :] > 0.5, first, second)
    one_hot_rows(select, pos)
    high, middle, low = split3(spectrum[...])
    parts[:, 0:MX] = high
    parts[:, MX : 2 * MX] = middle
    parts[:, 2 * MX : 3 * MX] = low
    got = dot_nn(select[...], parts[...])
    value = got[:, 0:MX] + (got[:, MX : 2 * MX] + got[:, 2 * MX :])
    up[0:count, :] = value[0:count]
    down[0:count, :] = value[K - count :]
    weights = jnp.broadcast_to(level[...], (8, L))
    flat_u = dot_exact(weights, currents[0])
    flat_v = dot_exact(weights, currents[1])
    surface[...] = flat_u
    surface[1:2, :] = flat_v[0:1, :]
    zonal[...] = currents[0]
    half = L // 2
    for message in (up, down):
        message[count : count + 1, 0:OX] = flat_u[0:1, :]
        message[count : count + 1, OX : 2 * OX] = flat_v[0:1, :]
        message[count + 1 : count + 5, 0:OX] = ocean_index[...].astype(F32)
        message[count + 1 : count + 5, OX : 2 * OX] = ocean_weight[...]
        message[count + 5 : count + 8, :] = jnp.zeros((3, MX), F32)
        message[count + 5 : count + 6, 0:OX] = coriolis[...]
        for flow in range(2):
            at = count + 8 + flow * half
            message[at : at + half, 0:OX] = currents[flow, 0:half, :]
            message[at : at + half, OX : 2 * OX] = currents[flow, half:, :]


def table_kernel(
    row, pos, sign, courant, nonlinear, quad_index, quad_weight, stokes_table, point_index,
    point_weight, quad, back, stokes_sorted, wide, spread, select, rows, parts, columns,
):
    one_hot_rows(select, pos)
    sense = (2 * sign[...] - 1).astype(F32)
    speed = courant[...]
    rows[...] = jnp.zeros((32, K), F32)
    rows[0:2, :] = speed
    rows[2:4, :] = 0.5 * speed * sense
    rows[4:6, :] = sense
    rows[6:7, :] = nonlinear[...]
    for config in range(4):
        index = quad_index[config]
        weight = quad_weight[config]
        same = index[0:1] == index[1:2]
        first = jnp.where(same, weight[0:1] + weight[1:2], weight[0:1])
        second = jnp.where(same, 0.0, weight[1:2])
        rows[8 + 2 * config : 9 + 2 * config, :] = first.astype(BF16).astype(F32)
        rows[9 + 2 * config : 10 + 2 * config, :] = second.astype(BF16).astype(F32)
        rows[16 + 2 * config : 18 + 2 * config, :] = index.astype(F32)
    high, middle, low = split3(rows[...])
    parts[0:32, :] = high
    parts[32:64, :] = middle
    parts[64:96, :] = low
    component = lax.broadcasted_iota(jnp.int32, (16, K), 1)
    line = lax.broadcasted_iota(jnp.int32, (16, K), 0)
    digits = jnp.where(line == 0, component // 32, component % 32).astype(F32).astype(BF16)
    found = dot_nt(digits, select[...])
    order = found[0:1] * 32.0 + found[1:2]
    stokes_sorted[...] = dot_nt(stokes_table[...], select[...]).astype(BF16)

    got = dot_nt(select[...], parts[...])
    columns[...] = got[:, 0:32] + (got[:, 32:64] + got[:, 64:96])

    def block_rows(block, carry):
        at = pl.ds(pl.multiple_of(block * 64, 64), 64)
        column = columns[at, :]
        for item in range(7):
            wide[item, at, :] = jnp.broadcast_to(column[:, item : item + 1], (64, 128))
        original = (lax.broadcasted_iota(jnp.int32, (64, K), 0) + block * 64).astype(F32)
        back[at, :] = jnp.where(order == original, 1.0, 0.0).astype(BF16)
        for config in range(4):
            a = 8 + 2 * config
            b = 16 + 2 * config
            value = jnp.where(
                order == column[:, b : b + 1],
                column[:, a : a + 1],
                jnp.where(order == column[:, b + 1 : b + 2], column[:, a + 1 : a + 2], 0.0),
            )
            quad[config, at, :] = value.astype(BF16)
        return carry

    lax.fori_loop(0, K // 64, block_rows, 0)
    here = row[0]
    for shift in range(3):
        base = ((here + (shift + 255)) % 256) * OX
        slot = lax.broadcasted_iota(jnp.int32, (OX, MX), 0) + base
        total = jnp.zeros((OX, MX), F32)
        for config in range(4):
            total = total + jnp.where(
                point_index[config : config + 1, :] == slot, point_weight[config : config + 1, :], 0.0
            )
        spread[shift * OX : (shift + 1) * OX, :] = total


def cell_table(base, index, weight):
    point = (lax.broadcasted_iota(jnp.int32, (MX, OX), 0) + base).astype(F32)
    total = jnp.zeros((MX, OX), F32)
    for config in range(4):
        total = total + jnp.where(
            index[config : config + 1, :] == point, weight[config : config + 1, :], 0.0
        )
    return total


def update(count, own_up, own_down, from_below, from_above, flow, quad, wide, stokes_sorted, wet,
           advected, rounded, interp):
    bend = jnp.tanh(flow)
    bend_x = bend[0:1, :]
    bend_y = bend[1:2, :]
    skip = K - count
    size = 32

    def advect(start, own, shift, behind):
        def body(block, carry):
            at = pl.multiple_of(block * size + start, size)
            here = own[pl.ds(at - shift, size), :]
            west = pltpu.roll(here, 1, 1)
            east = pltpu.roll(here, MX - 1, 1)

            def both(item):
                half = wide[item, pl.ds(at, size), :]
                return jnp.concatenate([half, half], axis=1)

            behind_x = jnp.where(both(4) > 0.0, west, east)
            speed_x = both(0) + both(2) * bend_x
            speed_y = both(1) + both(3) * bend_y
            value = here - speed_x * (here - behind_x) - speed_y * (here - behind(at, both))
            advected[pl.ds(at, size), :] = value
            rounded[pl.ds(at, size), :] = value.astype(BF16)
            return carry

        return body

    def below(at, both):
        return from_below[pl.ds(at, size), :]

    def above(at, both):
        return from_above[pl.ds(at - skip, size), :]

    def either(at, both):
        return jnp.where(both(5) > 0.0, below(at, both), above(at, both))

    if skip:
        lax.fori_loop(0, skip // size, advect(0, own_up, 0, below), 0)
    lax.fori_loop(0, (count - skip) // size, advect(skip, own_up, 0, either), 0)
    if skip:
        lax.fori_loop(0, skip // size, advect(count, own_down, skip, above), 0)

    for config in range(4):
        interp[config] = dot_nn(quad[config], rounded[...])

    def source(block, carry):
        at = pl.ds(pl.multiple_of(block * size, size), size)
        members = [interp[config, at, :] for config in range(4)]
        value = advected[at, :]
        pairs = members[0] * members[1] + members[2] * members[3]
        total = (members[0] + members[1]) + (members[2] + members[3])
        gain = wide[6, at, :]
        gain = jnp.concatenate([gain, gain], axis=1)
        result = wet * (value + gain * (value * (value * total - pairs)))
        advected[at, :] = result
        rounded[at, :] = result.astype(BF16)
        return carry

    lax.fori_loop(0, K // size, source, 0)
    return dot_nn(stokes_sorted[...], rounded[...])


def flow_of(below_surface, own_surface, above_surface, spread):
    wide_u = jnp.concatenate([below_surface[0], own_surface[0], above_surface[0]], axis=1)
    wide_v = jnp.concatenate([below_surface[1], own_surface[1], above_surface[1]], axis=1)
    line = lax.broadcasted_iota(jnp.int32, (8, 3 * OX), 0)
    both = jnp.where(line == 0, wide_u, wide_v)
    return dot_exact(both, spread[...])


def tall(block):
    return jnp.concatenate([block[:, 0:OX], block[:, OX:]], axis=0)


def turn(v, u_below, u_above):
    return 0.5 * (pltpu.roll(v, OX - 1, 1) - pltpu.roll(v, 1, 1)) - 0.5 * (u_above - u_below)


def mix(profile, mixing):
    line = lax.broadcasted_iota(jnp.int32, (L, OX), 0)
    before = jnp.where(line == 0, profile, pltpu.roll(profile, 1, 0))
    after = jnp.where(line == L - 1, profile, pltpu.roll(profile, L - 1, 0))
    return mixing * (before - 2.0 * profile + after)


def ocean_step(u, v, u_below, u_above, drift, rotation, mixing):
    vorticity = turn(v, u_below, u_above)
    drift_x = drift[0:L, :]
    drift_y = drift[L:, :]
    new_u = u + 0.5 * (rotation * (v + drift_y) + vorticity * drift_y + mix(u, mixing))
    new_v = v + 0.5 * (-rotation * (u + drift_x) - vorticity * drift_x + mix(v, mixing))
    return new_u, new_v


def level_sum(weights, x):
    return jnp.sum(weights * x, axis=0, keepdims=True)


def first_kernel(
    count, row, own_up, own_down, from_below, from_above, below_two, above_two, surface, quad, wide,
    stokes_sorted, spread, wet, ocean_index, ocean_weight, currents, coriolis, mixing, level,
    up, down, own_part, surface_part, far_up, far_down, cells, advected, rounded, interp,
):
    base = row[0] * MX
    half = L // 2
    below_extra = from_below[count:, :]
    above_extra = from_above[count:, :]
    cells[:, 0:OX] = cell_table(base, below_extra[1:5, 0:OX], below_extra[1:5, OX:])
    cells[:, OX : 2 * OX] = cell_table(base, ocean_index[...].astype(F32), ocean_weight[...])
    cells[:, 2 * OX :] = cell_table(base, above_extra[1:5, 0:OX], above_extra[1:5, OX:])
    sides = [(extra[0:1, 0:OX], extra[0:1, OX:]) for extra in (below_extra, above_extra)]
    flow = flow_of(sides[0], (surface[0:1, :], surface[1:2, :]), sides[1], spread)
    wet_row = wet[...].astype(F32)
    stokes = update(count, own_up, own_down, from_below, from_above, flow, quad, wide, stokes_sorted,
                    wet_row, advected, rounded, interp)
    up[0:count, :] = advected[0:count, :]
    down[0:count, :] = advected[K - count :, :]
    part = dot_exact(stokes, cells[...])
    u, v = currents[0], currents[1]
    u_below, v_below = tall(below_extra[8 : 8 + half]), tall(below_extra[8 + half : 8 + 2 * half])
    u_above, v_above = tall(above_extra[8 : 8 + half]), tall(above_extra[8 + half : 8 + 2 * half])
    weights = level[...]
    rotations = (below_extra[5:6, 0:OX], coriolis[...], above_extra[5:6, 0:OX])
    turns = (turn(v_below, below_two[...], u), turn(v, u_below, u_above), turn(v_above, u, above_two[...]))
    shares = []
    for side in range(3):
        factor = 0.5 * weights * (rotations[side] + turns[side])
        block = part[:, side * OX : (side + 1) * OX]
        shares.append((jnp.sum(factor * block[L:], axis=0, keepdims=True),
                       -jnp.sum(factor * block[0:L], axis=0, keepdims=True)))
    own_u = shares[1][0] + level_sum(weights, u + 0.5 * (coriolis[...] * v + mix(u, mixing[...])))
    own_v = shares[1][1] + level_sum(weights, v + 0.5 * (mix(v, mixing[...]) - coriolis[...] * u))
    own_part[...] = part[:, OX : 2 * OX]
    surface_part[...] = jnp.zeros((8, MX), F32)
    for side, message, far in ((0, down, far_down), (2, up, far_up)):
        block = part[:, side * OX : (side + 1) * OX]
        message[count : count + L, 0:OX] = block[0:L]
        message[count : count + L, OX:] = block[L:]
        message[count + L :, :] = jnp.zeros((8, MX), F32)
        message[count + L : count + L + 1, 0:OX] = own_u
        message[count + L : count + L + 1, OX:] = own_v
        message[count + L + 1 : count + L + 2, 0:OX] = shares[side][0]
        message[count + L + 1 : count + L + 2, OX:] = shares[side][1]
        far[...] = jnp.zeros((8, MX), F32)
        far[0:1, 0:OX] = shares[side][0]
        far[0:1, OX:] = shares[side][1]
        at = side // 2
        surface_part[at : at + 1, 0:OX] = shares[side][0]
        surface_part[at : at + 1, OX:] = shares[side][1]
    surface_part[2:3, 0:OX] = own_u
    surface_part[2:3, OX:] = own_v


def second_kernel(
    count, own_up, own_down, from_below, from_above, below_two, above_two, zonal_below, zonal_above,
    own_part, surface_part, quad, wide, stokes_sorted, spread, wet, cells, currents, coriolis, mixing,
    spectra, state, to_above, to_below, last_part, rounded, interp,
):
    half = L // 2
    below_extra = from_below[count:, :]
    above_extra = from_above[count:, :]
    own = surface_part[...]
    surf_below = below_extra[L : L + 1] + below_two[0:1, :] + own[0:1]
    surf_own = own[2:3] + below_extra[L + 1 : L + 2] + above_extra[L + 1 : L + 2]
    surf_above = above_extra[L : L + 1] + above_two[0:1, :] + own[1:2]
    flow = flow_of(*[(x[:, 0:OX], x[:, OX:]) for x in (surf_below, surf_own, surf_above)], spread)
    drift = own_part[...] + tall(below_extra[0:L]) + tall(above_extra[0:L])
    new_u, new_v = ocean_step(
        currents[0], currents[1], tall(zonal_below[count + 8 : count + 8 + half, :]),
        tall(zonal_above[count + 8 : count + 8 + half, :]), drift, coriolis[...], mixing[...]
    )
    state[0] = new_u
    state[1] = new_v
    wet_row = wet[...].astype(F32)
    stokes = update(count, own_up, own_down, from_below, from_above, flow, quad, wide, stokes_sorted,
                    wet_row, spectra, rounded, interp)
    part = dot_exact(stokes, cells[...])
    to_below[0:128, :] = part[:, 0:OX]
    last_part[...] = part[:, OX : 2 * OX]
    to_above[0:128, :] = part[:, 2 * OX :]
    to_below[128:, :] = new_u
    to_above[128:, :] = new_u


def restore_kernel(spectra, back, out):
    high, middle, low = split3(spectra[...])
    out[...] = dot_nn(back[...], high) + (dot_nn(back[...], middle) + dot_nn(back[...], low))


def last_ocean(state, from_below, from_above, own_part, coriolis, mixing, out):
    drift = own_part[...] + from_below[0:128, :] + from_above[0:128, :]
    new_u, new_v = ocean_step(
        state[0], state[1], from_below[128:, :], from_above[128:, :], drift, coriolis[...], mixing[...]
    )
    out[0] = new_u
    out[1] = new_v


def shape(*dims, dtype=F32):
    return jax.ShapeDtypeStruct(dims, dtype)


def call(body, outs, scratch=(), scalars=0, inputs=0, flops=0, data=0, name=None, out_specs=None):
    return pl.pallas_call(
        body,
        out_shape=outs,
        in_specs=[SMEM] * scalars + [VMEM] * (inputs - scalars),
        out_specs=out_specs or jax.tree.map(lambda _: VMEM, outs),
        scratch_shapes=scratch,
        cost_estimate=pl.CostEstimate(flops=flops, bytes_accessed=data, transcendentals=0),
        compiler_params=pltpu.CompilerParams(vmem_limit_bytes=LIMIT),
        name=name,
    )


def exchange(to_above, to_below, distance=1):
    total = lax.axis_size("mp") * lax.axis_size("dev")
    up = [(i, (i + distance) % total) for i in range(total)]
    return (
        lax.ppermute(to_above, AXES, up),
        lax.ppermute(to_below, AXES, [(b, a) for a, b in up]),
    )


def pack(count, stencil_sign, spectrum, currents, level, coriolis, ocean_index, ocean_weight):
    message = shape(count + EXTRA, MX)
    return call(
        functools.partial(pack_kernel, count),
        (message, message, shape(8, 128), shape(8, 128), shape(L, OX), shape(1, dtype=jnp.int32)),
        (pltpu.VMEM((K, K), BF16), pltpu.VMEM((K, 3 * MX), BF16)),
        inputs=7, flops=2 * K * K * 3 * MX, data=1 << 20, name="pack",
        out_specs=(VMEM, VMEM, VMEM, VMEM, VMEM, SMEM),
    )(stencil_sign, spectrum, currents, level, coriolis, ocean_index, ocean_weight)


def steps(
    count, packed, row, wet, courant, stencil_sign, quad_index, quad_weight, nonlinear, stokes_table,
    point_index, point_weight, ocean_index, ocean_weight, currents, coriolis, mixing, level_wide,
):
    up, down, pos, surface, zonal = packed
    part = shape(128, OX)
    message = shape(count + EXTRA, MX)
    far = shape(8, MX)
    work = (pltpu.VMEM((K, MX), BF16), pltpu.VMEM((4, K, MX), F32))
    below, above = exchange(up, down)
    quad, back, stokes_sorted, wide, spread = call(
        table_kernel,
        (
            shape(4, K, K, dtype=BF16), shape(K, K, dtype=BF16), shape(128, K, dtype=BF16),
            shape(7, K, 128), shape(3 * OX, MX),
        ),
        (pltpu.VMEM((K, K), BF16), pltpu.VMEM((32, K), F32), pltpu.VMEM((96, K), BF16),
         pltpu.VMEM((K, 32), F32)),
        scalars=1, inputs=10, flops=4 << 30, data=12 << 20, name="tables",
    )(row, pos, stencil_sign, courant, nonlinear, quad_index, quad_weight, stokes_table, point_index,
      point_weight)
    below_two, above_two = exchange(zonal, zonal, 2)
    next_up, next_down, own_part, surface_part, far_up, far_down, cells = call(
        functools.partial(first_kernel, count),
        (message, message, part, far, far, far, shape(MX, 3 * OX)),
        (pltpu.VMEM((K, MX), F32),) + work,
        scalars=1, inputs=19, flops=3 << 30, data=12 << 20, name="first",
    )(row, up, down, below, above, below_two, above_two, surface, quad, wide, stokes_sorted, spread,
      wet, ocean_index, ocean_weight, currents, coriolis, mixing, level_wide)
    next_below, next_above = exchange(next_up, next_down)
    far_below, far_above = exchange(far_up, far_down, 2)
    end = shape(128 + L, OX)
    spectra, state, to_above, to_below, last_part = call(
        functools.partial(second_kernel, count),
        (shape(K, MX), shape(2, L, OX), end, end, part),
        work, inputs=19, flops=3 << 30, data=12 << 20, name="second",
    )(next_up, next_down, next_below, next_above, far_below, far_above, below, above, own_part,
      surface_part, quad, wide, stokes_sorted, spread, wet, cells, currents, coriolis, mixing)
    end_below, end_above = exchange(to_above, to_below)
    out = call(
        restore_kernel, shape(K, MX), inputs=2, flops=2 * K * K * 3 * MX, data=4 << 20, name="restore",
    )(spectra, back)
    final = call(
        last_ocean, shape(2, L, OX), inputs=6, flops=1 << 20, data=1 << 18, name="ocean",
    )(state, end_below, end_above, last_part, coriolis, mixing)
    return out, final


def local(
    spectrum, water_mask, courant, stencil_sign, quad_index, quad_weight, nonlinear, stokes_table,
    point_index, point_weight, ocean_index, ocean_weight, currents, coriolis, mixing, surface_weights,
):
    row = (lax.axis_index("mp") * lax.axis_size("dev") + lax.axis_index("dev")).reshape(1)
    rotation = coriolis.reshape(1, OX)
    level = surface_weights.reshape(1, L)
    to_pack = (stencil_sign, spectrum, currents, level, rotation, ocean_index, ocean_weight)
    *packed, fits = pack(FAST, *to_pack)
    rest = (
        row.astype(jnp.int32),
        water_mask.reshape(1, MX),
        courant,
        stencil_sign,
        quad_index.transpose(0, 2, 1),
        quad_weight.transpose(0, 2, 1),
        nonlinear.reshape(1, K),
        stokes_table,
        point_index,
        point_weight,
        ocean_index,
        ocean_weight,
        currents,
        rotation,
        jnp.broadcast_to(mixing[:, None], (L, OX)),
        jnp.broadcast_to(surface_weights[:, None], (L, OX)),
    )

    def balanced(packed, to_pack, rest):
        return steps(FAST, packed, *rest)

    def general(packed, to_pack, rest):
        return steps(K, pack(K, *to_pack)[:-1], *rest)

    return lax.cond(fits[0] == 1, balanced, general, tuple(packed), to_pack, rest)


def solution(mesh):
    whole = P(AXES)
    last = P(None, AXES)
    return jax.shard_map(
        local,
        mesh=mesh,
        in_specs=(
            last, whole, P(), P(), P(), P(), P(), P(), last, last, last, last,
            P(None, None, AXES), whole, P(), P(),
        ),
        out_specs=(last, P(None, None, AXES)),
        check_vma=False,
    )
```

```python
import functools

import jax
import jax.numpy as jnp
from jax import lax
from jax.experimental import pallas as pl
from jax.experimental.pallas import tpu as pltpu
from jax.sharding import PartitionSpec as P

K = 1024
L = 64
MX = 256
OX = 128
AXES = ("mp", "dev")
EXTRA = 72
LIMIT = 24 << 20
FAST = 576
F32 = jnp.float32
BF16 = jnp.bfloat16
VMEM = pl.BlockSpec(memory_space=pltpu.VMEM)
SMEM = pl.BlockSpec(memory_space=pltpu.SMEM)
HIGHEST = lax.Precision.HIGHEST


def dot_nt(a, b):
    return lax.dot_general(a, b, (((1,), (1,)), ((), ())), preferred_element_type=F32)


def dot_nn(a, b):
    return jnp.dot(a, b, preferred_element_type=F32)


def dot_exact(a, b):
    return jnp.dot(a, b, precision=HIGHEST, preferred_element_type=F32)


def split3(x):
    high = x.astype(BF16)
    rest = x - high.astype(F32)
    middle = rest.astype(BF16)
    low = (rest - middle.astype(F32)).astype(BF16)
    return high, middle, low


def one_hot_rows(select_ref, pos_ref, copies=1):
    place = lax.broadcasted_iota(jnp.int32, (K, 128), 0).astype(F32)
    for block in range(8):
        hit = place == pos_ref[block : block + 1, :]
        ones = jnp.where(hit, 1.0, 0.0).astype(BF16)
        for copy in range(copies):
            start = copy * K + block * 128
            select_ref[:, start : start + 128] = ones


def pack_kernel(
    count, sign, spectrum, currents, level, coriolis, ocean_index, ocean_weight,
    up, down, pos, surface, zonal, fits, select, parts,
):
    for block in range(8):
        pos[block : block + 1, :] = sign[1:2, block * 128 : (block + 1) * 128].astype(F32)
    ones = pos[...]
    upper = lax.broadcasted_iota(jnp.int32, (128, 128), 0) <= lax.broadcasted_iota(
        jnp.int32, (128, 128), 1
    )
    before = dot_nn(ones.astype(BF16), jnp.where(upper, 1.0, 0.0).astype(BF16))
    running = jnp.zeros((1, 1), F32)
    counts = []
    for block in range(8):
        counts.append(before[block : block + 1, :] + running)
        running = running + before[block : block + 1, 127:128]
    northward = jnp.sum(running)
    fits[0] = jnp.logical_and(northward <= count, K - northward <= count).astype(jnp.int32)
    lane = lax.broadcasted_iota(jnp.int32, (1, 128), 1).astype(F32)
    for block in range(8):
        index = lane + float(block * 128)
        first = counts[block] - 1.0
        second = running + index - counts[block]
        pos[block : block + 1, :] = jnp.where(ones[block : block + 1, :] > 0.5, first, second)
    one_hot_rows(select, pos, 3)
    high, middle, low = split3(spectrum[...])
    parts[0:K, :] = low
    parts[K : 2 * K, :] = middle
    parts[2 * K :, :] = high
    value = dot_nn(select[...], parts[...])
    up[0:count, :] = value[0:count, :]
    down[0:count, :] = value[K - count :, :]
    weights = jnp.broadcast_to(level[...], (8, L))
    flat_u = dot_exact(weights, currents[0])
    flat_v = dot_exact(weights, currents[1])
    surface[...] = flat_u
    surface[1:2, :] = flat_v[0:1, :]
    zonal[...] = currents[0]
    half = L // 2
    for message in (up, down):
        message[count : count + 1, 0:OX] = flat_u[0:1, :]
        message[count : count + 1, OX : 2 * OX] = flat_v[0:1, :]
        message[count + 1 : count + 5, 0:OX] = ocean_index[...].astype(F32)
        message[count + 1 : count + 5, OX : 2 * OX] = ocean_weight[...]
        message[count + 5 : count + 8, :] = jnp.zeros((3, MX), F32)
        message[count + 5 : count + 6, 0:OX] = coriolis[...]
        for flow in range(2):
            at = count + 8 + flow * half
            message[at : at + half, 0:OX] = currents[flow, 0:half, :]
            message[at : at + half, OX : 2 * OX] = currents[flow, half:, :]


def table_kernel(
    row, pos, sign, courant, nonlinear, quad_index, quad_weight, stokes_table, point_index,
    point_weight, mixing, level, quad, back, stokes_sorted, wide, cell_column, cell_side, cell_weight,
    mixing_wide, level_wide, select, rows, parts, columns,
):
    one_hot_rows(select, pos)
    sense = (2 * sign[...] - 1).astype(F32)
    speed = courant[...]
    rows[...] = jnp.zeros((32, K), F32)
    rows[0:2, :] = speed
    rows[2:4, :] = 0.5 * speed * sense
    rows[4:6, :] = sense
    rows[6:7, :] = nonlinear[...]
    for config in range(4):
        index = quad_index[config]
        weight = quad_weight[config]
        same = index[0:1] == index[1:2]
        first = jnp.where(same, weight[0:1] + weight[1:2], weight[0:1])
        second = jnp.where(same, 0.0, weight[1:2])
        rows[8 + 2 * config : 9 + 2 * config, :] = first.astype(BF16).astype(F32)
        rows[9 + 2 * config : 10 + 2 * config, :] = second.astype(BF16).astype(F32)
        rows[16 + 2 * config : 18 + 2 * config, :] = index.astype(F32)
    high, middle, low = split3(rows[...])
    parts[0:32, :] = high
    parts[32:64, :] = middle
    parts[64:96, :] = low
    component = lax.broadcasted_iota(jnp.int32, (16, K), 1)
    line = lax.broadcasted_iota(jnp.int32, (16, K), 0)
    digits = jnp.where(line == 0, component // 32, component % 32).astype(F32).astype(BF16)
    found = dot_nt(digits, select[...])
    order = found[0:1] * 32.0 + found[1:2]
    stokes_sorted[...] = dot_nt(stokes_table[...], select[...]).astype(BF16)

    got = dot_nt(select[...], parts[...])
    columns[...] = got[:, 0:32] + (got[:, 32:64] + got[:, 64:96])

    def block_rows(block, carry):
        at = pl.ds(pl.multiple_of(block * 64, 64), 64)
        column = columns[at, :]
        for item in range(7):
            wide[item, at, :] = jnp.broadcast_to(column[:, item : item + 1], (64, 128))
        original = (lax.broadcasted_iota(jnp.int32, (64, K), 0) + block * 64).astype(F32)
        back[at, :] = jnp.where(order == original, 1.0, 0.0).astype(BF16)
        for config in range(4):
            a = 8 + 2 * config
            b = 16 + 2 * config
            value = jnp.where(
                order == column[:, b : b + 1],
                column[:, a : a + 1],
                jnp.where(order == column[:, b + 1 : b + 2], column[:, a + 1 : a + 2], 0.0),
            )
            quad[config, at, :] = value.astype(BF16)
        return carry

    lax.fori_loop(0, K // 64, block_rows, 0)
    for config in range(4):
        for half in range(2):
            line = slice(2 * config + half, 2 * config + half + 1)
            cell = point_index[config : config + 1, half * 128 : (half + 1) * 128]
            cell_column[line, :] = cell % OX
            cell_side[line, :] = (cell // OX - row[0] + 257) % 256
            cell_weight[line, :] = point_weight[config : config + 1, half * 128 : (half + 1) * 128]
    diagonal = lax.broadcasted_iota(jnp.int32, (L, L), 0) == lax.broadcasted_iota(jnp.int32, (L, L), 1)
    for line, wide_column in ((mixing, mixing_wide), (level, level_wide)):
        column = jnp.sum(jnp.where(diagonal, line[...], 0.0), axis=1, keepdims=True)
        wide_column[...] = jnp.broadcast_to(column, (L, OX))


def cell_table(base, index, weight):
    point = (lax.broadcasted_iota(jnp.int32, (MX, OX), 0) + base).astype(F32)
    total = jnp.zeros((MX, OX), F32)
    for config in range(4):
        total = total + jnp.where(
            index[config : config + 1, :] == point, weight[config : config + 1, :], 0.0
        )
    return total


def update(count, own_up, own_down, from_below, from_above, flow, quad, wide, stokes_sorted, wet,
           advected, rounded, interp):
    bend_x = jnp.tanh(flow[0])
    bend_y = jnp.tanh(flow[1])
    skip = K - count
    size = 64

    def advect(start, own, shift, behind):
        def body(block, carry):
            at = pl.multiple_of(block * size + start, size)
            here = own[pl.ds(at - shift, size), :]
            west = pltpu.roll(here, 1, 1)
            east = pltpu.roll(here, MX - 1, 1)

            def both(item):
                half = wide[item, pl.ds(at, size), :]
                return jnp.concatenate([half, half], axis=1)

            behind_x = jnp.where(both(4) > 0.0, west, east)
            speed_x = both(0) + both(2) * bend_x
            speed_y = both(1) + both(3) * bend_y
            value = here - speed_x * (here - behind_x) - speed_y * (here - behind(at, both))
            advected[pl.ds(at, size), :] = value
            rounded[pl.ds(at, size), :] = value.astype(BF16)
            return carry

        return body

    def below(at, both):
        return from_below[pl.ds(at, size), :]

    def above(at, both):
        return from_above[pl.ds(at - skip, size), :]

    def either(at, both):
        return jnp.where(both(5) > 0.0, below(at, both), above(at, both))

    if skip:
        lax.fori_loop(0, skip // size, advect(0, own_up, 0, below), 0)
    lax.fori_loop(0, (count - skip) // size, advect(skip, own_up, 0, either), 0)
    if skip:
        lax.fori_loop(0, skip // size, advect(count, own_down, skip, above), 0)

    def member(config, carry):
        interp[config] = dot_nn(quad[config], rounded[...])
        return carry

    lax.fori_loop(0, 4, member, 0)

    def source(block, carry):
        at = pl.ds(pl.multiple_of(block * size, size), size)
        members = [interp[config, at, :] for config in range(4)]
        value = advected[at, :]
        pairs = members[0] * members[1] + members[2] * members[3]
        total = (members[0] + members[1]) + (members[2] + members[3])
        gain = wide[6, at, :]
        gain = jnp.concatenate([gain, gain], axis=1)
        result = wet * (value + gain * (value * (value * total - pairs)))
        advected[at, :] = result
        rounded[at, :] = result.astype(BF16)
        return carry

    lax.fori_loop(0, K // size, source, 0)
    return dot_nn(stokes_sorted[...], rounded[...])


def flow_of(sides, column, side, weight):
    index = column[...]
    where = side[...]
    flow = []
    for component in range(2):
        total = jnp.zeros((8, OX), F32)
        for item in range(3):
            line = jnp.broadcast_to(sides[item][:, component * OX : (component + 1) * OX], (8, OX))
            got = jnp.take_along_axis(line, index, axis=1, mode="promise_in_bounds")
            total = jnp.where(where == item, got, total)
        total = total * weight[...]
        halves = [
            (total[h : h + 1] + total[h + 2 : h + 3]) + (total[h + 4 : h + 5] + total[h + 6 : h + 7])
            for h in range(2)
        ]
        flow.append(jnp.concatenate(halves, axis=1))
    return flow


def drift_parts(stokes, cells, cells_low):
    high = stokes.astype(BF16)
    low = (stokes - high.astype(F32)).astype(BF16)
    both = dot_nn(jnp.concatenate([high, low], axis=0), cells[...])
    return both[0:128] + (both[128:] + dot_nn(high, cells_low[...]))


def tall(block):
    return jnp.concatenate([block[:, 0:OX], block[:, OX:]], axis=0)


def turn(v, u_below, u_above):
    return 0.5 * (pltpu.roll(v, OX - 1, 1) - pltpu.roll(v, 1, 1)) - 0.5 * (u_above - u_below)


def mix(profile, mixing):
    line = lax.broadcasted_iota(jnp.int32, (L, OX), 0)
    before = jnp.where(line == 0, profile, pltpu.roll(profile, 1, 0))
    after = jnp.where(line == L - 1, profile, pltpu.roll(profile, L - 1, 0))
    return mixing * (before - 2.0 * profile + after)


def ocean_step(u, v, u_below, u_above, drift, rotation, mixing):
    vorticity = turn(v, u_below, u_above)
    drift_x = drift[0:L, :]
    drift_y = drift[L:, :]
    new_u = u + 0.5 * (rotation * (v + drift_y) + vorticity * drift_y + mix(u, mixing))
    new_v = v + 0.5 * (-rotation * (u + drift_x) - vorticity * drift_x + mix(v, mixing))
    return new_u, new_v


def level_sum(weights, x):
    return jnp.sum(weights * x, axis=0, keepdims=True)


def first_kernel(
    count, row, own_up, own_down, from_below, from_above, below_two, above_two, surface, quad, wide,
    stokes_sorted, cell_column, cell_side, cell_weight, wet, ocean_index, ocean_weight, currents,
    coriolis, mixing, level,
    up, down, own_part, surface_part, far_up, far_down, cells, cells_low, advected, rounded, interp,
):
    base = row[0] * MX
    half = L // 2
    below_extra = from_below[count:, :]
    above_extra = from_above[count:, :]
    for side, index, weight in (
        (0, below_extra[1:5, 0:OX], below_extra[1:5, OX:]),
        (1, ocean_index[...].astype(F32), ocean_weight[...]),
        (2, above_extra[1:5, 0:OX], above_extra[1:5, OX:]),
    ):
        table = cell_table(base, index, weight)
        high = table.astype(BF16)
        cells[:, side * OX : (side + 1) * OX] = high
        cells_low[:, side * OX : (side + 1) * OX] = (table - high.astype(F32)).astype(BF16)
    own = jnp.concatenate([surface[0:1, :], surface[1:2, :]], axis=1)
    sides = (below_extra[0:1, :], own, above_extra[0:1, :])
    flow = flow_of(sides, cell_column, cell_side, cell_weight)
    wet_row = wet[...].astype(F32)
    stokes = update(count, own_up, own_down, from_below, from_above, flow, quad, wide, stokes_sorted,
                    wet_row, advected, rounded, interp)
    up[0:count, :] = advected[0:count, :]
    down[0:count, :] = advected[K - count :, :]
    part = drift_parts(stokes, cells, cells_low)
    u, v = currents[0], currents[1]
    u_below, v_below = tall(below_extra[8 : 8 + half]), tall(below_extra[8 + half : 8 + 2 * half])
    u_above, v_above = tall(above_extra[8 : 8 + half]), tall(above_extra[8 + half : 8 + 2 * half])
    weights = level[...]
    rotations = (below_extra[5:6, 0:OX], coriolis[...], above_extra[5:6, 0:OX])
    turns = (turn(v_below, below_two[...], u), turn(v, u_below, u_above), turn(v_above, u, above_two[...]))
    shares = []
    for side in range(3):
        factor = 0.5 * weights * (rotations[side] + turns[side])
        block = part[:, side * OX : (side + 1) * OX]
        shares.append((jnp.sum(factor * block[L:], axis=0, keepdims=True),
                       -jnp.sum(factor * block[0:L], axis=0, keepdims=True)))
    own_u = shares[1][0] + level_sum(weights, u + 0.5 * (coriolis[...] * v + mix(u, mixing[...])))
    own_v = shares[1][1] + level_sum(weights, v + 0.5 * (mix(v, mixing[...]) - coriolis[...] * u))
    own_part[...] = part[:, OX : 2 * OX]
    surface_part[...] = jnp.zeros((8, MX), F32)
    for side, message, far in ((0, down, far_down), (2, up, far_up)):
        block = part[:, side * OX : (side + 1) * OX]
        message[count : count + L, 0:OX] = block[0:L]
        message[count : count + L, OX:] = block[L:]
        message[count + L :, :] = jnp.zeros((8, MX), F32)
        message[count + L : count + L + 1, 0:OX] = own_u
        message[count + L : count + L + 1, OX:] = own_v
        message[count + L + 1 : count + L + 2, 0:OX] = shares[side][0]
        message[count + L + 1 : count + L + 2, OX:] = shares[side][1]
        far[...] = jnp.zeros((8, MX), F32)
        far[0:1, 0:OX] = shares[side][0]
        far[0:1, OX:] = shares[side][1]
        at = side // 2
        surface_part[at : at + 1, 0:OX] = shares[side][0]
        surface_part[at : at + 1, OX:] = shares[side][1]
    surface_part[2:3, 0:OX] = own_u
    surface_part[2:3, OX:] = own_v


def second_kernel(
    count, own_up, own_down, from_below, from_above, below_two, above_two, zonal_below, zonal_above,
    own_part, surface_part, quad, wide, stokes_sorted, cell_column, cell_side, cell_weight, wet, cells,
    cells_low, currents, coriolis, mixing,
    spectra, state, to_above, to_below, last_part, rounded, interp,
):
    half = L // 2
    below_extra = from_below[count:, :]
    above_extra = from_above[count:, :]
    own = surface_part[...]
    surf_below = below_extra[L : L + 1] + below_two[0:1, :] + own[0:1]
    surf_own = own[2:3] + below_extra[L + 1 : L + 2] + above_extra[L + 1 : L + 2]
    surf_above = above_extra[L : L + 1] + above_two[0:1, :] + own[1:2]
    flow = flow_of((surf_below, surf_own, surf_above), cell_column, cell_side, cell_weight)
    drift = own_part[...] + tall(below_extra[0:L]) + tall(above_extra[0:L])
    new_u, new_v = ocean_step(
        currents[0], currents[1], tall(zonal_below[count + 8 : count + 8 + half, :]),
        tall(zonal_above[count + 8 : count + 8 + half, :]), drift, coriolis[...], mixing[...]
    )
    state[0] = new_u
    state[1] = new_v
    wet_row = wet[...].astype(F32)
    stokes = update(count, own_up, own_down, from_below, from_above, flow, quad, wide, stokes_sorted,
                    wet_row, spectra, rounded, interp)
    part = drift_parts(stokes, cells, cells_low)
    to_below[0:128, :] = part[:, 0:OX]
    last_part[...] = part[:, OX : 2 * OX]
    to_above[0:128, :] = part[:, 2 * OX :]
    to_below[128:, :] = new_u
    to_above[128:, :] = new_u


def restore_kernel(spectra, back, out, parts):
    high, middle, low = split3(spectra[...])
    parts[0] = low
    parts[1] = middle
    parts[2] = high
    out[...] = jnp.zeros((K, MX), F32)

    def add(item, carry):
        out[...] += dot_nn(back[...], parts[item])
        return carry

    lax.fori_loop(0, 3, add, 0)


def last_ocean(state, from_below, from_above, own_part, coriolis, mixing, out):
    drift = own_part[...] + from_below[0:128, :] + from_above[0:128, :]
    new_u, new_v = ocean_step(
        state[0], state[1], from_below[128:, :], from_above[128:, :], drift, coriolis[...], mixing[...]
    )
    out[0] = new_u
    out[1] = new_v


def shape(*dims, dtype=F32):
    return jax.ShapeDtypeStruct(dims, dtype)


def call(body, outs, scratch=(), scalars=0, inputs=0, flops=0, data=0, name=None, out_specs=None):
    return pl.pallas_call(
        body,
        out_shape=outs,
        in_specs=[SMEM] * scalars + [VMEM] * (inputs - scalars),
        out_specs=out_specs or jax.tree.map(lambda _: VMEM, outs),
        scratch_shapes=scratch,
        cost_estimate=pl.CostEstimate(flops=flops, bytes_accessed=data, transcendentals=0),
        compiler_params=pltpu.CompilerParams(vmem_limit_bytes=LIMIT),
        name=name,
    )


def exchange(to_above, to_below, distance=1):
    total = lax.axis_size("mp") * lax.axis_size("dev")
    up = [(i, (i + distance) % total) for i in range(total)]
    return (
        lax.ppermute(to_above, AXES, up),
        lax.ppermute(to_below, AXES, [(b, a) for a, b in up]),
    )


def pack(count, stencil_sign, spectrum, currents, level, coriolis, ocean_index, ocean_weight):
    message = shape(count + EXTRA, MX)
    return call(
        functools.partial(pack_kernel, count),
        (message, message, shape(8, 128), shape(8, 128), shape(L, OX), shape(1, dtype=jnp.int32)),
        (pltpu.VMEM((K, 3 * K), BF16), pltpu.VMEM((3 * K, MX), BF16)),
        inputs=7, flops=2 * K * K * 3 * MX, data=1 << 20, name="pack",
        out_specs=(VMEM, VMEM, VMEM, VMEM, VMEM, SMEM),
    )(stencil_sign, spectrum, currents, level, coriolis, ocean_index, ocean_weight)


def steps(
    count, packed, row, wet, courant, stencil_sign, quad_index, quad_weight, nonlinear, stokes_table,
    point_index, point_weight, ocean_index, ocean_weight, currents, coriolis, mixing, level,
):
    up, down, pos, surface, zonal = packed
    part = shape(128, OX)
    message = shape(count + EXTRA, MX)
    far = shape(8, MX)
    table = shape(MX, 3 * OX, dtype=BF16)
    work = (pltpu.VMEM((K, MX), BF16), pltpu.VMEM((4, K, MX), F32))
    below, above = exchange(up, down)
    whole = jnp.int32
    quad, back, stokes_sorted, wide, cell_column, cell_side, cell_weight, mixing, level = call(
        table_kernel,
        (
            shape(4, K, K, dtype=BF16), shape(K, K, dtype=BF16), shape(128, K, dtype=BF16),
            shape(7, K, 128), shape(8, OX, dtype=whole), shape(8, OX, dtype=whole), shape(8, OX),
            shape(L, OX), shape(L, OX),
        ),
        (pltpu.VMEM((K, K), BF16), pltpu.VMEM((32, K), F32), pltpu.VMEM((96, K), BF16),
         pltpu.VMEM((K, 32), F32)),
        scalars=1, inputs=12, flops=4 << 30, data=12 << 20, name="tables",
    )(row, pos, stencil_sign, courant, nonlinear, quad_index, quad_weight, stokes_table, point_index,
      point_weight, mixing, level)
    below_two, above_two = exchange(zonal, zonal, 2)
    next_up, next_down, own_part, surface_part, far_up, far_down, cells, cells_low = call(
        functools.partial(first_kernel, count),
        (message, message, part, far, far, far, table, table),
        (pltpu.VMEM((K, MX), F32),) + work,
        scalars=1, inputs=21, flops=3 << 30, data=12 << 20, name="first",
    )(row, up, down, below, above, below_two, above_two, surface, quad, wide, stokes_sorted,
      cell_column, cell_side, cell_weight, wet, ocean_index, ocean_weight, currents, coriolis, mixing,
      level)
    next_below, next_above = exchange(next_up, next_down)
    far_below, far_above = exchange(far_up, far_down, 2)
    end = shape(128 + L, OX)
    spectra, state, to_above, to_below, last_part = call(
        functools.partial(second_kernel, count),
        (shape(K, MX), shape(2, L, OX), end, end, part),
        work, inputs=22, flops=3 << 30, data=12 << 20, name="second",
    )(next_up, next_down, next_below, next_above, far_below, far_above, below, above, own_part,
      surface_part, quad, wide, stokes_sorted, cell_column, cell_side, cell_weight, wet, cells,
      cells_low, currents, coriolis, mixing)
    end_below, end_above = exchange(to_above, to_below)
    out = call(
        restore_kernel, shape(K, MX), (pltpu.VMEM((3, K, MX), BF16),), inputs=2, flops=2 * K * K * 3 * MX, data=4 << 20, name="restore",
    )(spectra, back)
    final = call(
        last_ocean, shape(2, L, OX), inputs=6, flops=1 << 20, data=1 << 18, name="ocean",
    )(state, end_below, end_above, last_part, coriolis, mixing)
    return out, final


def local(
    spectrum, water_mask, courant, stencil_sign, quad_index, quad_weight, nonlinear, stokes_table,
    point_index, point_weight, ocean_index, ocean_weight, currents, coriolis, mixing, surface_weights,
):
    row = (lax.axis_index("mp") * lax.axis_size("dev") + lax.axis_index("dev")).reshape(1)
    rotation = coriolis.reshape(1, OX)
    level = surface_weights.reshape(1, L)
    to_pack = (stencil_sign, spectrum, currents, level, rotation, ocean_index, ocean_weight)
    *packed, fits = pack(FAST, *to_pack)
    rest = (
        row.astype(jnp.int32),
        water_mask.reshape(1, MX),
        courant,
        stencil_sign,
        quad_index.transpose(0, 2, 1),
        quad_weight.transpose(0, 2, 1),
        nonlinear.reshape(1, K),
        stokes_table,
        point_index,
        point_weight,
        ocean_index,
        ocean_weight,
        currents,
        rotation,
        mixing.reshape(1, L),
        level,
    )

    def balanced(packed, to_pack, rest):
        return steps(FAST, packed, *rest)

    def general(packed, to_pack, rest):
        return steps(K, pack(K, *to_pack)[:-1], *rest)

    return lax.cond(fits[0] == 1, balanced, general, tuple(packed), to_pack, rest)


def solution(mesh):
    whole = P(AXES)
    last = P(None, AXES)
    return jax.shard_map(
        local,
        mesh=mesh,
        in_specs=(
            last, whole, P(), P(), P(), P(), P(), P(), last, last, last, last,
            P(None, None, AXES), whole, P(), P(),
        ),
        out_specs=(last, P(None, None, AXES)),
        check_vma=False,
    )
```

```python
import functools

import jax
import jax.numpy as jnp
from jax import lax
from jax.experimental import pallas as pl
from jax.experimental.pallas import tpu as pltpu
from jax.sharding import PartitionSpec as P

K = 1024
L = 64
MX = 256
OX = 128
AXES = ("mp", "dev")
EXTRA = 72
LIMIT = 24 << 20
FAST = 560
F32 = jnp.float32
BF16 = jnp.bfloat16
VMEM = pl.BlockSpec(memory_space=pltpu.VMEM)
SMEM = pl.BlockSpec(memory_space=pltpu.SMEM)
HIGHEST = lax.Precision.HIGHEST


def dot_nt(a, b):
    return lax.dot_general(a, b, (((1,), (1,)), ((), ())), preferred_element_type=F32)


def dot_nn(a, b):
    return jnp.dot(a, b, preferred_element_type=F32)


def dot_exact(a, b):
    return jnp.dot(a, b, precision=HIGHEST, preferred_element_type=F32)


def split2(x):
    high = x.astype(BF16)
    return high, (x - high.astype(F32)).astype(BF16)


def split3(x):
    high, middle = split2(x)
    low = (x - high.astype(F32) - middle.astype(F32)).astype(BF16)
    return high, middle, low


def one_hot_rows(select_ref, pos_ref, copies=1):
    place = lax.broadcasted_iota(jnp.int32, (K, 128), 0).astype(F32)
    for block in range(8):
        hit = place == pos_ref[block : block + 1, :]
        ones = jnp.where(hit, 1.0, 0.0).astype(BF16)
        for copy in range(copies):
            start = copy * K + block * 128
            select_ref[:, start : start + 128] = ones


def pack_kernel(
    count, sign, spectrum, currents, level, coriolis, ocean_index, ocean_weight,
    up, down, pos, surface, zonal, fits, select, parts,
):
    for block in range(8):
        pos[block : block + 1, :] = sign[1:2, block * 128 : (block + 1) * 128].astype(F32)
    ones = pos[...]
    upper = lax.broadcasted_iota(jnp.int32, (128, 128), 0) <= lax.broadcasted_iota(
        jnp.int32, (128, 128), 1
    )
    before = dot_nn(ones.astype(BF16), jnp.where(upper, 1.0, 0.0).astype(BF16))
    running = jnp.zeros((1, 1), F32)
    counts = []
    for block in range(8):
        counts.append(before[block : block + 1, :] + running)
        running = running + before[block : block + 1, 127:128]
    northward = jnp.sum(running)
    fits[0] = jnp.logical_and(northward <= count, K - northward <= count).astype(jnp.int32)
    lane = lax.broadcasted_iota(jnp.int32, (1, 128), 1).astype(F32)
    for block in range(8):
        index = lane + float(block * 128)
        first = counts[block] - 1.0
        second = running + index - counts[block]
        pos[block : block + 1, :] = jnp.where(ones[block : block + 1, :] > 0.5, first, second)
    one_hot_rows(select, pos, 2)
    high, low = split2(spectrum[...])
    parts[0:K, :] = low
    parts[K:, :] = high
    value = dot_nn(select[...], parts[...])
    up[0:count, :] = value[0:count, :]
    down[0:count, :] = value[K - count :, :]
    weights = jnp.broadcast_to(level[...], (8, L))
    flat_u = dot_exact(weights, currents[0])
    flat_v = dot_exact(weights, currents[1])
    surface[...] = flat_u
    surface[1:2, :] = flat_v[0:1, :]
    zonal[...] = currents[0]
    half = L // 2
    for message in (up, down):
        message[count : count + 1, 0:OX] = flat_u[0:1, :]
        message[count : count + 1, OX : 2 * OX] = flat_v[0:1, :]
        message[count + 1 : count + 5, 0:OX] = ocean_index[...].astype(F32)
        message[count + 1 : count + 5, OX : 2 * OX] = ocean_weight[...]
        message[count + 5 : count + 8, :] = jnp.zeros((3, MX), F32)
        message[count + 5 : count + 6, 0:OX] = coriolis[...]
        for flow in range(2):
            at = count + 8 + flow * half
            message[at : at + half, 0:OX] = currents[flow, 0:half, :]
            message[at : at + half, OX : 2 * OX] = currents[flow, half:, :]


def table_kernel(
    row, pos, sign, courant, nonlinear, quad_index, quad_weight, stokes_table, point_index,
    point_weight, mixing, level, quad, back, stokes_sorted, wide, cell_column, cell_side, cell_weight,
    mixing_wide, level_wide, select, rows, parts, columns,
):
    one_hot_rows(select, pos)
    sense = (2 * sign[...] - 1).astype(F32)
    speed = courant[...]
    rows[...] = jnp.zeros((32, K), F32)
    rows[0:2, :] = speed
    rows[2:4, :] = 0.5 * speed * sense
    rows[4:6, :] = sense
    rows[6:7, :] = nonlinear[...]
    for config in range(4):
        index = quad_index[config]
        weight = quad_weight[config]
        same = index[0:1] == index[1:2]
        first = jnp.where(same, weight[0:1] + weight[1:2], weight[0:1])
        second = jnp.where(same, 0.0, weight[1:2])
        rows[8 + 2 * config : 9 + 2 * config, :] = first.astype(BF16).astype(F32)
        rows[9 + 2 * config : 10 + 2 * config, :] = second.astype(BF16).astype(F32)
        rows[16 + 2 * config : 18 + 2 * config, :] = index.astype(F32)
    high, middle, low = split3(rows[...])
    parts[0:32, :] = high
    parts[32:64, :] = middle
    parts[64:96, :] = low
    component = lax.broadcasted_iota(jnp.int32, (16, K), 1)
    line = lax.broadcasted_iota(jnp.int32, (16, K), 0)
    digits = jnp.where(line == 0, component // 32, component % 32).astype(F32).astype(BF16)
    found = dot_nt(digits, select[...])
    order = found[0:1] * 32.0 + found[1:2]
    stokes_sorted[...] = dot_nt(stokes_table[...], select[...]).astype(BF16)

    got = dot_nt(select[...], parts[...])
    columns[...] = got[:, 0:32] + (got[:, 32:64] + got[:, 64:96])

    def block_rows(block, carry):
        at = pl.ds(pl.multiple_of(block * 64, 64), 64)
        column = columns[at, :]
        for item in range(7):
            wide[item, at, :] = jnp.broadcast_to(column[:, item : item + 1], (64, 128))
        original = (lax.broadcasted_iota(jnp.int32, (64, K), 0) + block * 64).astype(F32)
        back[at, :] = jnp.where(order == original, 1.0, 0.0).astype(BF16)
        for config in range(4):
            a = 8 + 2 * config
            b = 16 + 2 * config
            value = jnp.where(
                order == column[:, b : b + 1],
                column[:, a : a + 1],
                jnp.where(order == column[:, b + 1 : b + 2], column[:, a + 1 : a + 2], 0.0),
            )
            quad[config, at, :] = value.astype(BF16)
        return carry

    lax.fori_loop(0, K // 64, block_rows, 0)
    for config in range(4):
        for half in range(2):
            line = slice(2 * config + half, 2 * config + half + 1)
            cell = point_index[config : config + 1, half * 128 : (half + 1) * 128]
            cell_column[line, :] = cell % OX
            cell_side[line, :] = (cell // OX - row[0] + 257) % 256
            cell_weight[line, :] = point_weight[config : config + 1, half * 128 : (half + 1) * 128]
    diagonal = lax.broadcasted_iota(jnp.int32, (L, L), 0) == lax.broadcasted_iota(jnp.int32, (L, L), 1)
    for line, wide_column in ((mixing, mixing_wide), (level, level_wide)):
        column = jnp.sum(jnp.where(diagonal, line[...], 0.0), axis=1, keepdims=True)
        wide_column[...] = jnp.broadcast_to(column, (L, OX))


def cell_table(base, index, weight):
    point = (lax.broadcasted_iota(jnp.int32, (MX, OX), 0) + base).astype(F32)
    total = jnp.zeros((MX, OX), F32)
    for config in range(4):
        total = total + jnp.where(
            index[config : config + 1, :] == point, weight[config : config + 1, :], 0.0
        )
    return total


def blocks(start, stop, body):
    for at in range(start, stop, 64):
        body(at, min(64, stop - at))


def slope_kernel(count, own_up, own_down, wide, slope):
    def along(own, shift):
        def body(at, size):
            here = own[pl.ds(at - shift, size), :]
            sense = wide[4, pl.ds(at, size), :]
            sense = jnp.concatenate([sense, sense], axis=1)
            behind = jnp.where(sense > 0.0, pltpu.roll(here, 1, 1), pltpu.roll(here, MX - 1, 1))
            slope[pl.ds(at, size), :] = here - behind

        return body

    blocks(0, count, along(own_up, 0))
    blocks(count, K, along(own_down, K - count))


def update(count, own_up, own_down, from_below, from_above, flow, slope, quad, wide, stokes_sorted, wet,
           advected, rounded, interp):
    bend_x = jnp.tanh(flow[0])
    bend_y = jnp.tanh(flow[1])
    skip = K - count

    def advect(own, shift, behind):
        def body(at, size):
            here = own[pl.ds(at - shift, size), :]
            rows = pl.ds(at, size)
            base_x, base_y, bend_of_x, bend_of_y = [wide[item, rows, :] for item in range(4)]
            step_x = slope[rows, :]
            step_y = here - behind(at, size)
            for half in range(2):
                lanes = slice(half * 128, (half + 1) * 128)
                speed_x = base_x + bend_of_x * bend_x[:, lanes]
                speed_y = base_y + bend_of_y * bend_y[:, lanes]
                value = here[:, lanes] - speed_x * step_x[:, lanes] - speed_y * step_y[:, lanes]
                advected[rows, lanes] = value
                rounded[rows, lanes] = value.astype(BF16)

        return body

    def below(at, size):
        return from_below[pl.ds(at, size), :]

    def above(at, size):
        return from_above[pl.ds(at - skip, size), :]

    def either(at, size):
        sense = wide[5, pl.ds(at, size), :]
        sense = jnp.concatenate([sense, sense], axis=1)
        return jnp.where(sense > 0.0, below(at, size), above(at, size))

    if skip:
        blocks(0, skip, advect(own_up, 0, below))
    blocks(skip, count, advect(own_up, 0, either))
    if skip:
        blocks(count, K, advect(own_down, skip, above))

    def member(config, carry):
        interp[config] = dot_nn(quad[config], rounded[...])
        return carry

    lax.fori_loop(0, 4, member, 0)

    def source(at, size):
        at = pl.ds(at, size)
        members = [interp[config, at, :] for config in range(4)]
        value = advected[at, :]
        pairs = members[0] * members[1] + members[2] * members[3]
        total = (members[0] + members[1]) + (members[2] + members[3])
        gain = wide[6, at, :]
        gain = jnp.concatenate([gain, gain], axis=1)
        result = wet * (value + gain * (value * (value * total - pairs)))
        advected[at, :] = result
        rounded[at, :] = result.astype(BF16)

    blocks(0, K, source)
    return dot_nn(stokes_sorted[...], rounded[...])


def flow_of(sides, column, side, weight):
    index = column[...]
    where = side[...]
    flow = []
    for component in range(2):
        total = jnp.zeros((8, OX), F32)
        for item in range(3):
            line = jnp.broadcast_to(sides[item][:, component * OX : (component + 1) * OX], (8, OX))
            got = jnp.take_along_axis(line, index, axis=1, mode="promise_in_bounds")
            total = jnp.where(where == item, got, total)
        total = total * weight[...]
        halves = [
            (total[h : h + 1] + total[h + 2 : h + 3]) + (total[h + 4 : h + 5] + total[h + 6 : h + 7])
            for h in range(2)
        ]
        flow.append(jnp.concatenate(halves, axis=1))
    return flow


def drift_parts(stokes, cells, cells_low):
    high = stokes.astype(BF16)
    low = (stokes - high.astype(F32)).astype(BF16)
    both = dot_nn(jnp.concatenate([high, low], axis=0), cells[...])
    return both[0:128] + (both[128:] + dot_nn(high, cells_low[...]))


def tall(block):
    return jnp.concatenate([block[:, 0:OX], block[:, OX:]], axis=0)


def turn(v, u_below, u_above):
    return 0.5 * (pltpu.roll(v, OX - 1, 1) - pltpu.roll(v, 1, 1)) - 0.5 * (u_above - u_below)


def mix(profile, mixing):
    line = lax.broadcasted_iota(jnp.int32, (L, OX), 0)
    before = jnp.where(line == 0, profile, pltpu.roll(profile, 1, 0))
    after = jnp.where(line == L - 1, profile, pltpu.roll(profile, L - 1, 0))
    return mixing * (before - 2.0 * profile + after)


def ocean_step(u, v, u_below, u_above, drift, rotation, mixing):
    vorticity = turn(v, u_below, u_above)
    drift_x = drift[0:L, :]
    drift_y = drift[L:, :]
    new_u = u + 0.5 * (rotation * (v + drift_y) + vorticity * drift_y + mix(u, mixing))
    new_v = v + 0.5 * (-rotation * (u + drift_x) - vorticity * drift_x + mix(v, mixing))
    return new_u, new_v


def level_sum(weights, x):
    return jnp.sum(weights * x, axis=0, keepdims=True)


def first_kernel(
    count, row, own_up, own_down, from_below, from_above, below_two, above_two, surface, slope, quad, wide,
    stokes_sorted, cell_column, cell_side, cell_weight, wet, ocean_index, ocean_weight, currents,
    coriolis, mixing, level,
    up, down, own_part, surface_part, far_up, far_down, cells, cells_low, advected, rounded, interp,
):
    base = row[0] * MX
    half = L // 2
    below_extra = from_below[count:, :]
    above_extra = from_above[count:, :]
    for side, index, weight in (
        (0, below_extra[1:5, 0:OX], below_extra[1:5, OX:]),
        (1, ocean_index[...].astype(F32), ocean_weight[...]),
        (2, above_extra[1:5, 0:OX], above_extra[1:5, OX:]),
    ):
        table = cell_table(base, index, weight)
        high = table.astype(BF16)
        cells[:, side * OX : (side + 1) * OX] = high
        cells_low[:, side * OX : (side + 1) * OX] = (table - high.astype(F32)).astype(BF16)
    own = jnp.concatenate([surface[0:1, :], surface[1:2, :]], axis=1)
    sides = (below_extra[0:1, :], own, above_extra[0:1, :])
    flow = flow_of(sides, cell_column, cell_side, cell_weight)
    wet_row = wet[...].astype(F32)
    stokes = update(count, own_up, own_down, from_below, from_above, flow, slope, quad, wide,
                    stokes_sorted, wet_row, advected, rounded, interp)
    up[0:count, :] = advected[0:count, :]
    down[0:count, :] = advected[K - count :, :]
    part = drift_parts(stokes, cells, cells_low)
    u, v = currents[0], currents[1]
    u_below, v_below = tall(below_extra[8 : 8 + half]), tall(below_extra[8 + half : 8 + 2 * half])
    u_above, v_above = tall(above_extra[8 : 8 + half]), tall(above_extra[8 + half : 8 + 2 * half])
    weights = level[...]
    rotations = (below_extra[5:6, 0:OX], coriolis[...], above_extra[5:6, 0:OX])
    turns = (turn(v_below, below_two[...], u), turn(v, u_below, u_above), turn(v_above, u, above_two[...]))
    shares = []
    for side in range(3):
        factor = 0.5 * weights * (rotations[side] + turns[side])
        block = part[:, side * OX : (side + 1) * OX]
        shares.append((jnp.sum(factor * block[L:], axis=0, keepdims=True),
                       -jnp.sum(factor * block[0:L], axis=0, keepdims=True)))
    own_u = shares[1][0] + level_sum(weights, u + 0.5 * (coriolis[...] * v + mix(u, mixing[...])))
    own_v = shares[1][1] + level_sum(weights, v + 0.5 * (mix(v, mixing[...]) - coriolis[...] * u))
    own_part[...] = part[:, OX : 2 * OX]
    surface_part[...] = jnp.zeros((8, MX), F32)
    for side, message, far in ((0, down, far_down), (2, up, far_up)):
        block = part[:, side * OX : (side + 1) * OX]
        message[count : count + L, 0:OX] = block[0:L]
        message[count : count + L, OX:] = block[L:]
        message[count + L :, :] = jnp.zeros((8, MX), F32)
        message[count + L : count + L + 1, 0:OX] = own_u
        message[count + L : count + L + 1, OX:] = own_v
        message[count + L + 1 : count + L + 2, 0:OX] = shares[side][0]
        message[count + L + 1 : count + L + 2, OX:] = shares[side][1]
        far[...] = jnp.zeros((8, MX), F32)
        far[0:1, 0:OX] = shares[side][0]
        far[0:1, OX:] = shares[side][1]
        at = side // 2
        surface_part[at : at + 1, 0:OX] = shares[side][0]
        surface_part[at : at + 1, OX:] = shares[side][1]
    surface_part[2:3, 0:OX] = own_u
    surface_part[2:3, OX:] = own_v


def second_kernel(
    count, own_up, own_down, from_below, from_above, below_two, above_two, zonal_below, zonal_above,
    own_part, surface_part, slope, quad, wide, stokes_sorted, cell_column, cell_side, cell_weight, wet, cells,
    cells_low, currents, coriolis, mixing,
    spectra, state, to_above, to_below, last_part, rounded, interp,
):
    half = L // 2
    below_extra = from_below[count:, :]
    above_extra = from_above[count:, :]
    own = surface_part[...]
    surf_below = below_extra[L : L + 1] + below_two[0:1, :] + own[0:1]
    surf_own = own[2:3] + below_extra[L + 1 : L + 2] + above_extra[L + 1 : L + 2]
    surf_above = above_extra[L : L + 1] + above_two[0:1, :] + own[1:2]
    flow = flow_of((surf_below, surf_own, surf_above), cell_column, cell_side, cell_weight)
    drift = own_part[...] + tall(below_extra[0:L]) + tall(above_extra[0:L])
    new_u, new_v = ocean_step(
        currents[0], currents[1], tall(zonal_below[count + 8 : count + 8 + half, :]),
        tall(zonal_above[count + 8 : count + 8 + half, :]), drift, coriolis[...], mixing[...]
    )
    state[0] = new_u
    state[1] = new_v
    wet_row = wet[...].astype(F32)
    stokes = update(count, own_up, own_down, from_below, from_above, flow, slope, quad, wide,
                    stokes_sorted, wet_row, spectra, rounded, interp)
    part = drift_parts(stokes, cells, cells_low)
    to_below[0:128, :] = part[:, 0:OX]
    last_part[...] = part[:, OX : 2 * OX]
    to_above[0:128, :] = part[:, 2 * OX :]
    to_below[128:, :] = new_u
    to_above[128:, :] = new_u


def restore_kernel(spectra, back, out, parts):
    high, low = split2(spectra[...])
    parts[:, 0:MX] = high
    parts[:, MX:] = low
    both = dot_nn(back[...], parts[...])
    out[...] = both[:, 0:MX] + both[:, MX:]


def last_ocean(state, from_below, from_above, own_part, coriolis, mixing, out):
    drift = own_part[...] + from_below[0:128, :] + from_above[0:128, :]
    new_u, new_v = ocean_step(
        state[0], state[1], from_below[128:, :], from_above[128:, :], drift, coriolis[...], mixing[...]
    )
    out[0] = new_u
    out[1] = new_v


def shape(*dims, dtype=F32):
    return jax.ShapeDtypeStruct(dims, dtype)


def call(body, outs, scratch=(), scalars=0, inputs=0, flops=0, data=0, name=None, out_specs=None):
    return pl.pallas_call(
        body,
        out_shape=outs,
        in_specs=[SMEM] * scalars + [VMEM] * (inputs - scalars),
        out_specs=out_specs or jax.tree.map(lambda _: VMEM, outs),
        scratch_shapes=scratch,
        cost_estimate=pl.CostEstimate(flops=flops, bytes_accessed=data, transcendentals=0),
        compiler_params=pltpu.CompilerParams(vmem_limit_bytes=LIMIT),
        name=name,
    )


def exchange(to_above, to_below, distance=1):
    total = lax.axis_size("mp") * lax.axis_size("dev")
    up = [(i, (i + distance) % total) for i in range(total)]
    return (
        lax.ppermute(to_above, AXES, up),
        lax.ppermute(to_below, AXES, [(b, a) for a, b in up]),
    )


def pack(count, stencil_sign, spectrum, currents, level, coriolis, ocean_index, ocean_weight):
    message = pltpu.VMEM((count + EXTRA, MX), F32)
    return call(
        functools.partial(pack_kernel, count),
        (message, message, shape(8, 128), shape(8, 128), shape(L, OX), shape(1, dtype=jnp.int32)),
        (pltpu.VMEM((K, 2 * K), BF16), pltpu.VMEM((2 * K, MX), BF16)),
        inputs=7, flops=2 * K * K * 3 * MX, data=1 << 20, name="pack",
        out_specs=(VMEM, VMEM, VMEM, VMEM, VMEM, SMEM),
    )(stencil_sign, spectrum, currents, level, coriolis, ocean_index, ocean_weight)


def slopes(count, up, down, wide):
    return call(
        functools.partial(slope_kernel, count), shape(K, MX), inputs=3, flops=1 << 30, data=4 << 20,
        name="slopes",
    )(up, down, wide)


def tables(row, pos, stencil_sign, courant, nonlinear, quad_index, quad_weight, stokes_table, point_index,
           point_weight, mixing, level):
    whole = jnp.int32
    return call(
        table_kernel,
        (
            shape(4, K, K, dtype=BF16), shape(K, K, dtype=BF16), shape(128, K, dtype=BF16),
            shape(7, K, 128), shape(8, OX, dtype=whole), shape(8, OX, dtype=whole), shape(8, OX),
            shape(L, OX), shape(L, OX),
        ),
        (pltpu.VMEM((K, K), BF16), pltpu.VMEM((32, K), F32), pltpu.VMEM((96, K), BF16),
         pltpu.VMEM((K, 32), F32)),
        scalars=1, inputs=12, flops=4 << 30, data=12 << 20, name="tables",
    )(row, pos, stencil_sign, courant, nonlinear, quad_index, quad_weight, stokes_table, point_index,
      point_weight, mixing, level)


def steps(
    count, up, down, below, above, slope, below_two, above_two, surface, made, row, wet, ocean_index,
    ocean_weight, currents, coriolis,
):
    quad, back, stokes_sorted, wide, cell_column, cell_side, cell_weight, mixing, level = made
    part = shape(128, OX)
    message = shape(count + EXTRA, MX)
    far = shape(8, MX)
    table = shape(MX, 3 * OX, dtype=BF16)
    work = (pltpu.VMEM((K, MX), BF16), pltpu.VMEM((4, K, MX), F32))
    next_up, next_down, own_part, surface_part, far_up, far_down, cells, cells_low = call(
        functools.partial(first_kernel, count),
        (message, message, part, far, far, far, table, table),
        (pltpu.VMEM((K, MX), F32),) + work,
        scalars=1, inputs=22, flops=3 << 30, data=12 << 20, name="first",
    )(row, up, down, below, above, below_two, above_two, surface, slope, quad, wide, stokes_sorted,
      cell_column, cell_side, cell_weight, wet, ocean_index, ocean_weight, currents, coriolis, mixing,
      level)
    next_below, next_above = exchange(next_up, next_down)
    far_below, far_above = exchange(far_up, far_down, 2)
    slope = slopes(count, next_up, next_down, wide)
    end = shape(128 + L, OX)
    spectra, state, to_above, to_below, last_part = call(
        functools.partial(second_kernel, count),
        (shape(K, MX), shape(2, L, OX), end, end, part),
        work, inputs=23, flops=3 << 30, data=12 << 20, name="second",
    )(next_up, next_down, next_below, next_above, far_below, far_above, below, above, own_part,
      surface_part, slope, quad, wide, stokes_sorted, cell_column, cell_side, cell_weight, wet, cells,
      cells_low, currents, coriolis, mixing)
    end_below, end_above = exchange(to_above, to_below)
    out = call(
        restore_kernel, shape(K, MX), (pltpu.VMEM((K, 2 * MX), BF16),), inputs=2, flops=2 * K * K * 2 * MX,
        data=4 << 20, name="restore",
    )(spectra, back)
    final = call(
        last_ocean, shape(2, L, OX), inputs=6, flops=1 << 20, data=1 << 18, name="ocean",
    )(state, end_below, end_above, last_part, coriolis, mixing)
    return out, final


def local(
    spectrum, water_mask, courant, stencil_sign, quad_index, quad_weight, nonlinear, stokes_table,
    point_index, point_weight, ocean_index, ocean_weight, currents, coriolis, mixing, surface_weights,
):
    row = (lax.axis_index("mp") * lax.axis_size("dev") + lax.axis_index("dev")).reshape(1)
    row = row.astype(jnp.int32)
    rotation = coriolis.reshape(1, OX)
    level = surface_weights.reshape(1, L)
    to_pack = (stencil_sign, spectrum, currents, level, rotation, ocean_index, ocean_weight)
    up, down, pos, surface, zonal, fits = pack(FAST, *to_pack)
    below, above = exchange(up, down)
    below = pltpu.with_memory_space_constraint(below, pltpu.VMEM)
    above = pltpu.with_memory_space_constraint(above, pltpu.VMEM)
    below_two, above_two = exchange(zonal, zonal, 2)
    made = tables(
        row, pos, stencil_sign, courant, nonlinear.reshape(1, K), quad_index.transpose(0, 2, 1),
        quad_weight.transpose(0, 2, 1), stokes_table, point_index, point_weight, mixing.reshape(1, L),
        level,
    )
    slope = slopes(FAST, up, down, made[3])
    rest = (
        below_two, above_two, surface, made, row, water_mask.reshape(1, MX), ocean_index, ocean_weight,
        currents, rotation,
    )

    def balanced(sent, to_pack, rest):
        return steps(FAST, *sent, *rest)

    def general(sent, to_pack, rest):
        up, down = pack(K, *to_pack)[:2]
        below, above = exchange(up, down)
        return steps(K, up, down, below, above, slopes(K, up, down, rest[3][3]), *rest)

    return lax.cond(fits[0] == 1, balanced, general, (up, down, below, above, slope), to_pack, rest)


def solution(mesh):
    whole = P(AXES)
    last = P(None, AXES)
    return jax.shard_map(
        local,
        mesh=mesh,
        in_specs=(
            last, whole, P(), P(), P(), P(), P(), P(), last, last, last, last,
            P(None, None, AXES), whole, P(), P(),
        ),
        out_specs=(last, P(None, None, AXES)),
        check_vma=False,
    )
```

```python
import functools

import jax
import jax.numpy as jnp
from jax import lax
from jax.experimental import pallas as pl
from jax.experimental.pallas import tpu as pltpu
from jax.sharding import PartitionSpec as P

K = 1024
L = 64
MX = 256
OX = 128
AXES = ("mp", "dev")
EXTRA = 72
LIMIT = 24 << 20
FAST = 560
F32 = jnp.float32
BF16 = jnp.bfloat16
VMEM = pl.BlockSpec(memory_space=pltpu.VMEM)
SMEM = pl.BlockSpec(memory_space=pltpu.SMEM)
HIGHEST = lax.Precision.HIGHEST


def dot_nt(a, b):
    return lax.dot_general(a, b, (((1,), (1,)), ((), ())), preferred_element_type=F32)


def dot_nn(a, b):
    return jnp.dot(a, b, preferred_element_type=F32)


def dot_exact(a, b):
    return jnp.dot(a, b, precision=HIGHEST, preferred_element_type=F32)


def split2(x):
    high = x.astype(BF16)
    return high, (x - high.astype(F32)).astype(BF16)


def split3(x):
    high, middle = split2(x)
    low = (x - high.astype(F32) - middle.astype(F32)).astype(BF16)
    return high, middle, low


def one_hot_rows(select_ref, pos_ref, copies=1):
    place = lax.broadcasted_iota(jnp.int16, (K, 128), 0)
    for block in range(8):
        line = pos_ref[block : block + 1, :].astype(jnp.int32)
        line = jnp.broadcast_to(line, (16, 128)).astype(jnp.int16)[0:1]
        ones = jnp.where(place == line, jnp.ones((), BF16), jnp.zeros((), BF16))
        for copy in range(copies):
            start = copy * K + block * 128
            select_ref[:, start : start + 128] = ones


def pack_kernel(
    count, sign, spectrum, currents, level, coriolis, ocean_index, ocean_weight,
    up, down, pos, surface, zonal, fits, select, parts,
):
    for block in range(8):
        pos[block : block + 1, :] = sign[1:2, block * 128 : (block + 1) * 128].astype(F32)
    ones = pos[...]
    upper = lax.broadcasted_iota(jnp.int32, (128, 128), 0) <= lax.broadcasted_iota(
        jnp.int32, (128, 128), 1
    )
    before = dot_nn(ones.astype(BF16), jnp.where(upper, 1.0, 0.0).astype(BF16))
    running = jnp.zeros((1, 1), F32)
    counts = []
    for block in range(8):
        counts.append(before[block : block + 1, :] + running)
        running = running + before[block : block + 1, 127:128]
    northward = jnp.sum(running)
    fits[0] = jnp.logical_and(northward <= count, K - northward <= count).astype(jnp.int32)
    lane = lax.broadcasted_iota(jnp.int32, (1, 128), 1).astype(F32)
    for block in range(8):
        index = lane + float(block * 128)
        first = counts[block] - 1.0
        second = running + index - counts[block]
        pos[block : block + 1, :] = jnp.where(ones[block : block + 1, :] > 0.5, first, second)
    one_hot_rows(select, pos, 2)
    high, low = split2(spectrum[...])
    parts[0:K, :] = low
    parts[K:, :] = high
    value = dot_nn(select[...], parts[...])
    up[0:count, :] = value[0:count, :]
    down[0:count, :] = value[K - count :, :]
    weights = jnp.broadcast_to(level[...], (8, L))
    flat_u = dot_exact(weights, currents[0])
    flat_v = dot_exact(weights, currents[1])
    surface[...] = flat_u
    surface[1:2, :] = flat_v[0:1, :]
    zonal[...] = currents[0]
    half = L // 2
    for message in (up, down):
        message[count : count + 1, 0:OX] = flat_u[0:1, :]
        message[count : count + 1, OX : 2 * OX] = flat_v[0:1, :]
        message[count + 1 : count + 5, 0:OX] = ocean_index[...].astype(F32)
        message[count + 1 : count + 5, OX : 2 * OX] = ocean_weight[...]
        message[count + 5 : count + 8, :] = jnp.zeros((3, MX), F32)
        message[count + 5 : count + 6, 0:OX] = coriolis[...]
        for flow in range(2):
            at = count + 8 + flow * half
            message[at : at + half, 0:OX] = currents[flow, 0:half, :]
            message[at : at + half, OX : 2 * OX] = currents[flow, half:, :]


def table_kernel(
    row, pos, sign, courant, nonlinear, quad_index, quad_weight, stokes_table, point_index,
    point_weight, mixing, level, quad, back, stokes_sorted, wide, cell_column, cell_side, cell_weight,
    mixing_wide, level_wide, select, rows, parts, columns,
):
    one_hot_rows(select, pos)
    sense = (2 * sign[...] - 1).astype(F32)
    speed = courant[...]
    rows[...] = jnp.zeros((32, K), F32)
    rows[0:2, :] = speed
    rows[2:4, :] = 0.5 * speed * sense
    rows[4:6, :] = sense
    rows[6:7, :] = nonlinear[...]
    for config in range(4):
        index = quad_index[config]
        weight = quad_weight[config]
        same = index[0:1] == index[1:2]
        first = jnp.where(same, weight[0:1] + weight[1:2], weight[0:1])
        second = jnp.where(same, 0.0, weight[1:2])
        rows[8 + 2 * config : 9 + 2 * config, :] = first.astype(BF16).astype(F32)
        rows[9 + 2 * config : 10 + 2 * config, :] = second.astype(BF16).astype(F32)
        rows[16 + 2 * config : 18 + 2 * config, :] = index.astype(F32)
    high, middle, low = split3(rows[...])
    parts[0:32, :] = high
    parts[32:64, :] = middle
    parts[64:96, :] = low
    component = lax.broadcasted_iota(jnp.int32, (16, K), 1)
    line = lax.broadcasted_iota(jnp.int32, (16, K), 0)
    digits = jnp.where(line == 0, component // 32, component % 32).astype(F32).astype(BF16)
    found = dot_nt(digits, select[...])
    order = found[0:1] * 32.0 + found[1:2]
    stokes_sorted[...] = dot_nt(stokes_table[...], select[...]).astype(BF16)

    got = dot_nt(select[...], parts[...])
    columns[...] = got[:, 0:32] + (got[:, 32:64] + got[:, 64:96])

    def block_rows(block, carry):
        at = pl.ds(pl.multiple_of(block * 64, 64), 64)
        column = columns[at, :]
        for item in range(7):
            wide[item, at, :] = jnp.broadcast_to(column[:, item : item + 1], (64, 128))
        original = (lax.broadcasted_iota(jnp.int32, (64, K), 0) + block * 64).astype(F32)
        back[at, :] = jnp.where(order == original, 1.0, 0.0).astype(BF16)
        for config in range(4):
            a = 8 + 2 * config
            b = 16 + 2 * config
            value = jnp.where(
                order == column[:, b : b + 1],
                column[:, a : a + 1],
                jnp.where(order == column[:, b + 1 : b + 2], column[:, a + 1 : a + 2], 0.0),
            )
            quad[config, at, :] = value.astype(BF16)
        return carry

    lax.fori_loop(0, K // 64, block_rows, 0)
    for config in range(4):
        for half in range(2):
            line = slice(2 * config + half, 2 * config + half + 1)
            cell = point_index[config : config + 1, half * 128 : (half + 1) * 128]
            cell_column[line, :] = cell % OX
            cell_side[line, :] = (cell // OX - row[0] + 257) % 256
            cell_weight[line, :] = point_weight[config : config + 1, half * 128 : (half + 1) * 128]
    diagonal = lax.broadcasted_iota(jnp.int32, (L, L), 0) == lax.broadcasted_iota(jnp.int32, (L, L), 1)
    for line, wide_column in ((mixing, mixing_wide), (level, level_wide)):
        column = jnp.sum(jnp.where(diagonal, line[...], 0.0), axis=1, keepdims=True)
        wide_column[...] = jnp.broadcast_to(column, (L, OX))


def cell_table(base, index, weight):
    point = (lax.broadcasted_iota(jnp.int32, (MX, OX), 0) + base).astype(F32)
    total = jnp.zeros((MX, OX), F32)
    for config in range(4):
        total = total + jnp.where(
            index[config : config + 1, :] == point, weight[config : config + 1, :], 0.0
        )
    return total


def blocks(start, stop, body):
    for at in range(start, stop, 64):
        body(at, min(64, stop - at))


def slope_kernel(count, own_up, own_down, wide, slope):
    def along(own, shift):
        def body(at, size):
            here = own[pl.ds(at - shift, size), :]
            sense = wide[4, pl.ds(at, size), :]
            sense = jnp.concatenate([sense, sense], axis=1)
            behind = jnp.where(sense > 0.0, pltpu.roll(here, 1, 1), pltpu.roll(here, MX - 1, 1))
            slope[pl.ds(at, size), :] = here - behind

        return body

    blocks(0, count, along(own_up, 0))
    blocks(count, K, along(own_down, K - count))


def update(count, own_up, own_down, from_below, from_above, flow, slope, quad, wide, stokes_sorted, wet,
           advected, rounded, finished):
    bend_x = jnp.tanh(flow[0])
    bend_y = jnp.tanh(flow[1])
    skip = K - count

    def advect(own, shift, behind):
        def body(at, size):
            here = own[pl.ds(at - shift, size), :]
            rows = pl.ds(at, size)
            base_x, base_y, bend_of_x, bend_of_y = [wide[item, rows, :] for item in range(4)]
            step_x = slope[rows, :]
            step_y = here - behind(at, size)
            for half in range(2):
                lanes = slice(half * 128, (half + 1) * 128)
                speed_x = base_x + bend_of_x * bend_x[:, lanes]
                speed_y = base_y + bend_of_y * bend_y[:, lanes]
                value = here[:, lanes] - speed_x * step_x[:, lanes] - speed_y * step_y[:, lanes]
                advected[rows, lanes] = value
                rounded[rows, lanes] = value.astype(BF16)

        return body

    def below(at, size):
        return from_below[pl.ds(at, size), :]

    def above(at, size):
        return from_above[pl.ds(at - skip, size), :]

    def either(at, size):
        sense = wide[5, pl.ds(at, size), :]
        sense = jnp.concatenate([sense, sense], axis=1)
        return jnp.where(sense > 0.0, below(at, size), above(at, size))

    if skip:
        blocks(0, skip, advect(own_up, 0, below))
    blocks(skip, count, advect(own_up, 0, either))
    if skip:
        blocks(count, K, advect(own_down, skip, above))

    def source(at, size):
        rows = pl.ds(at, size)
        members = [dot_nn(quad[config, rows, :], rounded[...]) for config in range(4)]
        value = advected[rows, :]
        pairs = members[0] * members[1] + members[2] * members[3]
        total = (members[0] + members[1]) + (members[2] + members[3])
        gain = wide[6, rows, :]
        gain = jnp.concatenate([gain, gain], axis=1)
        result = wet * (value + gain * (value * (value * total - pairs)))
        advected[rows, :] = result
        finished[rows, :] = result.astype(BF16)

    for at in range(0, K, 512):
        source(at, 512)
    return dot_nn(stokes_sorted[...], finished[...])


def flow_of(sides, column, side, weight):
    index = column[...]
    where = side[...]
    flow = []
    for component in range(2):
        total = jnp.zeros((8, OX), F32)
        for item in range(3):
            line = jnp.broadcast_to(sides[item][:, component * OX : (component + 1) * OX], (8, OX))
            got = jnp.take_along_axis(line, index, axis=1, mode="promise_in_bounds")
            total = jnp.where(where == item, got, total)
        total = total * weight[...]
        halves = [
            (total[h : h + 1] + total[h + 2 : h + 3]) + (total[h + 4 : h + 5] + total[h + 6 : h + 7])
            for h in range(2)
        ]
        flow.append(jnp.concatenate(halves, axis=1))
    return flow


def drift_parts(stokes, cells, cells_low):
    high = stokes.astype(BF16)
    low = (stokes - high.astype(F32)).astype(BF16)
    both = dot_nn(jnp.concatenate([high, low], axis=0), cells[...])
    return both[0:128] + (both[128:] + dot_nn(high, cells_low[...]))


def tall(block):
    return jnp.concatenate([block[:, 0:OX], block[:, OX:]], axis=0)


def turn(v, u_below, u_above):
    return 0.5 * (pltpu.roll(v, OX - 1, 1) - pltpu.roll(v, 1, 1)) - 0.5 * (u_above - u_below)


def mix(profile, mixing):
    line = lax.broadcasted_iota(jnp.int32, (L, OX), 0)
    before = jnp.where(line == 0, profile, pltpu.roll(profile, 1, 0))
    after = jnp.where(line == L - 1, profile, pltpu.roll(profile, L - 1, 0))
    return mixing * (before - 2.0 * profile + after)


def ocean_step(u, v, u_below, u_above, drift, rotation, mixing):
    vorticity = turn(v, u_below, u_above)
    drift_x = drift[0:L, :]
    drift_y = drift[L:, :]
    new_u = u + 0.5 * (rotation * (v + drift_y) + vorticity * drift_y + mix(u, mixing))
    new_v = v + 0.5 * (-rotation * (u + drift_x) - vorticity * drift_x + mix(v, mixing))
    return new_u, new_v


def level_sum(weights, x):
    return jnp.sum(weights * x, axis=0, keepdims=True)


def first_kernel(
    count, row, own_up, own_down, from_below, from_above, below_two, above_two, surface, slope, quad, wide,
    stokes_sorted, cell_column, cell_side, cell_weight, wet, ocean_index, ocean_weight, currents,
    coriolis, mixing, level,
    up, down, own_part, surface_part, far_up, far_down, cells, cells_low, advected, rounded, finished,
):
    base = row[0] * MX
    half = L // 2
    below_extra = from_below[count:, :]
    above_extra = from_above[count:, :]
    for side, index, weight in (
        (0, below_extra[1:5, 0:OX], below_extra[1:5, OX:]),
        (1, ocean_index[...].astype(F32), ocean_weight[...]),
        (2, above_extra[1:5, 0:OX], above_extra[1:5, OX:]),
    ):
        table = cell_table(base, index, weight)
        high = table.astype(BF16)
        cells[:, side * OX : (side + 1) * OX] = high
        cells_low[:, side * OX : (side + 1) * OX] = (table - high.astype(F32)).astype(BF16)
    own = jnp.concatenate([surface[0:1, :], surface[1:2, :]], axis=1)
    sides = (below_extra[0:1, :], own, above_extra[0:1, :])
    flow = flow_of(sides, cell_column, cell_side, cell_weight)
    wet_row = wet[...].astype(F32)
    stokes = update(count, own_up, own_down, from_below, from_above, flow, slope, quad, wide,
                    stokes_sorted, wet_row, advected, rounded, finished)
    up[0:count, :] = advected[0:count, :]
    down[0:count, :] = advected[K - count :, :]
    part = drift_parts(stokes, cells, cells_low)
    u, v = currents[0], currents[1]
    u_below, v_below = tall(below_extra[8 : 8 + half]), tall(below_extra[8 + half : 8 + 2 * half])
    u_above, v_above = tall(above_extra[8 : 8 + half]), tall(above_extra[8 + half : 8 + 2 * half])
    weights = level[...]
    rotations = (below_extra[5:6, 0:OX], coriolis[...], above_extra[5:6, 0:OX])
    turns = (turn(v_below, below_two[...], u), turn(v, u_below, u_above), turn(v_above, u, above_two[...]))
    shares = []
    for side in range(3):
        factor = 0.5 * weights * (rotations[side] + turns[side])
        block = part[:, side * OX : (side + 1) * OX]
        shares.append((jnp.sum(factor * block[L:], axis=0, keepdims=True),
                       -jnp.sum(factor * block[0:L], axis=0, keepdims=True)))
    own_u = shares[1][0] + level_sum(weights, u + 0.5 * (coriolis[...] * v + mix(u, mixing[...])))
    own_v = shares[1][1] + level_sum(weights, v + 0.5 * (mix(v, mixing[...]) - coriolis[...] * u))
    own_part[...] = part[:, OX : 2 * OX]
    surface_part[...] = jnp.zeros((8, MX), F32)
    for side, message, far in ((0, down, far_down), (2, up, far_up)):
        block = part[:, side * OX : (side + 1) * OX]
        message[count : count + L, 0:OX] = block[0:L]
        message[count : count + L, OX:] = block[L:]
        message[count + L :, :] = jnp.zeros((8, MX), F32)
        message[count + L : count + L + 1, 0:OX] = own_u
        message[count + L : count + L + 1, OX:] = own_v
        message[count + L + 1 : count + L + 2, 0:OX] = shares[side][0]
        message[count + L + 1 : count + L + 2, OX:] = shares[side][1]
        far[...] = jnp.zeros((8, MX), F32)
        far[0:1, 0:OX] = shares[side][0]
        far[0:1, OX:] = shares[side][1]
        at = side // 2
        surface_part[at : at + 1, 0:OX] = shares[side][0]
        surface_part[at : at + 1, OX:] = shares[side][1]
    surface_part[2:3, 0:OX] = own_u
    surface_part[2:3, OX:] = own_v


def second_kernel(
    count, own_up, own_down, from_below, from_above, below_two, above_two, zonal_below, zonal_above,
    own_part, surface_part, slope, quad, wide, stokes_sorted, cell_column, cell_side, cell_weight, wet, cells,
    cells_low, currents, coriolis, mixing,
    spectra, state, to_above, to_below, last_part, rounded, finished,
):
    half = L // 2
    below_extra = from_below[count:, :]
    above_extra = from_above[count:, :]
    own = surface_part[...]
    surf_below = below_extra[L : L + 1] + below_two[0:1, :] + own[0:1]
    surf_own = own[2:3] + below_extra[L + 1 : L + 2] + above_extra[L + 1 : L + 2]
    surf_above = above_extra[L : L + 1] + above_two[0:1, :] + own[1:2]
    flow = flow_of((surf_below, surf_own, surf_above), cell_column, cell_side, cell_weight)
    drift = own_part[...] + tall(below_extra[0:L]) + tall(above_extra[0:L])
    new_u, new_v = ocean_step(
        currents[0], currents[1], tall(zonal_below[count + 8 : count + 8 + half, :]),
        tall(zonal_above[count + 8 : count + 8 + half, :]), drift, coriolis[...], mixing[...]
    )
    state[0] = new_u
    state[1] = new_v
    wet_row = wet[...].astype(F32)
    stokes = update(count, own_up, own_down, from_below, from_above, flow, slope, quad, wide,
                    stokes_sorted, wet_row, spectra, rounded, finished)
    part = drift_parts(stokes, cells, cells_low)
    to_below[0:128, :] = part[:, 0:OX]
    last_part[...] = part[:, OX : 2 * OX]
    to_above[0:128, :] = part[:, 2 * OX :]
    to_below[128:, :] = new_u
    to_above[128:, :] = new_u


def restore_kernel(spectra, back, out, parts):
    high, low = split2(spectra[...])
    parts[:, 0:MX] = high
    parts[:, MX:] = low
    both = dot_nn(back[...], parts[...])
    out[...] = both[:, 0:MX] + both[:, MX:]


def last_ocean(state, from_below, from_above, own_part, coriolis, mixing, out):
    drift = own_part[...] + from_below[0:128, :] + from_above[0:128, :]
    new_u, new_v = ocean_step(
        state[0], state[1], from_below[128:, :], from_above[128:, :], drift, coriolis[...], mixing[...]
    )
    out[0] = new_u
    out[1] = new_v


def shape(*dims, dtype=F32):
    return jax.ShapeDtypeStruct(dims, dtype)


def call(body, outs, scratch=(), scalars=0, inputs=0, flops=0, data=0, name=None, out_specs=None):
    return pl.pallas_call(
        body,
        out_shape=outs,
        in_specs=[SMEM] * scalars + [VMEM] * (inputs - scalars),
        out_specs=out_specs or jax.tree.map(lambda _: VMEM, outs),
        scratch_shapes=scratch,
        cost_estimate=pl.CostEstimate(flops=flops, bytes_accessed=data, transcendentals=0),
        compiler_params=pltpu.CompilerParams(vmem_limit_bytes=LIMIT),
        name=name,
    )


def exchange(to_above, to_below, distance=1):
    total = lax.axis_size("mp") * lax.axis_size("dev")
    up = [(i, (i + distance) % total) for i in range(total)]
    return (
        lax.ppermute(to_above, AXES, up),
        lax.ppermute(to_below, AXES, [(b, a) for a, b in up]),
    )


def pack(count, stencil_sign, spectrum, currents, level, coriolis, ocean_index, ocean_weight):
    message = pltpu.VMEM((count + EXTRA, MX), F32)
    return call(
        functools.partial(pack_kernel, count),
        (message, message, shape(8, 128), shape(8, 128), shape(L, OX), shape(1, dtype=jnp.int32)),
        (pltpu.VMEM((K, 2 * K), BF16), pltpu.VMEM((2 * K, MX), BF16)),
        inputs=7, flops=2 * K * K * 3 * MX, data=1 << 20, name="pack",
        out_specs=(VMEM, VMEM, VMEM, VMEM, VMEM, SMEM),
    )(stencil_sign, spectrum, currents, level, coriolis, ocean_index, ocean_weight)


def slopes(count, up, down, wide):
    return call(
        functools.partial(slope_kernel, count), shape(K, MX), inputs=3, flops=1 << 30, data=4 << 20,
        name="slopes",
    )(up, down, wide)


def tables(row, pos, stencil_sign, courant, nonlinear, quad_index, quad_weight, stokes_table, point_index,
           point_weight, mixing, level):
    whole = jnp.int32
    return call(
        table_kernel,
        (
            shape(4, K, K, dtype=BF16), shape(K, K, dtype=BF16), shape(128, K, dtype=BF16),
            shape(7, K, 128), shape(8, OX, dtype=whole), shape(8, OX, dtype=whole), shape(8, OX),
            shape(L, OX), shape(L, OX),
        ),
        (pltpu.VMEM((K, K), BF16), pltpu.VMEM((32, K), F32), pltpu.VMEM((96, K), BF16),
         pltpu.VMEM((K, 32), F32)),
        scalars=1, inputs=12, flops=4 << 30, data=12 << 20, name="tables",
    )(row, pos, stencil_sign, courant, nonlinear, quad_index, quad_weight, stokes_table, point_index,
      point_weight, mixing, level)


def steps(
    count, up, down, below, above, slope, below_two, above_two, surface, made, row, wet, ocean_index,
    ocean_weight, currents, coriolis,
):
    quad, back, stokes_sorted, wide, cell_column, cell_side, cell_weight, mixing, level = made
    part = shape(128, OX)
    message = shape(count + EXTRA, MX)
    far = shape(8, MX)
    table = shape(MX, 3 * OX, dtype=BF16)
    work = (pltpu.VMEM((K, MX), BF16), pltpu.VMEM((K, MX), BF16))
    next_up, next_down, own_part, surface_part, far_up, far_down, cells, cells_low = call(
        functools.partial(first_kernel, count),
        (message, message, part, far, far, far, table, table),
        (pltpu.VMEM((K, MX), F32),) + work,
        scalars=1, inputs=22, flops=3 << 30, data=12 << 20, name="first",
    )(row, up, down, below, above, below_two, above_two, surface, slope, quad, wide, stokes_sorted,
      cell_column, cell_side, cell_weight, wet, ocean_index, ocean_weight, currents, coriolis, mixing,
      level)
    next_below, next_above = exchange(next_up, next_down)
    far_below, far_above = exchange(far_up, far_down, 2)
    slope = slopes(count, next_up, next_down, wide)
    end = shape(128 + L, OX)
    spectra, state, to_above, to_below, last_part = call(
        functools.partial(second_kernel, count),
        (shape(K, MX), shape(2, L, OX), end, end, part),
        work, inputs=23, flops=3 << 30, data=12 << 20, name="second",
    )(next_up, next_down, next_below, next_above, far_below, far_above, below, above, own_part,
      surface_part, slope, quad, wide, stokes_sorted, cell_column, cell_side, cell_weight, wet, cells,
      cells_low, currents, coriolis, mixing)
    end_below, end_above = exchange(to_above, to_below)
    out = call(
        restore_kernel, shape(K, MX), (pltpu.VMEM((K, 2 * MX), BF16),), inputs=2, flops=2 * K * K * 2 * MX,
        data=4 << 20, name="restore",
    )(spectra, back)
    final = call(
        last_ocean, shape(2, L, OX), inputs=6, flops=1 << 20, data=1 << 18, name="ocean",
    )(state, end_below, end_above, last_part, coriolis, mixing)
    return out, final


def local(
    spectrum, water_mask, courant, stencil_sign, quad_index, quad_weight, nonlinear, stokes_table,
    point_index, point_weight, ocean_index, ocean_weight, currents, coriolis, mixing, surface_weights,
):
    row = (lax.axis_index("mp") * lax.axis_size("dev") + lax.axis_index("dev")).reshape(1)
    row = row.astype(jnp.int32)
    rotation = coriolis.reshape(1, OX)
    level = surface_weights.reshape(1, L)
    to_pack = (stencil_sign, spectrum, currents, level, rotation, ocean_index, ocean_weight)
    up, down, pos, surface, zonal, fits = pack(FAST, *to_pack)
    below, above = exchange(up, down)
    below = pltpu.with_memory_space_constraint(below, pltpu.VMEM)
    above = pltpu.with_memory_space_constraint(above, pltpu.VMEM)
    below_two, above_two = exchange(zonal, zonal, 2)
    made = tables(
        row, pos, stencil_sign, courant, nonlinear.reshape(1, K), quad_index.transpose(0, 2, 1),
        quad_weight.transpose(0, 2, 1), stokes_table, point_index, point_weight, mixing.reshape(1, L),
        level,
    )
    slope = slopes(FAST, up, down, made[3])
    rest = (
        below_two, above_two, surface, made, row, water_mask.reshape(1, MX), ocean_index, ocean_weight,
        currents, rotation,
    )

    def balanced(sent, to_pack, rest):
        return steps(FAST, *sent, *rest)

    def general(sent, to_pack, rest):
        up, down = pack(K, *to_pack)[:2]
        below, above = exchange(up, down)
        return steps(K, up, down, below, above, slopes(K, up, down, rest[3][3]), *rest)

    return lax.cond(fits[0] == 1, balanced, general, (up, down, below, above, slope), to_pack, rest)


def solution(mesh):
    whole = P(AXES)
    last = P(None, AXES)
    return jax.shard_map(
        local,
        mesh=mesh,
        in_specs=(
            last, whole, P(), P(), P(), P(), P(), P(), last, last, last, last,
            P(None, None, AXES), whole, P(), P(),
        ),
        out_specs=(last, P(None, None, AXES)),
        check_vma=False,
    )
```

```python
import functools

import jax
import jax.numpy as jnp
from jax import lax
from jax.experimental import pallas as pl
from jax.experimental.pallas import tpu as pltpu
from jax.sharding import PartitionSpec as P

K = 1024
L = 64
MX = 256
OX = 128
AXES = ("mp", "dev")
EXTRA = 72
LIMIT = 24 << 20
FAST = 560
F32 = jnp.float32
BF16 = jnp.bfloat16
VMEM = pl.BlockSpec(memory_space=pltpu.VMEM)
SMEM = pl.BlockSpec(memory_space=pltpu.SMEM)
HIGHEST = lax.Precision.HIGHEST


def dot_nt(a, b):
    return lax.dot_general(a, b, (((1,), (1,)), ((), ())), preferred_element_type=F32)


def dot_nn(a, b):
    return jnp.dot(a, b, preferred_element_type=F32)


def dot_exact(a, b):
    return jnp.dot(a, b, precision=HIGHEST, preferred_element_type=F32)


def split2(x):
    high = x.astype(BF16)
    return high, (x - high.astype(F32)).astype(BF16)


def split3(x):
    high, middle = split2(x)
    low = (x - high.astype(F32) - middle.astype(F32)).astype(BF16)
    return high, middle, low


def one_hot_rows(select_ref, pos_ref, copies=1):
    place = lax.broadcasted_iota(jnp.int16, (K, 128), 0)
    for block in range(8):
        line = pos_ref[block : block + 1, :].astype(jnp.int32)
        line = jnp.broadcast_to(line, (16, 128)).astype(jnp.int16)[0:1]
        ones = jnp.where(place == line, jnp.ones((), BF16), jnp.zeros((), BF16))
        for copy in range(copies):
            start = copy * K + block * 128
            select_ref[:, start : start + 128] = ones


def pack_kernel(
    count, sign, spectrum, currents, level, coriolis, ocean_index, ocean_weight,
    up, down, pos, surface, zonal, fits, select, parts,
):
    for block in range(8):
        pos[block : block + 1, :] = sign[1:2, block * 128 : (block + 1) * 128].astype(F32)
    ones = pos[...]
    upper = lax.broadcasted_iota(jnp.int32, (128, 256), 0) <= lax.broadcasted_iota(
        jnp.int32, (128, 256), 1
    )
    sums = dot_nn(ones.astype(BF16), jnp.where(upper, 1.0, 0.0).astype(BF16))
    in_line, total = sums[:, 0:128], sums[:, 128:]
    line = lax.broadcasted_iota(jnp.int32, (8, 128), 0)
    running = total
    northward = total
    for shift in (1, 2, 4):
        running = running + jnp.where(line >= shift, pltpu.roll(running, shift, 0), 0.0)
        northward = northward + pltpu.roll(northward, shift, 0)
    before = in_line + (running - total)
    index = (line * 128 + lax.broadcasted_iota(jnp.int32, (8, 128), 1)).astype(F32)
    pos[...] = jnp.where(ones > 0.5, before - 1.0, northward + index - before)
    one_hot_rows(select, pos)
    high, low = split2(spectrum[...])
    parts[:, 0:MX] = low
    parts[:, MX:] = high
    both = dot_nn(select[...], parts[...])
    value = both[:, 0:MX] + both[:, MX:]
    up[0:count, :] = value[0:count, :]
    down[0:count, :] = value[K - count :, :]
    some = jnp.sum(northward[0:1, 0:1])
    fits[0] = jnp.logical_and(some <= count, K - some <= count).astype(jnp.int32)
    weights = jnp.broadcast_to(level[...], (8, L))
    flat_u = dot_exact(weights, currents[0])
    flat_v = dot_exact(weights, currents[1])
    surface[...] = flat_u
    surface[1:2, :] = flat_v[0:1, :]
    zonal[...] = currents[0]
    half = L // 2
    for message in (up, down):
        message[count : count + 1, 0:OX] = flat_u[0:1, :]
        message[count : count + 1, OX : 2 * OX] = flat_v[0:1, :]
        message[count + 1 : count + 5, 0:OX] = ocean_index[...].astype(F32)
        message[count + 1 : count + 5, OX : 2 * OX] = ocean_weight[...]
        message[count + 5 : count + 8, :] = jnp.zeros((3, MX), F32)
        message[count + 5 : count + 6, 0:OX] = coriolis[...]
        for flow in range(2):
            at = count + 8 + flow * half
            message[at : at + half, 0:OX] = currents[flow, 0:half, :]
            message[at : at + half, OX : 2 * OX] = currents[flow, half:, :]


def table_kernel(
    row, pos, sign, courant, nonlinear, quad_index, quad_weight, stokes_table, point_index,
    point_weight, mixing, level, quad, back, stokes_sorted, wide, cell_column, cell_side, cell_weight,
    mixing_wide, level_wide, select, rows, parts, columns,
):
    one_hot_rows(select, pos)
    sense = (2 * sign[...] - 1).astype(F32)
    speed = courant[...]
    rows[...] = jnp.zeros((32, K), F32)
    rows[0:2, :] = speed
    rows[2:4, :] = 0.5 * speed * sense
    rows[4:6, :] = sense
    rows[6:7, :] = nonlinear[...]
    for config in range(4):
        index = quad_index[config]
        weight = quad_weight[config]
        same = index[0:1] == index[1:2]
        first = jnp.where(same, weight[0:1] + weight[1:2], weight[0:1])
        second = jnp.where(same, 0.0, weight[1:2])
        rows[8 + 2 * config : 9 + 2 * config, :] = first.astype(BF16).astype(F32)
        rows[9 + 2 * config : 10 + 2 * config, :] = second.astype(BF16).astype(F32)
        rows[16 + 2 * config : 18 + 2 * config, :] = index.astype(F32)
    high, middle, low = split3(rows[...])
    parts[0:32, :] = high
    parts[32:64, :] = middle
    parts[64:96, :] = low
    component = lax.broadcasted_iota(jnp.int32, (16, K), 1)
    line = lax.broadcasted_iota(jnp.int32, (16, K), 0)
    digits = jnp.where(line == 0, component // 32, component % 32).astype(F32).astype(BF16)
    found = dot_nt(digits, select[...])
    order = found[0:1] * 32.0 + found[1:2]
    stokes_sorted[...] = dot_nt(stokes_table[...], select[...]).astype(BF16)

    got = dot_nt(select[...], parts[...])
    columns[...] = got[:, 0:32] + (got[:, 32:64] + got[:, 64:96])

    def block_rows(block, carry):
        at = pl.ds(pl.multiple_of(block * 64, 64), 64)
        column = columns[at, :]
        for item in range(7):
            wide[item, at, :] = jnp.broadcast_to(column[:, item : item + 1], (64, 128))
        original = (lax.broadcasted_iota(jnp.int32, (64, K), 0) + block * 64).astype(F32)
        back[at, :] = jnp.where(order == original, 1.0, 0.0).astype(BF16)
        for config in range(4):
            a = 8 + 2 * config
            b = 16 + 2 * config
            value = jnp.where(
                order == column[:, b : b + 1],
                column[:, a : a + 1],
                jnp.where(order == column[:, b + 1 : b + 2], column[:, a + 1 : a + 2], 0.0),
            )
            quad[config, at, :] = value.astype(BF16)
        return carry

    lax.fori_loop(0, K // 64, block_rows, 0)
    for config in range(4):
        for half in range(2):
            line = slice(2 * config + half, 2 * config + half + 1)
            cell = point_index[config : config + 1, half * 128 : (half + 1) * 128]
            cell_column[line, :] = cell % OX
            cell_side[line, :] = (cell // OX - row[0] + 257) % 256
            cell_weight[line, :] = point_weight[config : config + 1, half * 128 : (half + 1) * 128]
    diagonal = lax.broadcasted_iota(jnp.int32, (L, L), 0) == lax.broadcasted_iota(jnp.int32, (L, L), 1)
    for line, wide_column in ((mixing, mixing_wide), (level, level_wide)):
        column = jnp.sum(jnp.where(diagonal, line[...], 0.0), axis=1, keepdims=True)
        wide_column[...] = jnp.broadcast_to(column, (L, OX))


def cell_table(base, index, weight):
    point = (lax.broadcasted_iota(jnp.int32, (MX, OX), 0) + base).astype(F32)
    total = jnp.zeros((MX, OX), F32)
    for config in range(4):
        total = total + jnp.where(
            index[config : config + 1, :] == point, weight[config : config + 1, :], 0.0
        )
    return total


def blocks(start, stop, body):
    for at in range(start, stop, 64):
        body(at, min(64, stop - at))


def slope_kernel(count, own_up, own_down, wide, slope):
    def along(own, shift):
        def body(at, size):
            here = own[pl.ds(at - shift, size), :]
            sense = wide[4, pl.ds(at, size), :]
            sense = jnp.concatenate([sense, sense], axis=1)
            behind = jnp.where(sense > 0.0, pltpu.roll(here, 1, 1), pltpu.roll(here, MX - 1, 1))
            slope[pl.ds(at, size), :] = here - behind

        return body

    blocks(0, count, along(own_up, 0))
    blocks(count, K, along(own_down, K - count))


def update(count, own_up, own_down, from_below, from_above, flow, slope, quad, wide, stokes_sorted, wet,
           write, advected, rounded, finished):
    bend_x = jnp.tanh(flow[0])
    bend_y = jnp.tanh(flow[1])
    skip = K - count

    def advect(own, shift, behind):
        def body(at, size):
            here = own[pl.ds(at - shift, size), :]
            rows = pl.ds(at, size)
            base_x, base_y, bend_of_x, bend_of_y = [wide[item, rows, :] for item in range(4)]
            step_x = slope[rows, :]
            step_y = here - behind(at, size)
            for half in range(2):
                lanes = slice(half * 128, (half + 1) * 128)
                speed_x = base_x + bend_of_x * bend_x[:, lanes]
                speed_y = base_y + bend_of_y * bend_y[:, lanes]
                value = here[:, lanes] - speed_x * step_x[:, lanes] - speed_y * step_y[:, lanes]
                advected[rows, lanes] = value
                rounded[rows, lanes] = value.astype(BF16)

        return body

    def below(at, size):
        return from_below[pl.ds(at, size), :]

    def above(at, size):
        return from_above[pl.ds(at - skip, size), :]

    def either(at, size):
        sense = wide[5, pl.ds(at, size), :]
        sense = jnp.concatenate([sense, sense], axis=1)
        return jnp.where(sense > 0.0, below(at, size), above(at, size))

    if skip:
        blocks(0, skip, advect(own_up, 0, below))
    blocks(skip, count, advect(own_up, 0, either))
    if skip:
        blocks(count, K, advect(own_down, skip, above))

    def source(at, size):
        rows = pl.ds(at, size)
        members = [dot_nn(quad[config, rows, :], rounded[...]) for config in range(4)]
        value = advected[rows, :]
        pairs = members[0] * members[1] + members[2] * members[3]
        total = (members[0] + members[1]) + (members[2] + members[3])
        gain = wide[6, rows, :]
        gain = jnp.concatenate([gain, gain], axis=1)
        result = wet * (value + gain * (value * (value * total - pairs)))
        write(at, size, result)
        finished[rows, :] = result.astype(BF16)

    for at in range(0, K, 512):
        source(at, 512)
    return dot_nn(stokes_sorted[...], finished[...])


def flow_of(sides, column, side, weight):
    index = column[...]
    where = side[...]
    flow = []
    for component in range(2):
        total = jnp.zeros((8, OX), F32)
        for item in range(3):
            line = jnp.broadcast_to(sides[item][:, component * OX : (component + 1) * OX], (8, OX))
            got = jnp.take_along_axis(line, index, axis=1, mode="promise_in_bounds")
            total = jnp.where(where == item, got, total)
        total = total * weight[...]
        halves = [
            (total[h : h + 1] + total[h + 2 : h + 3]) + (total[h + 4 : h + 5] + total[h + 6 : h + 7])
            for h in range(2)
        ]
        flow.append(jnp.concatenate(halves, axis=1))
    return flow


def drift_parts(stokes, cells, cells_low):
    high = stokes.astype(BF16)
    low = (stokes - high.astype(F32)).astype(BF16)
    both = dot_nn(jnp.concatenate([high, low], axis=0), cells[...])
    return both[0:128] + (both[128:] + dot_nn(high, cells_low[...]))


def tall(block):
    return jnp.concatenate([block[:, 0:OX], block[:, OX:]], axis=0)


def turn(v, u_below, u_above):
    return 0.5 * (pltpu.roll(v, OX - 1, 1) - pltpu.roll(v, 1, 1)) - 0.5 * (u_above - u_below)


def mix(profile, mixing):
    line = lax.broadcasted_iota(jnp.int32, (L, OX), 0)
    before = jnp.where(line == 0, profile, pltpu.roll(profile, 1, 0))
    after = jnp.where(line == L - 1, profile, pltpu.roll(profile, L - 1, 0))
    return mixing * (before - 2.0 * profile + after)


def ocean_step(u, v, u_below, u_above, drift, rotation, mixing):
    vorticity = turn(v, u_below, u_above)
    drift_x = drift[0:L, :]
    drift_y = drift[L:, :]
    new_u = u + 0.5 * (rotation * (v + drift_y) + vorticity * drift_y + mix(u, mixing))
    new_v = v + 0.5 * (-rotation * (u + drift_x) - vorticity * drift_x + mix(v, mixing))
    return new_u, new_v


def level_sum(weights, x):
    return jnp.sum(weights * x, axis=0, keepdims=True)


def first_kernel(
    count, row, own_up, own_down, from_below, from_above, below_two, above_two, surface, slope, quad, wide,
    stokes_sorted, cell_column, cell_side, cell_weight, wet, ocean_index, ocean_weight, currents,
    coriolis, mixing, level,
    up, down, own_part, surface_part, far_up, far_down, cells, cells_low, advected, rounded, finished,
):
    base = row[0] * MX
    half = L // 2
    below_extra = from_below[count:, :]
    above_extra = from_above[count:, :]
    for side, index, weight in (
        (0, below_extra[1:5, 0:OX], below_extra[1:5, OX:]),
        (1, ocean_index[...].astype(F32), ocean_weight[...]),
        (2, above_extra[1:5, 0:OX], above_extra[1:5, OX:]),
    ):
        table = cell_table(base, index, weight)
        high = table.astype(BF16)
        cells[:, side * OX : (side + 1) * OX] = high
        cells_low[:, side * OX : (side + 1) * OX] = (table - high.astype(F32)).astype(BF16)
    own = jnp.concatenate([surface[0:1, :], surface[1:2, :]], axis=1)
    sides = (below_extra[0:1, :], own, above_extra[0:1, :])
    flow = flow_of(sides, cell_column, cell_side, cell_weight)
    wet_row = wet[...].astype(F32)

    def write(at, size, result):
        top = min(at + size, count)
        if top > at:
            up[at:top, :] = result[0 : top - at]
        start = max(at, K - count)
        if start < at + size:
            down[start - K + count : at + size - K + count, :] = result[start - at :]

    stokes = update(count, own_up, own_down, from_below, from_above, flow, slope, quad, wide,
                    stokes_sorted, wet_row, write, advected, rounded, finished)
    part = drift_parts(stokes, cells, cells_low)
    u, v = currents[0], currents[1]
    u_below, v_below = tall(below_extra[8 : 8 + half]), tall(below_extra[8 + half : 8 + 2 * half])
    u_above, v_above = tall(above_extra[8 : 8 + half]), tall(above_extra[8 + half : 8 + 2 * half])
    weights = level[...]
    rotations = (below_extra[5:6, 0:OX], coriolis[...], above_extra[5:6, 0:OX])
    turns = (turn(v_below, below_two[...], u), turn(v, u_below, u_above), turn(v_above, u, above_two[...]))
    shares = []
    for side in range(3):
        factor = 0.5 * weights * (rotations[side] + turns[side])
        block = part[:, side * OX : (side + 1) * OX]
        shares.append((jnp.sum(factor * block[L:], axis=0, keepdims=True),
                       -jnp.sum(factor * block[0:L], axis=0, keepdims=True)))
    own_u = shares[1][0] + level_sum(weights, u + 0.5 * (coriolis[...] * v + mix(u, mixing[...])))
    own_v = shares[1][1] + level_sum(weights, v + 0.5 * (mix(v, mixing[...]) - coriolis[...] * u))
    own_part[...] = part[:, OX : 2 * OX]
    surface_part[...] = jnp.zeros((8, MX), F32)
    for side, message, far in ((0, down, far_down), (2, up, far_up)):
        block = part[:, side * OX : (side + 1) * OX]
        message[count : count + L, 0:OX] = block[0:L]
        message[count : count + L, OX:] = block[L:]
        message[count + L :, :] = jnp.zeros((8, MX), F32)
        message[count + L : count + L + 1, 0:OX] = own_u
        message[count + L : count + L + 1, OX:] = own_v
        message[count + L + 1 : count + L + 2, 0:OX] = shares[side][0]
        message[count + L + 1 : count + L + 2, OX:] = shares[side][1]
        far[...] = jnp.zeros((8, MX), F32)
        far[0:1, 0:OX] = shares[side][0]
        far[0:1, OX:] = shares[side][1]
        at = side // 2
        surface_part[at : at + 1, 0:OX] = shares[side][0]
        surface_part[at : at + 1, OX:] = shares[side][1]
    surface_part[2:3, 0:OX] = own_u
    surface_part[2:3, OX:] = own_v


def second_kernel(
    count, own_up, own_down, from_below, from_above, below_two, above_two, zonal_below, zonal_above,
    own_part, surface_part, slope, quad, wide, stokes_sorted, cell_column, cell_side, cell_weight, wet, cells,
    cells_low, currents, coriolis, mixing,
    spectra, state, to_above, to_below, last_part, rounded, finished,
):
    half = L // 2
    below_extra = from_below[count:, :]
    above_extra = from_above[count:, :]
    own = surface_part[...]
    surf_below = below_extra[L : L + 1] + below_two[0:1, :] + own[0:1]
    surf_own = own[2:3] + below_extra[L + 1 : L + 2] + above_extra[L + 1 : L + 2]
    surf_above = above_extra[L : L + 1] + above_two[0:1, :] + own[1:2]
    flow = flow_of((surf_below, surf_own, surf_above), cell_column, cell_side, cell_weight)
    drift = own_part[...] + tall(below_extra[0:L]) + tall(above_extra[0:L])
    new_u, new_v = ocean_step(
        currents[0], currents[1], tall(zonal_below[count + 8 : count + 8 + half, :]),
        tall(zonal_above[count + 8 : count + 8 + half, :]), drift, coriolis[...], mixing[...]
    )
    state[0] = new_u
    state[1] = new_v
    wet_row = wet[...].astype(F32)

    def write(at, size, result):
        spectra[at : at + size, :] = result

    stokes = update(count, own_up, own_down, from_below, from_above, flow, slope, quad, wide,
                    stokes_sorted, wet_row, write, spectra, rounded, finished)
    part = drift_parts(stokes, cells, cells_low)
    to_below[0:128, :] = part[:, 0:OX]
    last_part[...] = part[:, OX : 2 * OX]
    to_above[0:128, :] = part[:, 2 * OX :]
    to_below[128:, :] = new_u
    to_above[128:, :] = new_u


def restore_kernel(spectra, back, out, parts):
    high, low = split2(spectra[...])
    parts[:, 0:MX] = high
    parts[:, MX:] = low
    both = dot_nn(back[...], parts[...])
    out[...] = both[:, 0:MX] + both[:, MX:]


def last_ocean(state, from_below, from_above, own_part, coriolis, mixing, out):
    drift = own_part[...] + from_below[0:128, :] + from_above[0:128, :]
    new_u, new_v = ocean_step(
        state[0], state[1], from_below[128:, :], from_above[128:, :], drift, coriolis[...], mixing[...]
    )
    out[0] = new_u
    out[1] = new_v


def shape(*dims, dtype=F32):
    return jax.ShapeDtypeStruct(dims, dtype)


def call(body, outs, scratch=(), scalars=0, inputs=0, flops=0, data=0, name=None, out_specs=None):
    return pl.pallas_call(
        body,
        out_shape=outs,
        in_specs=[SMEM] * scalars + [VMEM] * (inputs - scalars),
        out_specs=out_specs or jax.tree.map(lambda _: VMEM, outs),
        scratch_shapes=scratch,
        cost_estimate=pl.CostEstimate(flops=flops, bytes_accessed=data, transcendentals=0),
        compiler_params=pltpu.CompilerParams(vmem_limit_bytes=LIMIT),
        name=name,
    )


def exchange(to_above, to_below, distance=1):
    total = lax.axis_size("mp") * lax.axis_size("dev")
    up = [(i, (i + distance) % total) for i in range(total)]
    return (
        lax.ppermute(to_above, AXES, up),
        lax.ppermute(to_below, AXES, [(b, a) for a, b in up]),
    )


def pack(count, stencil_sign, spectrum, currents, level, coriolis, ocean_index, ocean_weight):
    message = pltpu.VMEM((count + EXTRA, MX), F32)
    return call(
        functools.partial(pack_kernel, count),
        (message, message, shape(8, 128), shape(8, 128), shape(L, OX), shape(1, dtype=jnp.int32)),
        (pltpu.VMEM((K, K), BF16), pltpu.VMEM((K, 2 * MX), BF16)),
        inputs=7, flops=2 * K * K * 3 * MX, data=1 << 20, name="pack",
        out_specs=(VMEM, VMEM, VMEM, VMEM, VMEM, SMEM),
    )(stencil_sign, spectrum, currents, level, coriolis, ocean_index, ocean_weight)


def slopes(count, up, down, wide):
    return call(
        functools.partial(slope_kernel, count), shape(K, MX), inputs=3, flops=1 << 30, data=4 << 20,
        name="slopes",
    )(up, down, wide)


def tables(row, pos, stencil_sign, courant, nonlinear, quad_index, quad_weight, stokes_table, point_index,
           point_weight, mixing, level):
    whole = jnp.int32
    return call(
        table_kernel,
        (
            shape(4, K, K, dtype=BF16), shape(K, K, dtype=BF16), shape(128, K, dtype=BF16),
            shape(7, K, 128), shape(8, OX, dtype=whole), shape(8, OX, dtype=whole), shape(8, OX),
            shape(L, OX), shape(L, OX),
        ),
        (pltpu.VMEM((K, K), BF16), pltpu.VMEM((32, K), F32), pltpu.VMEM((96, K), BF16),
         pltpu.VMEM((K, 32), F32)),
        scalars=1, inputs=12, flops=4 << 30, data=12 << 20, name="tables",
    )(row, pos, stencil_sign, courant, nonlinear, quad_index, quad_weight, stokes_table, point_index,
      point_weight, mixing, level)


def steps(
    count, up, down, below, above, slope, below_two, above_two, surface, made, row, wet, ocean_index,
    ocean_weight, currents, coriolis,
):
    quad, back, stokes_sorted, wide, cell_column, cell_side, cell_weight, mixing, level = made
    part = shape(128, OX)
    message = shape(count + EXTRA, MX)
    far = shape(8, MX)
    table = shape(MX, 3 * OX, dtype=BF16)
    work = (pltpu.VMEM((K, MX), BF16), pltpu.VMEM((K, MX), BF16))
    next_up, next_down, own_part, surface_part, far_up, far_down, cells, cells_low = call(
        functools.partial(first_kernel, count),
        (message, message, part, far, far, far, table, table),
        (pltpu.VMEM((K, MX), F32),) + work,
        scalars=1, inputs=22, flops=3 << 30, data=12 << 20, name="first",
    )(row, up, down, below, above, below_two, above_two, surface, slope, quad, wide, stokes_sorted,
      cell_column, cell_side, cell_weight, wet, ocean_index, ocean_weight, currents, coriolis, mixing,
      level)
    next_below, next_above = exchange(next_up, next_down)
    far_below, far_above = exchange(far_up, far_down, 2)
    slope = slopes(count, next_up, next_down, wide)
    end = shape(128 + L, OX)
    spectra, state, to_above, to_below, last_part = call(
        functools.partial(second_kernel, count),
        (shape(K, MX), shape(2, L, OX), end, end, part),
        work, inputs=23, flops=3 << 30, data=12 << 20, name="second",
    )(next_up, next_down, next_below, next_above, far_below, far_above, below, above, own_part,
      surface_part, slope, quad, wide, stokes_sorted, cell_column, cell_side, cell_weight, wet, cells,
      cells_low, currents, coriolis, mixing)
    end_below, end_above = exchange(to_above, to_below)
    out = call(
        restore_kernel, shape(K, MX), (pltpu.VMEM((K, 2 * MX), BF16),), inputs=2, flops=2 * K * K * 2 * MX,
        data=4 << 20, name="restore",
    )(spectra, back)
    final = call(
        last_ocean, shape(2, L, OX), inputs=6, flops=1 << 20, data=1 << 18, name="ocean",
    )(state, end_below, end_above, last_part, coriolis, mixing)
    return out, final


def local(
    spectrum, water_mask, courant, stencil_sign, quad_index, quad_weight, nonlinear, stokes_table,
    point_index, point_weight, ocean_index, ocean_weight, currents, coriolis, mixing, surface_weights,
):
    row = (lax.axis_index("mp") * lax.axis_size("dev") + lax.axis_index("dev")).reshape(1)
    row = row.astype(jnp.int32)
    rotation = coriolis.reshape(1, OX)
    level = surface_weights.reshape(1, L)
    to_pack = (stencil_sign, spectrum, currents, level, rotation, ocean_index, ocean_weight)
    up, down, pos, surface, zonal, fits = pack(FAST, *to_pack)
    below, above = exchange(up, down)
    below = pltpu.with_memory_space_constraint(below, pltpu.VMEM)
    above = pltpu.with_memory_space_constraint(above, pltpu.VMEM)
    below_two, above_two = exchange(zonal, zonal, 2)
    made = tables(
        row, pos, stencil_sign, courant, nonlinear.reshape(1, K), quad_index.transpose(0, 2, 1),
        quad_weight.transpose(0, 2, 1), stokes_table, point_index, point_weight, mixing.reshape(1, L),
        level,
    )
    slope = slopes(FAST, up, down, made[3])
    rest = (
        below_two, above_two, surface, made, row, water_mask.reshape(1, MX), ocean_index, ocean_weight,
        currents, rotation,
    )

    def balanced(sent, to_pack, rest):
        return steps(FAST, *sent, *rest)

    def general(sent, to_pack, rest):
        up, down = pack(K, *to_pack)[:2]
        below, above = exchange(up, down)
        return steps(K, up, down, below, above, slopes(K, up, down, rest[3][3]), *rest)

    return lax.cond(fits[0] == 1, balanced, general, (up, down, below, above, slope), to_pack, rest)


def solution(mesh):
    whole = P(AXES)
    last = P(None, AXES)
    return jax.shard_map(
        local,
        mesh=mesh,
        in_specs=(
            last, whole, P(), P(), P(), P(), P(), P(), last, last, last, last,
            P(None, None, AXES), whole, P(), P(),
        ),
        out_specs=(last, P(None, None, AXES)),
        check_vma=False,
    )
```

```python
import functools

import jax
import jax.numpy as jnp
from jax import lax
from jax.experimental import pallas as pl
from jax.experimental.pallas import tpu as pltpu
from jax.sharding import PartitionSpec as P

K = 1024
L = 64
MX = 256
OX = 128
AXES = ("mp", "dev")
EXTRA = 72
LIMIT = 24 << 20
FAST = 560
F32 = jnp.float32
BF16 = jnp.bfloat16
VMEM = pl.BlockSpec(memory_space=pltpu.VMEM)
SMEM = pl.BlockSpec(memory_space=pltpu.SMEM)
HIGHEST = lax.Precision.HIGHEST


def dot_nt(a, b):
    return lax.dot_general(a, b, (((1,), (1,)), ((), ())), preferred_element_type=F32)


def dot_nn(a, b):
    return jnp.dot(a, b, preferred_element_type=F32)


def dot_exact(a, b):
    return jnp.dot(a, b, precision=HIGHEST, preferred_element_type=F32)


def split2(x):
    high = x.astype(BF16)
    return high, (x - high.astype(F32)).astype(BF16)


def split3(x):
    high, middle = split2(x)
    low = (x - high.astype(F32) - middle.astype(F32)).astype(BF16)
    return high, middle, low


def one_hot_rows(select_ref, pos_ref, copies=1):
    place = lax.broadcasted_iota(jnp.int16, (K, 128), 0)
    for block in range(8):
        line = pos_ref[block : block + 1, :].astype(jnp.int32)
        line = jnp.broadcast_to(line, (16, 128)).astype(jnp.int16)[0:1]
        ones = jnp.where(place == line, jnp.ones((), BF16), jnp.zeros((), BF16))
        for copy in range(copies):
            start = copy * K + block * 128
            select_ref[:, start : start + 128] = ones


def pack_kernel(
    count, sign, spectrum, currents, level, coriolis, ocean_index, ocean_weight,
    up, down, pos, surface, zonal, fits, select, parts,
):
    for block in range(8):
        pos[block : block + 1, :] = sign[1:2, block * 128 : (block + 1) * 128].astype(F32)
    ones = pos[...]
    upper = lax.broadcasted_iota(jnp.int32, (128, 256), 0) <= lax.broadcasted_iota(
        jnp.int32, (128, 256), 1
    )
    sums = dot_nn(ones.astype(BF16), jnp.where(upper, 1.0, 0.0).astype(BF16))
    in_line, total = sums[:, 0:128], sums[:, 128:]
    line = lax.broadcasted_iota(jnp.int32, (8, 128), 0)
    running = total
    northward = total
    for shift in (1, 2, 4):
        running = running + jnp.where(line >= shift, pltpu.roll(running, shift, 0), 0.0)
        northward = northward + pltpu.roll(northward, shift, 0)
    before = in_line + (running - total)
    index = (line * 128 + lax.broadcasted_iota(jnp.int32, (8, 128), 1)).astype(F32)
    pos[...] = jnp.where(ones > 0.5, before - 1.0, northward + index - before)
    one_hot_rows(select, pos)
    high, low = split2(spectrum[...])
    parts[:, 0:MX] = low
    parts[:, MX:] = high
    both = dot_nn(select[...], parts[...])
    value = both[:, 0:MX] + both[:, MX:]
    up[0:count, :] = value[0:count, :]
    down[0:count, :] = value[K - count :, :]
    some = jnp.sum(northward[0:1, 0:1])
    fits[0] = jnp.logical_and(some <= count, K - some <= count).astype(jnp.int32)
    weights = jnp.broadcast_to(level[...], (8, L))
    flat_u = dot_exact(weights, currents[0])
    flat_v = dot_exact(weights, currents[1])
    surface[...] = flat_u
    surface[1:2, :] = flat_v[0:1, :]
    zonal[...] = currents[0]
    half = L // 2
    for message in (up, down):
        message[count : count + 1, 0:OX] = flat_u[0:1, :]
        message[count : count + 1, OX : 2 * OX] = flat_v[0:1, :]
        message[count + 1 : count + 5, 0:OX] = ocean_index[...].astype(F32)
        message[count + 1 : count + 5, OX : 2 * OX] = ocean_weight[...]
        message[count + 5 : count + 8, :] = jnp.zeros((3, MX), F32)
        message[count + 5 : count + 6, 0:OX] = coriolis[...]
        for flow in range(2):
            at = count + 8 + flow * half
            message[at : at + half, 0:OX] = currents[flow, 0:half, :]
            message[at : at + half, OX : 2 * OX] = currents[flow, half:, :]


def table_kernel(
    row, pos, sign, courant, nonlinear, quad_index, quad_weight, stokes_table, point_index,
    point_weight, mixing, level, quad, back, stokes_sorted, wide, cell_column, cell_side, cell_weight,
    mixing_wide, level_wide, origin, select, rows, parts, columns,
):
    one_hot_rows(select, pos)
    sense = (2 * sign[...] - 1).astype(F32)
    speed = courant[...]
    rows[...] = jnp.zeros((32, K), F32)
    rows[0:2, :] = speed
    rows[2:4, :] = 0.5 * speed * sense
    rows[4:6, :] = sense
    rows[6:7, :] = nonlinear[...]
    for config in range(4):
        index = quad_index[config]
        weight = quad_weight[config]
        same = index[0:1] == index[1:2]
        first = jnp.where(same, weight[0:1] + weight[1:2], weight[0:1])
        second = jnp.where(same, 0.0, weight[1:2])
        rows[8 + 2 * config : 9 + 2 * config, :] = first.astype(BF16).astype(F32)
        rows[9 + 2 * config : 10 + 2 * config, :] = second.astype(BF16).astype(F32)
        rows[16 + 2 * config : 18 + 2 * config, :] = index.astype(F32)
    high, middle, low = split3(rows[...])
    parts[0:32, :] = high
    parts[32:64, :] = middle
    parts[64:96, :] = low
    component = lax.broadcasted_iota(jnp.int32, (16, K), 1)
    line = lax.broadcasted_iota(jnp.int32, (16, K), 0)
    digits = jnp.where(line == 0, component // 32, component % 32).astype(F32).astype(BF16)
    found = dot_nt(digits, select[...])
    order = found[0:1] * 32.0 + found[1:2]
    stokes_sorted[...] = dot_nt(stokes_table[...], select[...]).astype(BF16)

    got = dot_nt(select[...], parts[...])
    columns[...] = got[:, 0:32] + (got[:, 32:64] + got[:, 64:96])

    def block_rows(block, carry):
        at = pl.ds(pl.multiple_of(block * 64, 64), 64)
        column = columns[at, :]
        for item in range(7):
            wide[item, at, :] = jnp.broadcast_to(column[:, item : item + 1], (64, 128))
        original = (lax.broadcasted_iota(jnp.int32, (64, K), 0) + block * 64).astype(F32)
        back[at, :] = jnp.where(order == original, 1.0, 0.0).astype(BF16)
        for config in range(4):
            a = 8 + 2 * config
            b = 16 + 2 * config
            value = jnp.where(
                order == column[:, b : b + 1],
                column[:, a : a + 1],
                jnp.where(order == column[:, b + 1 : b + 2], column[:, a + 1 : a + 2], 0.0),
            )
            quad[config, at, :] = value.astype(BF16)
        return carry

    lax.fori_loop(0, K // 64, block_rows, 0)
    for config in range(4):
        for half in range(2):
            line = slice(2 * config + half, 2 * config + half + 1)
            cell = point_index[config : config + 1, half * 128 : (half + 1) * 128]
            cell_column[line, :] = cell % OX
            cell_side[line, :] = (cell // OX - row[0] + 257) % 256
            cell_weight[line, :] = point_weight[config : config + 1, half * 128 : (half + 1) * 128]
    origin[...] = jnp.zeros((1, OX), F32) + (row[0] * MX).astype(F32)
    diagonal = lax.broadcasted_iota(jnp.int32, (L, L), 0) == lax.broadcasted_iota(jnp.int32, (L, L), 1)
    for line, wide_column in ((mixing, mixing_wide), (level, level_wide)):
        column = jnp.sum(jnp.where(diagonal, line[...], 0.0), axis=1, keepdims=True)
        wide_column[...] = jnp.broadcast_to(column, (L, OX))


def cell_table(base, index, weight):
    point = lax.broadcasted_iota(jnp.int32, (MX, OX), 0).astype(F32) + base
    total = jnp.zeros((MX, OX), F32)
    for config in range(4):
        total = total + jnp.where(
            index[config : config + 1, :] == point, weight[config : config + 1, :], 0.0
        )
    return total


def blocks(start, stop, body):
    for at in range(start, stop, 64):
        body(at, min(64, stop - at))


def slope_kernel(count, own_up, own_down, wide, slope):
    def along(own, shift):
        def body(at, size):
            here = own[pl.ds(at - shift, size), :]
            sense = wide[4, pl.ds(at, size), :]
            sense = jnp.concatenate([sense, sense], axis=1)
            behind = jnp.where(sense > 0.0, pltpu.roll(here, 1, 1), pltpu.roll(here, MX - 1, 1))
            slope[pl.ds(at, size), :] = here - behind

        return body

    blocks(0, count, along(own_up, 0))
    blocks(count, K, along(own_down, K - count))


def update(count, own_up, own_down, from_below, from_above, flow, slope, quad, wide, stokes_sorted, wet,
           write, advected, rounded, finished):
    bend_x = jnp.tanh(flow[0])
    bend_y = jnp.tanh(flow[1])
    skip = K - count

    def advect(own, shift, behind):
        def body(at, size):
            here = own[pl.ds(at - shift, size), :]
            rows = pl.ds(at, size)
            base_x, base_y, bend_of_x, bend_of_y = [wide[item, rows, :] for item in range(4)]
            step_x = slope[rows, :]
            step_y = here - behind(at, size)
            for half in range(2):
                lanes = slice(half * 128, (half + 1) * 128)
                speed_x = base_x + bend_of_x * bend_x[:, lanes]
                speed_y = base_y + bend_of_y * bend_y[:, lanes]
                value = here[:, lanes] - speed_x * step_x[:, lanes] - speed_y * step_y[:, lanes]
                advected[rows, lanes] = value
                rounded[rows, lanes] = value.astype(BF16)

        return body

    def below(at, size):
        return from_below[pl.ds(at, size), :]

    def above(at, size):
        return from_above[pl.ds(at - skip, size), :]

    def either(at, size):
        sense = wide[5, pl.ds(at, size), :]
        sense = jnp.concatenate([sense, sense], axis=1)
        return jnp.where(sense > 0.0, below(at, size), above(at, size))

    if skip:
        blocks(0, skip, advect(own_up, 0, below))
    blocks(skip, count, advect(own_up, 0, either))
    if skip:
        blocks(count, K, advect(own_down, skip, above))

    def source(at, size):
        rows = pl.ds(at, size)
        members = [dot_nn(quad[config, rows, :], rounded[...]) for config in range(4)]
        value = advected[rows, :]
        pairs = members[0] * members[1] + members[2] * members[3]
        total = (members[0] + members[1]) + (members[2] + members[3])
        gain = wide[6, rows, :]
        gain = jnp.concatenate([gain, gain], axis=1)
        result = wet * (value + gain * (value * (value * total - pairs)))
        write(at, size, result)
        finished[rows, :] = result.astype(BF16)

    for at in range(0, K, 512):
        source(at, 512)
    return dot_nn(stokes_sorted[...], finished[...])


def flow_of(sides, column, side, weight):
    index = column[...]
    where = side[...]
    flow = []
    for component in range(2):
        total = jnp.zeros((8, OX), F32)
        for item in range(3):
            line = jnp.broadcast_to(sides[item][:, component * OX : (component + 1) * OX], (8, OX))
            got = jnp.take_along_axis(line, index, axis=1, mode="promise_in_bounds")
            total = jnp.where(where == item, got, total)
        total = total * weight[...]
        halves = [
            (total[h : h + 1] + total[h + 2 : h + 3]) + (total[h + 4 : h + 5] + total[h + 6 : h + 7])
            for h in range(2)
        ]
        flow.append(jnp.concatenate(halves, axis=1))
    return flow


def drift_parts(stokes, cells, cells_low):
    high = stokes.astype(BF16)
    low = (stokes - high.astype(F32)).astype(BF16)
    both = dot_nn(jnp.concatenate([high, low], axis=0), cells[...])
    return both[0:128] + (both[128:] + dot_nn(high, cells_low[...]))


def tall(block):
    return jnp.concatenate([block[:, 0:OX], block[:, OX:]], axis=0)


def turn(v, u_below, u_above):
    return 0.5 * (pltpu.roll(v, OX - 1, 1) - pltpu.roll(v, 1, 1)) - 0.5 * (u_above - u_below)


def mix(profile, mixing):
    line = lax.broadcasted_iota(jnp.int32, (L, OX), 0)
    before = jnp.where(line == 0, profile, pltpu.roll(profile, 1, 0))
    after = jnp.where(line == L - 1, profile, pltpu.roll(profile, L - 1, 0))
    return mixing * (before - 2.0 * profile + after)


def ocean_step(u, v, u_below, u_above, drift, rotation, mixing):
    vorticity = turn(v, u_below, u_above)
    drift_x = drift[0:L, :]
    drift_y = drift[L:, :]
    new_u = u + 0.5 * (rotation * (v + drift_y) + vorticity * drift_y + mix(u, mixing))
    new_v = v + 0.5 * (-rotation * (u + drift_x) - vorticity * drift_x + mix(v, mixing))
    return new_u, new_v


def level_sum(weights, x):
    return jnp.sum(weights * x, axis=0, keepdims=True)


def first_kernel(
    count, origin, own_up, own_down, from_below, from_above, below_two, above_two, surface, slope, quad, wide,
    stokes_sorted, cell_column, cell_side, cell_weight, wet, ocean_index, ocean_weight, currents,
    coriolis, mixing, level,
    up, down, own_part, surface_part, far_up, far_down, cells, cells_low, advected, rounded, finished,
):
    base = origin[...]
    half = L // 2
    below_extra = from_below[count:, :]
    above_extra = from_above[count:, :]
    for side, index, weight in (
        (0, below_extra[1:5, 0:OX], below_extra[1:5, OX:]),
        (1, ocean_index[...].astype(F32), ocean_weight[...]),
        (2, above_extra[1:5, 0:OX], above_extra[1:5, OX:]),
    ):
        table = cell_table(base, index, weight)
        high = table.astype(BF16)
        cells[:, side * OX : (side + 1) * OX] = high
        cells_low[:, side * OX : (side + 1) * OX] = (table - high.astype(F32)).astype(BF16)
    own = jnp.concatenate([surface[0:1, :], surface[1:2, :]], axis=1)
    sides = (below_extra[0:1, :], own, above_extra[0:1, :])
    flow = flow_of(sides, cell_column, cell_side, cell_weight)
    wet_row = wet[...].astype(F32)

    def write(at, size, result):
        top = min(at + size, count)
        if top > at:
            up[at:top, :] = result[0 : top - at]
        start = max(at, K - count)
        if start < at + size:
            down[start - K + count : at + size - K + count, :] = result[start - at :]

    stokes = update(count, own_up, own_down, from_below, from_above, flow, slope, quad, wide,
                    stokes_sorted, wet_row, write, advected, rounded, finished)
    part = drift_parts(stokes, cells, cells_low)
    u, v = currents[0], currents[1]
    u_below, v_below = tall(below_extra[8 : 8 + half]), tall(below_extra[8 + half : 8 + 2 * half])
    u_above, v_above = tall(above_extra[8 : 8 + half]), tall(above_extra[8 + half : 8 + 2 * half])
    weights = level[...]
    rotations = (below_extra[5:6, 0:OX], coriolis[...], above_extra[5:6, 0:OX])
    turns = (turn(v_below, below_two[...], u), turn(v, u_below, u_above), turn(v_above, u, above_two[...]))
    shares = []
    for side in range(3):
        factor = 0.5 * weights * (rotations[side] + turns[side])
        block = part[:, side * OX : (side + 1) * OX]
        shares.append((jnp.sum(factor * block[L:], axis=0, keepdims=True),
                       -jnp.sum(factor * block[0:L], axis=0, keepdims=True)))
    own_u = shares[1][0] + level_sum(weights, u + 0.5 * (coriolis[...] * v + mix(u, mixing[...])))
    own_v = shares[1][1] + level_sum(weights, v + 0.5 * (mix(v, mixing[...]) - coriolis[...] * u))
    own_part[...] = part[:, OX : 2 * OX]
    surface_part[...] = jnp.zeros((8, MX), F32)
    for side, message, far in ((0, down, far_down), (2, up, far_up)):
        block = part[:, side * OX : (side + 1) * OX]
        message[count : count + L, 0:OX] = block[0:L]
        message[count : count + L, OX:] = block[L:]
        message[count + L :, :] = jnp.zeros((8, MX), F32)
        message[count + L : count + L + 1, 0:OX] = own_u
        message[count + L : count + L + 1, OX:] = own_v
        message[count + L + 1 : count + L + 2, 0:OX] = shares[side][0]
        message[count + L + 1 : count + L + 2, OX:] = shares[side][1]
        far[...] = jnp.zeros((8, MX), F32)
        far[0:1, 0:OX] = shares[side][0]
        far[0:1, OX:] = shares[side][1]
        at = side // 2
        surface_part[at : at + 1, 0:OX] = shares[side][0]
        surface_part[at : at + 1, OX:] = shares[side][1]
    surface_part[2:3, 0:OX] = own_u
    surface_part[2:3, OX:] = own_v


def second_kernel(
    count, own_up, own_down, from_below, from_above, below_two, above_two, zonal_below, zonal_above,
    own_part, surface_part, slope, quad, wide, stokes_sorted, cell_column, cell_side, cell_weight, wet, cells,
    cells_low, currents, coriolis, mixing,
    spectra, state, to_above, to_below, last_part, rounded, finished,
):
    half = L // 2
    below_extra = from_below[count:, :]
    above_extra = from_above[count:, :]
    own = surface_part[...]
    surf_below = below_extra[L : L + 1] + below_two[0:1, :] + own[0:1]
    surf_own = own[2:3] + below_extra[L + 1 : L + 2] + above_extra[L + 1 : L + 2]
    surf_above = above_extra[L : L + 1] + above_two[0:1, :] + own[1:2]
    flow = flow_of((surf_below, surf_own, surf_above), cell_column, cell_side, cell_weight)
    drift = own_part[...] + tall(below_extra[0:L]) + tall(above_extra[0:L])
    new_u, new_v = ocean_step(
        currents[0], currents[1], tall(zonal_below[count + 8 : count + 8 + half, :]),
        tall(zonal_above[count + 8 : count + 8 + half, :]), drift, coriolis[...], mixing[...]
    )
    state[0] = new_u
    state[1] = new_v
    wet_row = wet[...].astype(F32)

    def write(at, size, result):
        spectra[at : at + size, :] = result

    stokes = update(count, own_up, own_down, from_below, from_above, flow, slope, quad, wide,
                    stokes_sorted, wet_row, write, spectra, rounded, finished)
    part = drift_parts(stokes, cells, cells_low)
    to_below[0:128, :] = part[:, 0:OX]
    last_part[...] = part[:, OX : 2 * OX]
    to_above[0:128, :] = part[:, 2 * OX :]
    to_below[128:, :] = new_u
    to_above[128:, :] = new_u


def restore_kernel(spectra, back, out, parts):
    high, low = split2(spectra[...])
    parts[:, 0:MX] = high
    parts[:, MX:] = low
    both = dot_nn(back[...], parts[...])
    out[...] = both[:, 0:MX] + both[:, MX:]


def last_ocean(state, from_below, from_above, own_part, coriolis, mixing, out):
    drift = own_part[...] + from_below[0:128, :] + from_above[0:128, :]
    new_u, new_v = ocean_step(
        state[0], state[1], from_below[128:, :], from_above[128:, :], drift, coriolis[...], mixing[...]
    )
    out[0] = new_u
    out[1] = new_v


def shape(*dims, dtype=F32):
    return jax.ShapeDtypeStruct(dims, dtype)


def call(body, outs, scratch=(), scalars=0, inputs=0, flops=0, data=0, name=None, out_specs=None):
    return pl.pallas_call(
        body,
        out_shape=outs,
        in_specs=[SMEM] * scalars + [VMEM] * (inputs - scalars),
        out_specs=out_specs or jax.tree.map(lambda _: VMEM, outs),
        scratch_shapes=scratch,
        cost_estimate=pl.CostEstimate(flops=flops, bytes_accessed=data, transcendentals=0),
        compiler_params=pltpu.CompilerParams(vmem_limit_bytes=LIMIT),
        name=name,
    )


def exchange(to_above, to_below, distance=1):
    total = lax.axis_size("mp") * lax.axis_size("dev")
    up = [(i, (i + distance) % total) for i in range(total)]
    return (
        lax.ppermute(to_above, AXES, up),
        lax.ppermute(to_below, AXES, [(b, a) for a, b in up]),
    )


def pack(count, stencil_sign, spectrum, currents, level, coriolis, ocean_index, ocean_weight):
    message = pltpu.VMEM((count + EXTRA, MX), F32)
    return call(
        functools.partial(pack_kernel, count),
        (message, message, shape(8, 128), shape(8, 128), shape(L, OX), shape(1, dtype=jnp.int32)),
        (pltpu.VMEM((K, K), BF16), pltpu.VMEM((K, 2 * MX), BF16)),
        inputs=7, flops=2 * K * K * 3 * MX, data=1 << 20, name="pack",
        out_specs=(VMEM, VMEM, VMEM, VMEM, VMEM, SMEM),
    )(stencil_sign, spectrum, currents, level, coriolis, ocean_index, ocean_weight)


def slopes(count, up, down, wide):
    return call(
        functools.partial(slope_kernel, count), shape(K, MX), inputs=3, flops=1 << 30, data=4 << 20,
        name="slopes",
    )(up, down, wide)


def tables(row, pos, stencil_sign, courant, nonlinear, quad_index, quad_weight, stokes_table, point_index,
           point_weight, mixing, level):
    whole = jnp.int32
    return call(
        table_kernel,
        (
            shape(4, K, K, dtype=BF16), shape(K, K, dtype=BF16), shape(128, K, dtype=BF16),
            shape(7, K, 128), shape(8, OX, dtype=whole), shape(8, OX, dtype=whole), shape(8, OX),
            shape(L, OX), shape(L, OX), shape(1, OX),
        ),
        (pltpu.VMEM((K, K), BF16), pltpu.VMEM((32, K), F32), pltpu.VMEM((96, K), BF16),
         pltpu.VMEM((K, 32), F32)),
        scalars=1, inputs=12, flops=4 << 30, data=12 << 20, name="tables",
    )(row, pos, stencil_sign, courant, nonlinear, quad_index, quad_weight, stokes_table, point_index,
      point_weight, mixing, level)


def steps(
    count, up, down, below, above, slope, below_two, above_two, surface, made, wet, ocean_index,
    ocean_weight, currents, coriolis,
):
    quad, back, stokes_sorted, wide, cell_column, cell_side, cell_weight, mixing, level, origin = made
    part = shape(128, OX)
    message = shape(count + EXTRA, MX)
    far = shape(8, MX)
    table = shape(MX, 3 * OX, dtype=BF16)
    work = (pltpu.VMEM((K, MX), BF16), pltpu.VMEM((K, MX), BF16))
    next_up, next_down, own_part, surface_part, far_up, far_down, cells, cells_low = call(
        functools.partial(first_kernel, count),
        (message, message, part, far, far, far, table, table),
        (pltpu.VMEM((K, MX), F32),) + work,
        inputs=22, flops=3 << 30, data=12 << 20, name="first",
    )(origin, up, down, below, above, below_two, above_two, surface, slope, quad, wide, stokes_sorted,
      cell_column, cell_side, cell_weight, wet, ocean_index, ocean_weight, currents, coriolis, mixing,
      level)
    next_below, next_above = exchange(next_up, next_down)
    far_below, far_above = exchange(far_up, far_down, 2)
    slope = slopes(count, next_up, next_down, wide)
    end = shape(128 + L, OX)
    spectra, state, to_above, to_below, last_part = call(
        functools.partial(second_kernel, count),
        (shape(K, MX), shape(2, L, OX), end, end, part),
        work, inputs=23, flops=3 << 30, data=12 << 20, name="second",
    )(next_up, next_down, next_below, next_above, far_below, far_above, below, above, own_part,
      surface_part, slope, quad, wide, stokes_sorted, cell_column, cell_side, cell_weight, wet, cells,
      cells_low, currents, coriolis, mixing)
    end_below, end_above = exchange(to_above, to_below)
    out = call(
        restore_kernel, shape(K, MX), (pltpu.VMEM((K, 2 * MX), BF16),), inputs=2, flops=2 * K * K * 2 * MX,
        data=4 << 20, name="restore",
    )(spectra, back)
    final = call(
        last_ocean, shape(2, L, OX), inputs=6, flops=1 << 20, data=1 << 18, name="ocean",
    )(state, end_below, end_above, last_part, coriolis, mixing)
    return out, final


def local(
    spectrum, water_mask, courant, stencil_sign, quad_index, quad_weight, nonlinear, stokes_table,
    point_index, point_weight, ocean_index, ocean_weight, currents, coriolis, mixing, surface_weights,
):
    row = (lax.axis_index("mp") * lax.axis_size("dev") + lax.axis_index("dev")).reshape(1)
    row = row.astype(jnp.int32)
    rotation = coriolis.reshape(1, OX)
    level = surface_weights.reshape(1, L)
    to_pack = (stencil_sign, spectrum, currents, level, rotation, ocean_index, ocean_weight)
    up, down, pos, surface, zonal, fits = pack(FAST, *to_pack)
    below, above = exchange(up, down)
    below = pltpu.with_memory_space_constraint(below, pltpu.VMEM)
    above = pltpu.with_memory_space_constraint(above, pltpu.VMEM)
    below_two, above_two = exchange(zonal, zonal, 2)
    made = tables(
        row, pos, stencil_sign, courant, nonlinear.reshape(1, K), quad_index.transpose(0, 2, 1),
        quad_weight.transpose(0, 2, 1), stokes_table, point_index, point_weight, mixing.reshape(1, L),
        level,
    )
    slope = slopes(FAST, up, down, made[3])
    rest = (
        below_two, above_two, surface, made, water_mask.reshape(1, MX), ocean_index, ocean_weight,
        currents, rotation,
    )

    def balanced(sent, to_pack, rest):
        return steps(FAST, *sent, *rest)

    def general(sent, to_pack, rest):
        up, down = pack(K, *to_pack)[:2]
        below, above = exchange(up, down)
        return steps(K, up, down, below, above, slopes(K, up, down, rest[3][3]), *rest)

    return lax.cond(fits[0] == 1, balanced, general, (up, down, below, above, slope), to_pack, rest)


def solution(mesh):
    whole = P(AXES)
    last = P(None, AXES)
    return jax.shard_map(
        local,
        mesh=mesh,
        in_specs=(
            last, whole, P(), P(), P(), P(), P(), P(), last, last, last, last,
            P(None, None, AXES), whole, P(), P(),
        ),
        out_specs=(last, P(None, None, AXES)),
        check_vma=False,
    )
```

```python
import functools

import jax
import jax.numpy as jnp
from jax import lax
from jax.experimental import pallas as pl
from jax.experimental.pallas import tpu as pltpu
from jax.sharding import PartitionSpec as P

K = 1024
L = 64
MX = 256
OX = 128
AXES = ("mp", "dev")
EXTRA = 72
LIMIT = 24 << 20
FAST = 560
F32 = jnp.float32
BF16 = jnp.bfloat16
VMEM = pl.BlockSpec(memory_space=pltpu.VMEM)
SMEM = pl.BlockSpec(memory_space=pltpu.SMEM)
HIGHEST = lax.Precision.HIGHEST


def dot_nt(a, b):
    return lax.dot_general(a, b, (((1,), (1,)), ((), ())), preferred_element_type=F32)


def dot_nn(a, b):
    return jnp.dot(a, b, preferred_element_type=F32)


def dot_exact(a, b):
    return jnp.dot(a, b, precision=HIGHEST, preferred_element_type=F32)


def split2(x):
    high = x.astype(BF16)
    return high, (x - high.astype(F32)).astype(BF16)


def split3(x):
    high, middle = split2(x)
    low = (x - high.astype(F32) - middle.astype(F32)).astype(BF16)
    return high, middle, low


def one_hot_rows(select_ref, pos_ref, copies=1):
    place = lax.broadcasted_iota(jnp.int16, (K, 128), 0)
    for block in range(8):
        line = pos_ref[block : block + 1, :].astype(jnp.int32)
        line = jnp.broadcast_to(line, (16, 128)).astype(jnp.int16)[0:1]
        ones = jnp.where(place == line, jnp.ones((), BF16), jnp.zeros((), BF16))
        for copy in range(copies):
            start = copy * K + block * 128
            select_ref[:, start : start + 128] = ones


def pack_kernel(
    count, sign, spectrum, currents, level, coriolis, ocean_index, ocean_weight,
    up, down, pos, surface, zonal, fits, select, parts,
):
    for block in range(8):
        pos[block : block + 1, :] = sign[1:2, block * 128 : (block + 1) * 128].astype(F32)
    ones = pos[...]
    upper = lax.broadcasted_iota(jnp.int32, (128, 256), 0) <= lax.broadcasted_iota(
        jnp.int32, (128, 256), 1
    )
    sums = dot_nn(ones.astype(BF16), jnp.where(upper, 1.0, 0.0).astype(BF16))
    in_line, total = sums[:, 0:128], sums[:, 128:]
    line = lax.broadcasted_iota(jnp.int32, (8, 128), 0)
    running = total
    northward = total
    for shift in (1, 2, 4):
        running = running + jnp.where(line >= shift, pltpu.roll(running, shift, 0), 0.0)
        northward = northward + pltpu.roll(northward, shift, 0)
    before = in_line + (running - total)
    index = (line * 128 + lax.broadcasted_iota(jnp.int32, (8, 128), 1)).astype(F32)
    pos[...] = jnp.where(ones > 0.5, before - 1.0, northward + index - before)
    one_hot_rows(select, pos)
    high, low = split2(spectrum[...])
    parts[:, 0:MX] = low
    parts[:, MX:] = high
    both = dot_nn(select[...], parts[...])
    value = both[:, 0:MX] + both[:, MX:]
    up[0:count, :] = value[0:count, :]
    down[0:count, :] = value[K - count :, :]
    some = jnp.sum(northward[0:1, 0:1])
    fits[0] = jnp.logical_and(some <= count, K - some <= count).astype(jnp.int32)
    weights = jnp.broadcast_to(level[...], (8, L))
    flat_u = dot_exact(weights, currents[0])
    flat_v = dot_exact(weights, currents[1])
    surface[...] = flat_u
    surface[1:2, :] = flat_v[0:1, :]
    zonal[...] = currents[0]
    half = L // 2
    for message in (up, down):
        message[count : count + 1, 0:OX] = flat_u[0:1, :]
        message[count : count + 1, OX : 2 * OX] = flat_v[0:1, :]
        message[count + 1 : count + 5, 0:OX] = ocean_index[...].astype(F32)
        message[count + 1 : count + 5, OX : 2 * OX] = ocean_weight[...]
        message[count + 5 : count + 8, :] = jnp.zeros((3, MX), F32)
        message[count + 5 : count + 6, 0:OX] = coriolis[...]
        for flow in range(2):
            at = count + 8 + flow * half
            message[at : at + half, 0:OX] = currents[flow, 0:half, :]
            message[at : at + half, OX : 2 * OX] = currents[flow, half:, :]


def table_kernel(
    row, pos, sign, courant, nonlinear, quad_index, quad_weight, stokes_table, point_index,
    point_weight, mixing, level, ocean_index, ocean_weight, quad, back, stokes_sorted, wide, cell_column, cell_side, cell_weight,
    mixing_wide, level_wide, own_cells, own_low, select, rows, parts, columns,
):
    one_hot_rows(select, pos)
    sense = (2 * sign[...] - 1).astype(F32)
    speed = courant[...]
    rows[...] = jnp.zeros((32, K), F32)
    rows[0:2, :] = speed
    rows[2:4, :] = 0.5 * speed * sense
    rows[4:6, :] = sense
    rows[6:7, :] = nonlinear[...]
    for config in range(4):
        index = quad_index[config]
        weight = quad_weight[config]
        same = index[0:1] == index[1:2]
        first = jnp.where(same, weight[0:1] + weight[1:2], weight[0:1])
        second = jnp.where(same, 0.0, weight[1:2])
        rows[8 + 2 * config : 9 + 2 * config, :] = first.astype(BF16).astype(F32)
        rows[9 + 2 * config : 10 + 2 * config, :] = second.astype(BF16).astype(F32)
        rows[16 + 2 * config : 18 + 2 * config, :] = index.astype(F32)
    high, middle, low = split3(rows[...])
    parts[0:32, :] = high
    parts[32:64, :] = middle
    parts[64:96, :] = low
    component = lax.broadcasted_iota(jnp.int32, (16, K), 1)
    line = lax.broadcasted_iota(jnp.int32, (16, K), 0)
    digits = jnp.where(line == 0, component // 32, component % 32).astype(F32).astype(BF16)
    found = dot_nt(digits, select[...])
    order = found[0:1] * 32.0 + found[1:2]
    stokes_sorted[...] = dot_nt(stokes_table[...], select[...]).astype(BF16)

    got = dot_nt(select[...], parts[...])
    columns[...] = got[:, 0:32] + (got[:, 32:64] + got[:, 64:96])

    def block_rows(block, carry):
        at = pl.ds(pl.multiple_of(block * 64, 64), 64)
        column = columns[at, :]
        for item in range(7):
            wide[item, at, :] = jnp.broadcast_to(column[:, item : item + 1], (64, 128))
        original = (lax.broadcasted_iota(jnp.int32, (64, K), 0) + block * 64).astype(F32)
        back[at, :] = jnp.where(order == original, 1.0, 0.0).astype(BF16)
        for config in range(4):
            a = 8 + 2 * config
            b = 16 + 2 * config
            value = jnp.where(
                order == column[:, b : b + 1],
                column[:, a : a + 1],
                jnp.where(order == column[:, b + 1 : b + 2], column[:, a + 1 : a + 2], 0.0),
            )
            quad[config, at, :] = value.astype(BF16)
        return carry

    lax.fori_loop(0, K // 64, block_rows, 0)
    for config in range(4):
        for half in range(2):
            line = slice(2 * config + half, 2 * config + half + 1)
            cell = point_index[config : config + 1, half * 128 : (half + 1) * 128]
            cell_column[line, :] = cell % OX
            cell_side[line, :] = (cell // OX - row[0] + 257) % 256
            cell_weight[line, :] = point_weight[config : config + 1, half * 128 : (half + 1) * 128]
    table = cell_table(row[0] * MX, ocean_index[...].astype(F32), ocean_weight[...])
    own_cells[...], own_low[...] = split2(table)
    diagonal = lax.broadcasted_iota(jnp.int32, (L, L), 0) == lax.broadcasted_iota(jnp.int32, (L, L), 1)
    for line, wide_column in ((mixing, mixing_wide), (level, level_wide)):
        column = jnp.sum(jnp.where(diagonal, line[...], 0.0), axis=1, keepdims=True)
        wide_column[...] = jnp.broadcast_to(column, (L, OX))


def cell_table(base, index, weight):
    point = (lax.broadcasted_iota(jnp.int32, (MX, OX), 0) + base).astype(F32)
    total = jnp.zeros((MX, OX), F32)
    for config in range(4):
        total = total + jnp.where(
            index[config : config + 1, :] == point, weight[config : config + 1, :], 0.0
        )
    return total


def blocks(start, stop, body):
    for at in range(start, stop, 64):
        body(at, min(64, stop - at))


def slope_kernel(count, own_up, own_down, wide, slope):
    def along(own, shift):
        def body(at, size):
            here = own[pl.ds(at - shift, size), :]
            sense = wide[4, pl.ds(at, size), :]
            sense = jnp.concatenate([sense, sense], axis=1)
            behind = jnp.where(sense > 0.0, pltpu.roll(here, 1, 1), pltpu.roll(here, MX - 1, 1))
            slope[pl.ds(at, size), :] = here - behind

        return body

    blocks(0, count, along(own_up, 0))
    blocks(count, K, along(own_down, K - count))


def update(count, own_up, own_down, from_below, from_above, flow, slope, quad, wide, stokes_sorted, wet,
           write, advected, rounded, finished):
    bend_x = jnp.tanh(flow[0])
    bend_y = jnp.tanh(flow[1])
    skip = K - count

    def advect(own, shift, behind):
        def body(at, size):
            here = own[pl.ds(at - shift, size), :]
            rows = pl.ds(at, size)
            base_x, base_y, bend_of_x, bend_of_y = [wide[item, rows, :] for item in range(4)]
            step_x = slope[rows, :]
            step_y = here - behind(at, size)
            for half in range(2):
                lanes = slice(half * 128, (half + 1) * 128)
                speed_x = base_x + bend_of_x * bend_x[:, lanes]
                speed_y = base_y + bend_of_y * bend_y[:, lanes]
                value = here[:, lanes] - speed_x * step_x[:, lanes] - speed_y * step_y[:, lanes]
                advected[rows, lanes] = value
                rounded[rows, lanes] = value.astype(BF16)

        return body

    def below(at, size):
        return from_below[pl.ds(at, size), :]

    def above(at, size):
        return from_above[pl.ds(at - skip, size), :]

    def either(at, size):
        sense = wide[5, pl.ds(at, size), :]
        sense = jnp.concatenate([sense, sense], axis=1)
        return jnp.where(sense > 0.0, below(at, size), above(at, size))

    if skip:
        blocks(0, skip, advect(own_up, 0, below))
    blocks(skip, count, advect(own_up, 0, either))
    if skip:
        blocks(count, K, advect(own_down, skip, above))

    def source(at, size):
        rows = pl.ds(at, size)
        members = [dot_nn(quad[config, rows, :], rounded[...]) for config in range(4)]
        value = advected[rows, :]
        pairs = members[0] * members[1] + members[2] * members[3]
        total = (members[0] + members[1]) + (members[2] + members[3])
        gain = wide[6, rows, :]
        gain = jnp.concatenate([gain, gain], axis=1)
        result = wet * (value + gain * (value * (value * total - pairs)))
        write(at, size, result)
        finished[rows, :] = result.astype(BF16)

    for at in range(0, K, 512):
        source(at, 512)
    return dot_nn(stokes_sorted[...], finished[...])


def flow_of(sides, column, side, weight):
    index = column[...]
    where = side[...]
    flow = []
    for component in range(2):
        total = jnp.zeros((8, OX), F32)
        for item in range(3):
            line = jnp.broadcast_to(sides[item][:, component * OX : (component + 1) * OX], (8, OX))
            got = jnp.take_along_axis(line, index, axis=1, mode="promise_in_bounds")
            total = jnp.where(where == item, got, total)
        total = total * weight[...]
        halves = [
            (total[h : h + 1] + total[h + 2 : h + 3]) + (total[h + 4 : h + 5] + total[h + 6 : h + 7])
            for h in range(2)
        ]
        flow.append(jnp.concatenate(halves, axis=1))
    return flow


def drift_parts(stokes, cells, cells_low):
    high = stokes.astype(BF16)
    low = (stokes - high.astype(F32)).astype(BF16)
    both = dot_nn(jnp.concatenate([high, low], axis=0), cells[...])
    return both[0:128] + (both[128:] + dot_nn(high, cells_low[...]))


def tall(block):
    return jnp.concatenate([block[:, 0:OX], block[:, OX:]], axis=0)


def turn(v, u_below, u_above):
    return 0.5 * (pltpu.roll(v, OX - 1, 1) - pltpu.roll(v, 1, 1)) - 0.5 * (u_above - u_below)


def mix(profile, mixing):
    line = lax.broadcasted_iota(jnp.int32, (L, OX), 0)
    before = jnp.where(line == 0, profile, pltpu.roll(profile, 1, 0))
    after = jnp.where(line == L - 1, profile, pltpu.roll(profile, L - 1, 0))
    return mixing * (before - 2.0 * profile + after)


def ocean_step(u, v, u_below, u_above, drift, rotation, mixing):
    vorticity = turn(v, u_below, u_above)
    drift_x = drift[0:L, :]
    drift_y = drift[L:, :]
    new_u = u + 0.5 * (rotation * (v + drift_y) + vorticity * drift_y + mix(u, mixing))
    new_v = v + 0.5 * (-rotation * (u + drift_x) - vorticity * drift_x + mix(v, mixing))
    return new_u, new_v


def level_sum(weights, x):
    return jnp.sum(weights * x, axis=0, keepdims=True)


def first_kernel(
    count, row, own_up, own_down, from_below, from_above, below_two, above_two, surface, slope, quad, wide,
    stokes_sorted, cell_column, cell_side, cell_weight, wet, own_cells, own_low, currents,
    coriolis, mixing, level,
    up, down, own_part, surface_part, far_up, far_down, cells, cells_low, advected, rounded, finished,
):
    base = row[0] * MX
    half = L // 2
    below_extra = from_below[count:, :]
    above_extra = from_above[count:, :]
    for side, index, weight in (
        (0, below_extra[1:5, 0:OX], below_extra[1:5, OX:]),
        (2, above_extra[1:5, 0:OX], above_extra[1:5, OX:]),
    ):
        table = cell_table(base, index, weight)
        high = table.astype(BF16)
        cells[:, side * OX : (side + 1) * OX] = high
        cells_low[:, side * OX : (side + 1) * OX] = (table - high.astype(F32)).astype(BF16)
    cells[:, OX : 2 * OX] = own_cells[...]
    cells_low[:, OX : 2 * OX] = own_low[...]
    own = jnp.concatenate([surface[0:1, :], surface[1:2, :]], axis=1)
    sides = (below_extra[0:1, :], own, above_extra[0:1, :])
    flow = flow_of(sides, cell_column, cell_side, cell_weight)
    wet_row = wet[...].astype(F32)

    def write(at, size, result):
        top = min(at + size, count)
        if top > at:
            up[at:top, :] = result[0 : top - at]
        start = max(at, K - count)
        if start < at + size:
            down[start - K + count : at + size - K + count, :] = result[start - at :]

    stokes = update(count, own_up, own_down, from_below, from_above, flow, slope, quad, wide,
                    stokes_sorted, wet_row, write, advected, rounded, finished)
    part = drift_parts(stokes, cells, cells_low)
    u, v = currents[0], currents[1]
    u_below, v_below = tall(below_extra[8 : 8 + half]), tall(below_extra[8 + half : 8 + 2 * half])
    u_above, v_above = tall(above_extra[8 : 8 + half]), tall(above_extra[8 + half : 8 + 2 * half])
    weights = level[...]
    rotations = (below_extra[5:6, 0:OX], coriolis[...], above_extra[5:6, 0:OX])
    turns = (turn(v_below, below_two[...], u), turn(v, u_below, u_above), turn(v_above, u, above_two[...]))
    shares = []
    for side in range(3):
        factor = 0.5 * weights * (rotations[side] + turns[side])
        block = part[:, side * OX : (side + 1) * OX]
        shares.append((jnp.sum(factor * block[L:], axis=0, keepdims=True),
                       -jnp.sum(factor * block[0:L], axis=0, keepdims=True)))
    own_u = shares[1][0] + level_sum(weights, u + 0.5 * (coriolis[...] * v + mix(u, mixing[...])))
    own_v = shares[1][1] + level_sum(weights, v + 0.5 * (mix(v, mixing[...]) - coriolis[...] * u))
    own_part[...] = part[:, OX : 2 * OX]
    surface_part[...] = jnp.zeros((8, MX), F32)
    for side, message, far in ((0, down, far_down), (2, up, far_up)):
        block = part[:, side * OX : (side + 1) * OX]
        message[count : count + L, 0:OX] = block[0:L]
        message[count : count + L, OX:] = block[L:]
        message[count + L :, :] = jnp.zeros((8, MX), F32)
        message[count + L : count + L + 1, 0:OX] = own_u
        message[count + L : count + L + 1, OX:] = own_v
        message[count + L + 1 : count + L + 2, 0:OX] = shares[side][0]
        message[count + L + 1 : count + L + 2, OX:] = shares[side][1]
        far[...] = jnp.zeros((8, MX), F32)
        far[0:1, 0:OX] = shares[side][0]
        far[0:1, OX:] = shares[side][1]
        at = side // 2
        surface_part[at : at + 1, 0:OX] = shares[side][0]
        surface_part[at : at + 1, OX:] = shares[side][1]
    surface_part[2:3, 0:OX] = own_u
    surface_part[2:3, OX:] = own_v


def second_kernel(
    count, own_up, own_down, from_below, from_above, below_two, above_two, zonal_below, zonal_above,
    own_part, surface_part, slope, quad, wide, stokes_sorted, cell_column, cell_side, cell_weight, wet, cells,
    cells_low, currents, coriolis, mixing,
    spectra, state, to_above, to_below, last_part, rounded, finished,
):
    half = L // 2
    below_extra = from_below[count:, :]
    above_extra = from_above[count:, :]
    own = surface_part[...]
    surf_below = below_extra[L : L + 1] + below_two[0:1, :] + own[0:1]
    surf_own = own[2:3] + below_extra[L + 1 : L + 2] + above_extra[L + 1 : L + 2]
    surf_above = above_extra[L : L + 1] + above_two[0:1, :] + own[1:2]
    flow = flow_of((surf_below, surf_own, surf_above), cell_column, cell_side, cell_weight)
    drift = own_part[...] + tall(below_extra[0:L]) + tall(above_extra[0:L])
    new_u, new_v = ocean_step(
        currents[0], currents[1], tall(zonal_below[count + 8 : count + 8 + half, :]),
        tall(zonal_above[count + 8 : count + 8 + half, :]), drift, coriolis[...], mixing[...]
    )
    state[0] = new_u
    state[1] = new_v
    wet_row = wet[...].astype(F32)

    def write(at, size, result):
        spectra[at : at + size, :] = result

    stokes = update(count, own_up, own_down, from_below, from_above, flow, slope, quad, wide,
                    stokes_sorted, wet_row, write, spectra, rounded, finished)
    part = drift_parts(stokes, cells, cells_low)
    to_below[0:128, :] = part[:, 0:OX]
    last_part[...] = part[:, OX : 2 * OX]
    to_above[0:128, :] = part[:, 2 * OX :]
    to_below[128:, :] = new_u
    to_above[128:, :] = new_u


def restore_kernel(spectra, back, out, parts):
    high, low = split2(spectra[...])
    parts[:, 0:MX] = high
    parts[:, MX:] = low
    both = dot_nn(back[...], parts[...])
    out[...] = both[:, 0:MX] + both[:, MX:]


def last_ocean(state, from_below, from_above, own_part, coriolis, mixing, out):
    drift = own_part[...] + from_below[0:128, :] + from_above[0:128, :]
    new_u, new_v = ocean_step(
        state[0], state[1], from_below[128:, :], from_above[128:, :], drift, coriolis[...], mixing[...]
    )
    out[0] = new_u
    out[1] = new_v


def shape(*dims, dtype=F32):
    return jax.ShapeDtypeStruct(dims, dtype)


def call(body, outs, scratch=(), scalars=0, inputs=0, flops=0, data=0, name=None, out_specs=None):
    return pl.pallas_call(
        body,
        out_shape=outs,
        in_specs=[SMEM] * scalars + [VMEM] * (inputs - scalars),
        out_specs=out_specs or jax.tree.map(lambda _: VMEM, outs),
        scratch_shapes=scratch,
        cost_estimate=pl.CostEstimate(flops=flops, bytes_accessed=data, transcendentals=0),
        compiler_params=pltpu.CompilerParams(vmem_limit_bytes=LIMIT),
        name=name,
    )


def exchange(to_above, to_below, distance=1):
    total = lax.axis_size("mp") * lax.axis_size("dev")
    up = [(i, (i + distance) % total) for i in range(total)]
    return (
        lax.ppermute(to_above, AXES, up),
        lax.ppermute(to_below, AXES, [(b, a) for a, b in up]),
    )


def pack(count, stencil_sign, spectrum, currents, level, coriolis, ocean_index, ocean_weight):
    message = pltpu.VMEM((count + EXTRA, MX), F32)
    return call(
        functools.partial(pack_kernel, count),
        (message, message, shape(8, 128), shape(8, 128), shape(L, OX), shape(1, dtype=jnp.int32)),
        (pltpu.VMEM((K, K), BF16), pltpu.VMEM((K, 2 * MX), BF16)),
        inputs=7, flops=2 * K * K * 3 * MX, data=1 << 20, name="pack",
        out_specs=(VMEM, VMEM, VMEM, VMEM, VMEM, SMEM),
    )(stencil_sign, spectrum, currents, level, coriolis, ocean_index, ocean_weight)


def slopes(count, up, down, wide):
    return call(
        functools.partial(slope_kernel, count), shape(K, MX), inputs=3, flops=1 << 30, data=4 << 20,
        name="slopes",
    )(up, down, wide)


def tables(row, pos, stencil_sign, courant, nonlinear, quad_index, quad_weight, stokes_table, point_index,
           point_weight, mixing, level, ocean_index, ocean_weight):
    whole = jnp.int32
    return call(
        table_kernel,
        (
            shape(4, K, K, dtype=BF16), shape(K, K, dtype=BF16), shape(128, K, dtype=BF16),
            shape(7, K, 128), shape(8, OX, dtype=whole), shape(8, OX, dtype=whole), shape(8, OX),
            shape(L, OX), shape(L, OX), shape(MX, OX, dtype=BF16), shape(MX, OX, dtype=BF16),
        ),
        (pltpu.VMEM((K, K), BF16), pltpu.VMEM((32, K), F32), pltpu.VMEM((96, K), BF16),
         pltpu.VMEM((K, 32), F32)),
        scalars=1, inputs=14, flops=4 << 30, data=12 << 20, name="tables",
    )(row, pos, stencil_sign, courant, nonlinear, quad_index, quad_weight, stokes_table, point_index,
      point_weight, mixing, level, ocean_index, ocean_weight)


def steps(
    count, up, down, below, above, slope, below_two, above_two, surface, made, row, wet,
    currents, coriolis,
):
    quad, back, stokes_sorted, wide, cell_column, cell_side, cell_weight, mixing, level, own_cells, own_low = made
    part = shape(128, OX)
    message = shape(count + EXTRA, MX)
    far = shape(8, MX)
    table = shape(MX, 3 * OX, dtype=BF16)
    work = (pltpu.VMEM((K, MX), BF16), pltpu.VMEM((K, MX), BF16))
    next_up, next_down, own_part, surface_part, far_up, far_down, cells, cells_low = call(
        functools.partial(first_kernel, count),
        (message, message, part, far, far, far, table, table),
        (pltpu.VMEM((K, MX), F32),) + work,
        scalars=1, inputs=22, flops=3 << 30, data=12 << 20, name="first",
    )(row, up, down, below, above, below_two, above_two, surface, slope, quad, wide, stokes_sorted,
      cell_column, cell_side, cell_weight, wet, own_cells, own_low, currents, coriolis, mixing,
      level)
    next_below, next_above = exchange(next_up, next_down)
    far_below, far_above = exchange(far_up, far_down, 2)
    slope = slopes(count, next_up, next_down, wide)
    end = shape(128 + L, OX)
    spectra, state, to_above, to_below, last_part = call(
        functools.partial(second_kernel, count),
        (shape(K, MX), shape(2, L, OX), end, end, part),
        work, inputs=23, flops=3 << 30, data=12 << 20, name="second",
    )(next_up, next_down, next_below, next_above, far_below, far_above, below, above, own_part,
      surface_part, slope, quad, wide, stokes_sorted, cell_column, cell_side, cell_weight, wet, cells,
      cells_low, currents, coriolis, mixing)
    end_below, end_above = exchange(to_above, to_below)
    out = call(
        restore_kernel, shape(K, MX), (pltpu.VMEM((K, 2 * MX), BF16),), inputs=2, flops=2 * K * K * 2 * MX,
        data=4 << 20, name="restore",
    )(spectra, back)
    final = call(
        last_ocean, shape(2, L, OX), inputs=6, flops=1 << 20, data=1 << 18, name="ocean",
    )(state, end_below, end_above, last_part, coriolis, mixing)
    return out, final


def local(
    spectrum, water_mask, courant, stencil_sign, quad_index, quad_weight, nonlinear, stokes_table,
    point_index, point_weight, ocean_index, ocean_weight, currents, coriolis, mixing, surface_weights,
):
    row = (lax.axis_index("mp") * lax.axis_size("dev") + lax.axis_index("dev")).reshape(1)
    row = row.astype(jnp.int32)
    rotation = coriolis.reshape(1, OX)
    level = surface_weights.reshape(1, L)
    to_pack = (stencil_sign, spectrum, currents, level, rotation, ocean_index, ocean_weight)
    up, down, pos, surface, zonal, fits = pack(FAST, *to_pack)
    below, above = exchange(up, down)
    below = pltpu.with_memory_space_constraint(below, pltpu.VMEM)
    above = pltpu.with_memory_space_constraint(above, pltpu.VMEM)
    below_two, above_two = exchange(zonal, zonal, 2)
    made = tables(
        row, pos, stencil_sign, courant, nonlinear.reshape(1, K), quad_index.transpose(0, 2, 1),
        quad_weight.transpose(0, 2, 1), stokes_table, point_index, point_weight, mixing.reshape(1, L),
        level, ocean_index, ocean_weight,
    )
    slope = slopes(FAST, up, down, made[3])
    rest = (
        below_two, above_two, surface, made, row, water_mask.reshape(1, MX),
        currents, rotation,
    )

    def balanced(sent, to_pack, rest):
        return steps(FAST, *sent, *rest)

    def general(sent, to_pack, rest):
        up, down = pack(K, *to_pack)[:2]
        below, above = exchange(up, down)
        return steps(K, up, down, below, above, slopes(K, up, down, rest[3][3]), *rest)

    return lax.cond(fits[0] == 1, balanced, general, (up, down, below, above, slope), to_pack, rest)


def solution(mesh):
    whole = P(AXES)
    last = P(None, AXES)
    return jax.shard_map(
        local,
        mesh=mesh,
        in_specs=(
            last, whole, P(), P(), P(), P(), P(), P(), last, last, last, last,
            P(None, None, AXES), whole, P(), P(),
        ),
        out_specs=(last, P(None, None, AXES)),
        check_vma=False,
    )
```
